32 devices in a mesh: dp: 8 (over z, x), mp: 4 (over y, core).
Axes of the slice: x: 2, y: 2, z: 4, core: 2. Of those that a mesh axis runs over, the one named last changes fastest.
Arguments:
- patches: bfloat16 [12704, 768], P('dp'), may hold values from -6 to 6
- norm1_gain: float32 [768], replicated, may hold values from 0.5 to 1.5
- norm1_bias: float32 [768], replicated, may hold values from -1.75 to 1.75
- qkv_weight: bfloat16 [768, 3, 768], P(None, None, 'mp'), may hold values from -0.21875 to 0.21875
- qv_bias: float32 [2, 768], P(None, 'mp'), may hold values from -1.25 to 1.25
- out_weight: bfloat16 [768, 768], P('mp'), may hold values from -0.875 to 0.875
- out_bias: float32 [768], replicated, may hold values from -1.75 to 1.75
- norm2_gain: float32 [768], replicated, may hold values from 0.5 to 1.5
- norm2_bias: float32 [768], replicated, may hold values from -1.75 to 1.75
- up_weight: bfloat16 [768, 3072], P(None, 'mp'), may hold values from -0.21875 to 0.21875
- up_bias: float32 [3072], P('mp'), may hold values from -3 to 3
- down_weight: bfloat16 [3072, 768], P('mp'), may hold values from -0.109375 to 0.109375
- down_bias: float32 [768], replicated, may hold values from -1.75 to 1.75
- dec_weight: bfloat16 [768, 512], P(None, 'mp'), may hold values from -0.21875 to 0.21875
- dec_bias: float32 [512], P('mp'), may hold values from -3 to 3
- mask_token: float32 [512], P('mp'), may hold values from -6 to 6
- lengths: int32 [32], replicated, may hold values from 40 to 529, as said below
- blank: int32 [32, 529], replicated, may hold values from 0 to 1, as said below
- visible: int32 [32, 397], replicated, may hold values from 0 to 528, as said below
- plan: int32 [32], replicated, may hold values from 0 to 7, as said below
- dec_cot: bfloat16 [32, 529, 512], P('dp', None, 'mp'), may hold values from -6 to 6
Outputs:
- decoder_input: bfloat16 [32, 529, 512], P('dp', None, 'mp')
- patches_grad: float32 [12704, 768], P('dp')
- norm1_gain_grad: float32 [768], replicated
- norm1_bias_grad: float32 [768], replicated
- qkv_weight_grad: float32 [768, 3, 768], P(None, None, 'mp')
- qv_bias_grad: float32 [2, 768], P(None, 'mp')
- out_weight_grad: float32 [768, 768], P('mp')
- out_bias_grad: float32 [768], replicated
- norm2_gain_grad: float32 [768], replicated
- norm2_bias_grad: float32 [768], replicated
- up_weight_grad: float32 [768, 3072], P(None, 'mp')
- up_bias_grad: float32 [3072], P('mp')
- down_weight_grad: float32 [3072, 768], P('mp')
- down_bias_grad: float32 [768], replicated
- dec_weight_grad: float32 [768, 512], P(None, 'mp')
- dec_bias_grad: float32 [512], P('mp')
- mask_token_grad: float32 [512], P('mp')
The draws below stay inside these ranges and needn't reach their ends.
Inputs may be any that keep to these rules, and one draw needn't show every extreme that they name: `lengths`: one strip in every draw has 529 text patches and another 40. blank[j, 0] is 0. `visible`: each row holds 397 distinct positions in increasing order, the first of them 0. `plan`: each data index is named by exactly 4 strips, and never by two strips of the same owner.
All inputs are finite; a program needn't handle non-finite values.
Results may differ from the reference program's by a relative error of at most 0.02.
Values may be sent and summed in bfloat16 or wider, within the bound.
A program may use at most 128 MiB of HBM per device.

```python
import jax
import jax.numpy as jnp
from jax import lax

D = 768
HEADS = 12
HD = 64
FF = 3072
DEC = 512
SEQ = 529
LMIN = 40
VIS = 397
SPD = 4
STRIPS = 32
ROWS = 12704
N_DP = 8
N_MP = 4


def draw_lengths(key, part):
    drawn = jax.random.randint(jax.random.fold_in(key, 11), (STRIPS,), LMIN, SEQ + 1)
    chosen = jax.random.randint(jax.random.fold_in(key, 12), (), 0, STRIPS)
    places = jnp.arange(STRIPS)
    drawn = jnp.where(places == chosen, SEQ, drawn)
    drawn = jnp.where(places == (chosen + 1) % STRIPS, LMIN, drawn)
    return drawn.astype(jnp.int32)


def draw_blank(key, part):
    drawn = jax.random.randint(jax.random.fold_in(key, 21), (STRIPS, SEQ), 0, 8)
    flagged = (drawn == 0).astype(jnp.int32)
    return flagged.at[:, 0].set(0).astype(jnp.int32)


def draw_visible(key, part):
    strip_keys = jax.random.split(jax.random.fold_in(key, 31), STRIPS)

    def one_strip(strip_key):
        shuffled = jax.random.permutation(strip_key, SEQ - 1) + 1
        remaining = jnp.sort(shuffled[SEQ - VIS:]).astype(jnp.int32)
        return jnp.concatenate([jnp.zeros((1,), jnp.int32), remaining])
    return jax.vmap(one_strip)(strip_keys).astype(jnp.int32)


def draw_plan(key, part):
    placed = jax.random.permutation(jax.random.fold_in(key, 41), N_DP)
    offsets = jax.random.permutation(jax.random.fold_in(key, 42), N_DP)[:SPD]
    owners = jnp.arange(STRIPS) // SPD
    within = jnp.arange(STRIPS) % SPD
    return ((placed[owners] + offsets[within]) % N_DP).astype(jnp.int32)


def shard_levels(rng, extent, cuts, least, largest):
    loudness, own = 1.0, jax.random.fold_in(rng, 6)
    for dim, shards_of in cuts:
        steps = jnp.exp(jax.random.uniform(jax.random.fold_in(own, dim), (shards_of,), jnp.float32, least / len(cuts), largest / len(cuts)))
        loudness = loudness * jnp.repeat(steps, extent[dim] // shards_of).reshape([-1 if axis == dim else 1 for axis in range(len(extent))])
    return loudness


def scatter_about(rng, dims, deviation, limit, cuts=(), kind=jnp.bfloat16):
    result = jax.random.normal(rng, dims, jnp.float32) * deviation
    if len(cuts) > 0:
        result = shard_levels(rng, dims, cuts, -0.22, 0.18) * result
    return jnp.clip(result, min=-limit, max=limit).astype(kind)


def setup_inputs(seed: int = 0) -> dict:
    key_of = jax.random.split(jax.random.key(seed), 22)
    patches = scatter_about(key_of[0], (ROWS, D), 1.0, 6.0, ((0, 8),))
    norm1_gain = jnp.clip(1.0 + 0.1 * jax.random.normal(key_of[1], (D,), jnp.float32), 0.5, 1.5)
    norm1_bias = scatter_about(key_of[2], (D,), 0.3, 1.75, (), jnp.float32)
    qkv_weight = scatter_about(key_of[3], (D, 3, D), D ** -0.5, 0.21875, ((2, 4),))
    qv_bias = scatter_about(key_of[4], (2, D), 0.2, 1.25, ((1, 4),), jnp.float32)
    out_weight = scatter_about(key_of[5], (D, D), (D // 16) ** -0.5, 0.875, ((0, 4),))
    out_bias = scatter_about(key_of[6], (D,), 0.3, 1.75, (), jnp.float32)
    norm2_gain = jnp.clip(1.0 + 0.1 * jax.random.normal(key_of[7], (D,), jnp.float32), 0.5, 1.5)
    norm2_bias = scatter_about(key_of[8], (D,), 0.3, 1.75, (), jnp.float32)
    up_weight = scatter_about(key_of[9], (D, FF), D ** -0.5, 0.21875, ((1, 4),))
    up_bias = scatter_about(key_of[10], (FF,), 0.5, 3.0, ((0, 4),), jnp.float32)
    down_weight = scatter_about(key_of[11], (FF, D), FF ** -0.5, 0.109375, ((0, 4),))
    down_bias = scatter_about(key_of[12], (D,), 0.3, 1.75, (), jnp.float32)
    dec_weight = scatter_about(key_of[13], (D, DEC), D ** -0.5, 0.21875, ((1, 4),))
    dec_bias = scatter_about(key_of[14], (DEC,), 0.5, 3.0, ((0, 4),), jnp.float32)
    mask_token = scatter_about(key_of[15], (DEC,), 1.0, 6.0, ((0, 4),), jnp.float32)
    lengths = draw_lengths(jax.random.fold_in(key_of[21], 71), 0)
    blank = draw_blank(jax.random.fold_in(key_of[21], 71), 0)
    visible = draw_visible(jax.random.fold_in(key_of[21], 71), 0)
    plan = draw_plan(jax.random.fold_in(key_of[21], 71), 0)
    dec_cot = scatter_about(key_of[20], (STRIPS, SEQ, DEC), 1.0, 6.0, ((0, 8), (2, 4)))
    return {"patches": patches, "norm1_gain": norm1_gain, "norm1_bias": norm1_bias, "qkv_weight": qkv_weight, "qv_bias": qv_bias, "out_weight": out_weight, "out_bias": out_bias, "norm2_gain": norm2_gain, "norm2_bias": norm2_bias, "up_weight": up_weight, "up_bias": up_bias, "down_weight": down_weight, "down_bias": down_bias, "dec_weight": dec_weight, "dec_bias": dec_bias, "mask_token": mask_token, "lengths": lengths, "blank": blank, "visible": visible, "plan": plan, "dec_cot": dec_cot}


EPSILON = 1e-06
NEGATIVE = -1e+30

@jax.custom_vjp
def low(v):
    return lax.optimization_barrier(v.astype(jnp.bfloat16)).astype(jnp.float32)

@jax.custom_vjp
def low_back(v):
    return v

def low_keep(v):
    return (low(v), None)

def low_pass(kept, grad):
    return (grad,)

def back_keep(v):
    return (v, None)

def back_low(kept, grad):
    return (low(grad),)
low.defvjp(low_keep, low_pass)
low_back.defvjp(back_keep, back_low)

def layer_norm(inputs, gain_vec, shift_vec):
    centered = inputs - lax.optimization_barrier(jnp.mean(inputs, -1, keepdims=True))
    inverse = lax.rsqrt(lax.optimization_barrier(jnp.mean(centered * centered, -1, keepdims=True)) + EPSILON)
    return centered * inverse * gain_vec + shift_vec

def product(left_arr, right_arr):
    return jnp.dot(left_arr, right_arr, precision=lax.Precision.HIGHEST, preferred_element_type=jnp.float32)

def split_sum(left_arr, right_arr):
    left_parts = left_arr.reshape(left_arr.shape[0], N_MP, -1)
    right_parts = right_arr.reshape(N_MP, -1, right_arr.shape[1])
    pieces = jnp.einsum('vmc,mcd->vmd', left_parts, right_parts, precision=lax.Precision.HIGHEST)
    return lax.optimization_barrier(jnp.sum(low(pieces), 1))

def one_strip(params, strip_rows, allowed):
    gain_one, shift_one, qkv_w, qv_b, out_w, out_b, gain_two, shift_two, up_w, up_b, down_w, down_b, dec_w, dec_b = params
    low_one = low(layer_norm(strip_rows, gain_one, shift_one))
    projected = product(low_one, qkv_w.reshape(D, 3 * D))
    query = low(low_back(projected[:, :D] + qv_b[0])).reshape(VIS, HEADS, HD)
    keys_all = low(low_back(projected[:, D:2 * D])).reshape(VIS, HEADS, HD)
    values_all = low(low_back(projected[:, 2 * D:] + qv_b[1])).reshape(VIS, HEADS, HD)
    raw_scores = low_back(jnp.einsum('qhd,khd->hqk', query, keys_all, precision=lax.Precision.HIGHEST) * HD ** (-0.5))
    masked = jnp.where(allowed[None, None, :], raw_scores, NEGATIVE)
    exponent = jnp.exp(masked - lax.optimization_barrier(jnp.max(masked, -1, keepdims=True)))
    probs = low(exponent / lax.optimization_barrier(jnp.sum(exponent, -1, keepdims=True)))
    attended = jnp.einsum('hqk,khd->qhd', probs, values_all, precision=lax.Precision.HIGHEST).reshape(VIS, D)
    attended = low(low_back(attended))
    middle = strip_rows + low_back(split_sum(attended, out_w)) + out_b
    low_two = low(layer_norm(middle, gain_two, shift_two))
    before_act = low_back(product(low_two, up_w) + up_b)
    activated = low(jax.nn.gelu(before_act, approximate=False))
    final_rows = middle + low_back(split_sum(activated, down_w)) + down_b
    return low(product(low(final_rows), dec_w) + dec_b)

def forward(packed, params, mask_vec, rows_index, allowed, strip_index, visible):
    gathered = packed[rows_index]

    def mapped(member):
        return jax.checkpoint(one_strip)(params, member[0], member[1])
    outputs = lax.map(mapped, (gathered, allowed))
    filled = jnp.broadcast_to(mask_vec, (STRIPS, SEQ, DEC))
    return filled.at[strip_index, visible].set(outputs)

def reference(patches, norm1_gain, norm1_bias, qkv_weight, qv_bias, out_weight, out_bias, norm2_gain, norm2_bias, up_weight, up_bias, down_weight, down_bias, dec_weight, dec_bias, mask_token, lengths, blank, visible, plan, dec_cot):
    strip_ids = jnp.arange(STRIPS, dtype=jnp.int32)
    earlier = (plan[None, :] == plan[:, None]) & (strip_ids[None, :] < strip_ids[:, None])
    before_count = lax.optimization_barrier(jnp.sum(earlier.astype(jnp.int32), 1)).astype(jnp.int32)
    start_rows = ((plan * SPD + before_count) * VIS).astype(jnp.int32)
    rows_index = (start_rows[:, None] + jnp.arange(VIS, dtype=jnp.int32)[None, :]).astype(jnp.int32)
    blank_at = jnp.take_along_axis(blank, visible, 1)
    allowed = (visible < lengths[:, None]) & (blank_at == 0)
    strip_index = jnp.broadcast_to(strip_ids[:, None], (STRIPS, VIS)).astype(jnp.int32)
    params = (norm1_gain.astype(jnp.float32), norm1_bias.astype(jnp.float32), qkv_weight.astype(jnp.float32), qv_bias.astype(jnp.float32), out_weight.astype(jnp.float32), out_bias.astype(jnp.float32), norm2_gain.astype(jnp.float32), norm2_bias.astype(jnp.float32), up_weight.astype(jnp.float32), up_bias.astype(jnp.float32), down_weight.astype(jnp.float32), down_bias.astype(jnp.float32), dec_weight.astype(jnp.float32), dec_bias.astype(jnp.float32))

    def run(packed, param_tuple, mask_vec):
        return forward(packed, param_tuple, mask_vec, rows_index, allowed, strip_index, visible)
    decoded, pullback = jax.vjp(run, patches.astype(jnp.float32), params, mask_token.astype(jnp.float32))
    patch_grad, param_grads, mask_grad = pullback(dec_cot.astype(jnp.float32))
    return (decoded.astype(jnp.bfloat16), patch_grad, param_grads[0], param_grads[1], param_grads[2], param_grads[3], param_grads[4], param_grads[5], param_grads[6], param_grads[7], param_grads[8], param_grads[9], param_grads[10], param_grads[11], param_grads[12], param_grads[13], mask_grad)
```

```python
from functools import partial

import jax
import jax.numpy as jnp
from jax import lax
from jax.experimental import pallas as pl
from jax.experimental.pallas import tpu as pltpu
from jax.sharding import PartitionSpec as P

HD = 64
EPSILON = 1e-06
NEGATIVE = -1e30
F32 = jnp.float32
BF16 = jnp.bfloat16


def nn(a, b):
    return lax.dot_general(a, b, (((1,), (0,)), ((), ())), preferred_element_type=F32)


def tn(a, b):
    return lax.dot_general(a, b, (((0,), (0,)), ((), ())), preferred_element_type=F32)


def nt(a, b):
    return lax.dot_general(a, b, (((1,), (1,)), ((), ())), preferred_element_type=F32)


def norm_stats(inputs):
    centered = inputs - jnp.mean(inputs, -1, keepdims=True)
    inverse = lax.rsqrt(jnp.mean(centered * centered, -1, keepdims=True) + EPSILON)
    return centered * inverse, inverse


def norm_backward(incoming, normed, inverse, gain_vec):
    weighted = incoming * gain_vec
    inner = (
        weighted
        - jnp.mean(weighted, -1, keepdims=True)
        - normed * jnp.mean(weighted * normed, -1, keepdims=True)
    )
    return inner * inverse, jnp.sum(incoming * normed, 0), jnp.sum(incoming, 0)


def take_rows_kernel(pos_ref, cot_ref, out_ref, mask_ref):
    @pl.when(pl.program_id(0) == 0)
    def _():
        mask_ref[...] = jnp.zeros_like(mask_ref)

    seq = cot_ref.shape[1]
    n, _, chunk, feats = out_ref.shape
    spot = lax.broadcasted_iota(jnp.int32, (n * chunk, seq), 1)
    chosen = (pos_ref[0] == spot).astype(F32)
    rows = nn(chosen.astype(BF16), cot_ref[0])
    out_ref[...] = rows.astype(BF16).reshape(n, 1, chunk, feats)
    hidden = 1.0 - jnp.sum(chosen, 0, keepdims=True)
    hidden = jnp.broadcast_to(hidden, (8, seq)).astype(BF16)
    mask_ref[...] += nn(hidden, cot_ref[0])


def take_rows(pos_col, cot, n, chunk):
    held, seq, feats = cot.shape
    return pl.pallas_call(
        take_rows_kernel,
        grid=(held,),
        in_specs=[
            pl.BlockSpec((1, n * chunk, 1), lambda s: (s, 0, 0)),
            pl.BlockSpec((1, seq, feats), lambda s: (s, 0, 0)),
        ],
        out_specs=[
            pl.BlockSpec((n, 1, chunk, feats), lambda s: (0, s, 0, 0)),
            pl.BlockSpec((8, feats), lambda s: (0, 0)),
        ],
        out_shape=[
            jax.ShapeDtypeStruct((n, held, chunk, feats), BF16),
            jax.ShapeDtypeStruct((8, feats), F32),
        ],
        name="take_rows",
        compiler_params=pltpu.CompilerParams(vmem_limit_bytes=24 << 20),
    )(pos_col, cot)


def put_rows_kernel(pos_ref, rows_ref, token_ref, out_ref):
    n, _, chunk, feats = rows_ref.shape
    seq = out_ref.shape[1]
    spot = lax.broadcasted_iota(jnp.int32, (seq, n * chunk), 0)
    chosen = (pos_ref[0] == spot).astype(F32)
    rows = nn(chosen.astype(BF16), rows_ref[...].reshape(n * chunk, feats))
    hidden = 1.0 - jnp.sum(chosen, 1, keepdims=True)
    out_ref[0] = (rows + hidden * token_ref[...].astype(BF16).astype(F32)).astype(BF16)


def put_rows(pos_row, rows, token, seq):
    n, held, chunk, feats = rows.shape
    return pl.pallas_call(
        put_rows_kernel,
        grid=(held,),
        in_specs=[
            pl.BlockSpec((1, 1, n * chunk), lambda s: (s, 0, 0)),
            pl.BlockSpec((n, 1, chunk, feats), lambda s: (0, s, 0, 0)),
            pl.BlockSpec((1, feats), lambda s: (0, 0)),
        ],
        out_specs=pl.BlockSpec((1, seq, feats), lambda s: (s, 0, 0)),
        out_shape=jax.ShapeDtypeStruct((held, seq, feats), BF16),
        name="put_rows",
        compiler_params=pltpu.CompilerParams(vmem_limit_bytes=24 << 20),
    )(pos_row, rows, token.reshape(1, feats))


def attention_forward_kernel(qkv_ref, bias_ref, att_ref, stat_ref):
    lw = att_ref.shape[2]
    bias = bias_ref[0]
    stats, outs = [], []
    for h in range(lw // HD):
        q = qkv_ref[0, :, h * HD : (h + 1) * HD]
        k = qkv_ref[0, :, lw + h * HD : lw + (h + 1) * HD]
        v = qkv_ref[0, :, 2 * lw + h * HD : 2 * lw + (h + 1) * HD]
        s = nt(q, k) + bias
        top = jnp.max(s, -1, keepdims=True)
        e = jnp.exp(s - top)
        total = jnp.sum(e, -1, keepdims=True)
        outs.append((nn(e.astype(BF16), v) / total).astype(BF16))
        stats.append(top + jnp.log(total))
    att_ref[0] = jnp.concatenate(outs, -1)
    lane = lax.broadcasted_iota(jnp.int32, stat_ref.shape[1:], 1)
    stat = jnp.zeros(stat_ref.shape[1:], F32)
    for h, column in enumerate(stats):
        stat = jnp.where(lane == h, column, stat)
    stat_ref[0] = stat


def attention_forward(qkv, bias):
    held, rows, wide = qkv.shape
    lw = wide // 3
    return pl.pallas_call(
        attention_forward_kernel,
        grid=(held,),
        in_specs=[
            pl.BlockSpec((1, rows, wide), lambda s: (s, 0, 0)),
            pl.BlockSpec((1, 1, rows), lambda s: (s, 0, 0)),
        ],
        out_specs=[
            pl.BlockSpec((1, rows, lw), lambda s: (s, 0, 0)),
            pl.BlockSpec((1, rows, 128), lambda s: (s, 0, 0)),
        ],
        out_shape=[
            jax.ShapeDtypeStruct((held, rows, lw), BF16),
            jax.ShapeDtypeStruct((held, rows, 128), F32),
        ],
        name="attention_forward",
        compiler_params=pltpu.CompilerParams(vmem_limit_bytes=32 << 20),
    )(qkv, bias)


def attention_backward_kernel(qkv_ref, bias_ref, att_ref, stat_ref, grad_ref, out_ref):
    lw = att_ref.shape[2]
    scale = HD ** (-0.5)
    bias = bias_ref[0]
    dq, dk, dv = [], [], []
    for h in range(lw // HD):
        q = qkv_ref[0, :, h * HD : (h + 1) * HD]
        k = qkv_ref[0, :, lw + h * HD : lw + (h + 1) * HD]
        v = qkv_ref[0, :, 2 * lw + h * HD : 2 * lw + (h + 1) * HD]
        g = grad_ref[0, :, h * HD : (h + 1) * HD]
        o = att_ref[0, :, h * HD : (h + 1) * HD]
        s = nt(q, k) + bias
        p = jnp.exp(s - stat_ref[0, :, h : h + 1])
        dv.append(tn(p.astype(BF16), g).astype(BF16))
        inner = jnp.sum(g.astype(F32) * o.astype(F32), -1, keepdims=True)
        ds = (p * (nt(g, v) - inner)).astype(BF16)
        dq.append((nn(ds, k) * scale).astype(BF16))
        dk.append(tn(ds, q).astype(BF16))
    out_ref[0] = jnp.concatenate(dq + dk + dv, -1)


def attention_backward(qkv, bias, att, stat, grad):
    held, rows, wide = qkv.shape
    lw = wide // 3
    block = lambda w: pl.BlockSpec((1, rows, w), lambda s: (s, 0, 0))
    return pl.pallas_call(
        attention_backward_kernel,
        grid=(held,),
        in_specs=[
            block(wide),
            pl.BlockSpec((1, 1, rows), lambda s: (s, 0, 0)),
            block(lw),
            block(128),
            block(lw),
        ],
        out_specs=block(wide),
        out_shape=jax.ShapeDtypeStruct((held, rows, wide), BF16),
        name="attention_backward",
        compiler_params=pltpu.CompilerParams(vmem_limit_bytes=32 << 20),
    )(qkv, bias, att, stat, grad)


def over_core(x):
    return lax.ppermute(x, "mp", [(i, i ^ 1) for i in range(lax.axis_size("mp"))])


def over_y(x):
    return lax.ppermute(x, "mp", [(i, i ^ 2) for i in range(lax.axis_size("mp"))])


def pick(x, index, axis):
    return lax.dynamic_index_in_dim(x, index, axis, keepdims=False)


def scatter_mp(parts):
    m = lax.axis_index("mp")
    core, y = m % 2, m // 2
    square = parts.reshape(2, 2, *parts.shape[1:])
    got = over_core(pick(square, 1 - core, 1))
    total = pick(square, core, 1).astype(F32) + got.astype(F32)
    away = over_y(pick(total, 1 - y, 0).astype(BF16))
    return pick(total, y, 0) + away.astype(F32)


def gather_mp(own):
    m = lax.axis_index("mp")
    core, y = m % 2, m // 2
    other = over_y(own)
    pair = jnp.stack([jnp.where(y == 0, own, other), jnp.where(y == 0, other, own)])
    twin = over_core(pair)
    square = jnp.stack([jnp.where(core == 0, pair, twin), jnp.where(core == 0, twin, pair)], 1)
    return square.reshape(4, *own.shape)


def sum_dp(x):
    count = lax.axis_size("dp")
    d = lax.axis_index("dp")
    bits = count.bit_length() - 1
    swap = lambda v, b: lax.ppermute(v, "dp", [(i, i ^ (1 << b)) for i in range(count)])
    for b in range(bits):
        half = x.shape[0] // 2
        up = (d >> b) % 2 == 1
        low_half, high_half = x[:half], x[half:]
        send = jnp.where(up, low_half, high_half).astype(BF16)
        x = jnp.where(up, high_half, low_half) + swap(send, b).astype(F32)
    x = x.astype(BF16)
    for b in reversed(range(bits)):
        up = (d >> b) % 2 == 1
        got = swap(x, b)
        x = jnp.where(up, jnp.concatenate([got, x]), jnp.concatenate([x, got]))
    return x.astype(F32)


def high_low(vec):
    high = vec.astype(BF16)
    return high, (vec - high.astype(F32)).astype(BF16)


def shards(
    patches,
    norm1_gain,
    norm1_bias,
    qkv_weight,
    qv_bias,
    out_weight,
    out_bias,
    norm2_gain,
    norm2_bias,
    up_weight,
    up_bias,
    down_weight,
    down_bias,
    dec_weight,
    dec_bias,
    mask_token,
    lengths,
    blank,
    visible,
    plan,
    dec_cot,
):
    n = lax.axis_size("dp")
    d = lax.axis_index("dp")
    m = lax.axis_index("mp")
    held, seq, feats = dec_cot.shape
    vis = visible.shape[1]
    strips = plan.shape[0]
    width = patches.shape[1]
    lw = qkv_weight.shape[2]
    rows = -(-vis // 16) * 16
    real = -(-vis // n)
    chunk = -(-real // 8) * 8
    scale = HD ** (-0.5)

    strip_ids = jnp.arange(strips, dtype=jnp.int32)
    earlier = (plan[None, :] == plan[:, None]) & (strip_ids[None, :] < strip_ids[:, None])
    packed_at = plan * held + jnp.sum(earlier.astype(jnp.int32), 1)
    strip_at = jnp.sum(
        jnp.where(packed_at[None, :] == strip_ids[:, None], strip_ids[None, :], 0), 1
    )
    held_strips = lax.dynamic_slice_in_dim(strip_at, d * held, held)
    held_pos = visible[held_strips]
    place = jnp.arange(seq, dtype=jnp.int32)
    usable = (blank[held_strips] == 0) & (place[None, :] < lengths[held_strips][:, None])
    allowed = jnp.any((held_pos[:, :, None] == place) & usable[:, None, :], -1)
    key_bias = jnp.where(allowed, 0.0, NEGATIVE).astype(F32)
    key_bias = jnp.pad(key_bias, ((0, 0), (0, rows - vis)), constant_values=NEGATIVE)
    key_bias = key_bias.reshape(held, 1, rows)
    owned_pos = lax.dynamic_slice_in_dim(visible, d * held, held)
    owned_pos = jnp.pad(owned_pos, ((0, 0), (0, n * real - vis)), constant_values=-1)
    owned_pos = jnp.pad(
        owned_pos.reshape(held, n, real), ((0, 0), (0, 0), (0, chunk - real)), constant_values=-1
    )

    def exchange(spread, order):
        swap = partial(lax.all_to_all, axis_name="dp", split_axis=0, concat_axis=0, tiled=True)
        midway = swap(spread).reshape(strips, chunk, feats)
        return swap(midway[order].reshape(n, held, chunk, feats))

    spread_cot, mask_grad = take_rows(owned_pos.reshape(held, n * chunk, 1), dec_cot, n, chunk)
    arrived_cot = exchange(spread_cot, strip_at)
    g_rows = arrived_cot[:, :, :real].transpose(1, 0, 2, 3).reshape(held, n * real, feats)
    g_rows = g_rows[:, :rows]
    g_rows = jnp.pad(g_rows, ((0, 0), (0, rows - g_rows.shape[1]), (0, 0)))
    g_rows = g_rows.reshape(held * rows, feats)
    dec_bias_grad = jnp.sum(g_rows.astype(F32), 0)
    g_all = gather_mp(g_rows)
    dec_all = gather_mp(dec_weight)
    parts = range(4)
    g_three = nt(
        jnp.concatenate([g_all[i] for i in parts], 1),
        jnp.concatenate([dec_all[i] for i in parts], 1),
    )
    g_three_low = g_three.astype(BF16)
    down_bias_grad = jnp.sum(g_three, 0)

    x_all = jnp.pad(patches.reshape(held, vis, width), ((0, 0), (0, rows - vis), (0, 0)))
    x_own = pick(x_all, m, 0).astype(F32)
    normed, _ = norm_stats(x_all.reshape(held * rows, width).astype(F32))
    low_one = (normed * norm1_gain + norm1_bias).astype(BF16)
    flat_qkv = qkv_weight.reshape(width, 3 * lw)
    proj = nn(low_one, flat_qkv)
    query = (proj[:, :lw] + qv_bias[0]).astype(BF16) * jnp.asarray(scale, BF16)
    keys = proj[:, lw : 2 * lw].astype(BF16)
    values = (proj[:, 2 * lw :] + qv_bias[1]).astype(BF16)
    qkv = jnp.concatenate([query, keys, values], 1).reshape(held, rows, 3 * lw)
    attended, stat = attention_forward(qkv, key_bias)
    att_flat = attended.reshape(held * rows, lw)
    attn_parts = nn(att_flat, out_weight).astype(BF16).reshape(held, rows, width)
    mid = x_own + scatter_mp(attn_parts) + out_bias

    normed_two, inverse_two = norm_stats(mid)
    low_two = gather_mp((normed_two * norm2_gain + norm2_bias).astype(BF16))
    low_two = low_two.reshape(held * rows, width)
    before = nn(low_two, up_weight) + up_bias
    act, pullback = jax.vjp(partial(jax.nn.gelu, approximate=False), before)
    act = act.astype(BF16)
    g_before = pullback(nt(g_three_low, down_weight))[0].astype(BF16)
    h_two_parts = nt(g_before, up_weight).astype(BF16).reshape(held, rows, width)
    g_h_two = scatter_mp(h_two_parts)
    g_norm_two, gain_two, bias_two = norm_backward(g_h_two, normed_two, inverse_two, norm2_gain)
    g_mid = pick(g_three.reshape(held, rows, width), m, 0) + g_norm_two
    extra = jnp.stack([*high_low(gain_two), *high_low(bias_two)])
    extra = jnp.pad(extra, ((0, 4), (0, 0)))
    mid_all = gather_mp(jnp.concatenate([g_mid.astype(BF16), extra]))
    mid_low = mid_all[:, :rows].reshape(held * rows, width)
    extra_two = jnp.sum(mid_all[:, rows:].astype(F32), 0)

    up_bias_grad = jnp.sum(g_before.astype(F32), 0)
    up_grad = tn(low_two, g_before)
    down_grad = tn(act, g_three_low)
    ff_grads = sum_dp(jnp.concatenate([up_grad, down_grad]))

    ffn_parts = nn(act, down_weight).astype(BF16).reshape(held, rows, width)
    final = mid + scatter_mp(ffn_parts) + down_bias
    final_low = gather_mp(final.astype(BF16)).reshape(held * rows, width)
    projected = (nn(final_low, dec_weight) + dec_bias).astype(BF16).reshape(held, rows, feats)
    if n * real > rows:
        projected = jnp.pad(projected, ((0, 0), (0, n * real - rows), (0, 0)))
    spread = projected[:, : n * real].reshape(held, n, real, feats)
    spread = jnp.pad(spread, ((0, 0), (0, 0), (0, chunk - real), (0, 0))).transpose(1, 0, 2, 3)
    arrived = exchange(spread, packed_at)
    decoded = put_rows(owned_pos.reshape(held, 1, n * chunk), arrived, mask_token, seq)
    dec_grad = tn(g_rows, final_low)

    out_bias_grad = jnp.sum(mid_low.astype(F32), 0)
    out_grad = tn(att_flat, mid_low)
    g_att = nt(mid_low, out_weight).astype(BF16).reshape(held, rows, lw)
    g_qkv = attention_backward(qkv, key_bias, attended, stat, g_att)
    g_qkv = g_qkv.reshape(held * rows, 3 * lw)
    qkv_grad = tn(g_qkv, low_one)
    column_sums = jnp.sum(g_qkv.astype(F32), 0)
    h_one_parts = nt(g_qkv, flat_qkv).astype(BF16).reshape(held, rows, width)
    g_h_one = scatter_mp(h_one_parts)
    normed_one, inverse_one = norm_stats(x_own)
    g_norm_one, gain_one, bias_one = norm_backward(g_h_one, normed_one, inverse_one, norm1_gain)
    extra = jnp.stack([*high_low(gain_one), *high_low(bias_one)])
    extra = jnp.pad(extra, ((0, 4), (0, 0)))
    patch_all = gather_mp(jnp.concatenate([(g_mid + g_norm_one).astype(BF16), extra]))
    patches_grad = patch_all[:, :vis].reshape(held * vis, width).astype(F32)
    extra_one = jnp.sum(patch_all[:, rows:].astype(F32), 0)

    mixed = jnp.concatenate(
        [
            column_sums[:lw],
            column_sums[2 * lw :],
            dec_bias_grad,
            mask_grad[0],
            jnp.zeros((width - 2 * lw - 2 * feats,), F32),
        ]
    )
    vectors = jnp.stack(
        [
            extra_one[0] + extra_one[1],
            extra_one[2] + extra_one[3],
            extra_two[0] + extra_two[1],
            extra_two[2] + extra_two[3],
            out_bias_grad,
            down_bias_grad,
            up_bias_grad,
            mixed,
        ]
    )
    rest = jnp.concatenate([out_grad, qkv_grad, dec_grad, vectors])
    rest = jnp.pad(rest, ((0, -rest.shape[0] % (8 * n)), (0, 0)))
    rest = sum_dp(rest)
    out_grad = rest[:lw]
    qkv_grad = rest[lw : 4 * lw].T.reshape(width, 3, lw)
    dec_grad = rest[4 * lw : 4 * lw + feats].T
    vectors = rest[4 * lw + feats : 4 * lw + feats + 8]
    mixed = vectors[7]
    return (
        decoded,
        patches_grad,
        vectors[0],
        vectors[1],
        qkv_grad,
        mixed[: 2 * lw].reshape(2, lw),
        out_grad,
        vectors[4],
        vectors[2],
        vectors[3],
        ff_grads[:width],
        vectors[6],
        ff_grads[width:],
        vectors[5],
        dec_grad,
        mixed[2 * lw : 2 * lw + feats],
        mixed[2 * lw + feats : 2 * lw + 2 * feats],
    )


def solution(mesh):
    return jax.shard_map(
        shards,
        mesh=mesh,
        in_specs=(
            P("dp", None),
            P(),
            P(),
            P(None, None, "mp"),
            P(None, "mp"),
            P("mp", None),
            P(),
            P(),
            P(),
            P(None, "mp"),
            P("mp"),
            P("mp", None),
            P(),
            P(None, "mp"),
            P("mp"),
            P("mp"),
            P(),
            P(),
            P(),
            P(),
            P("dp", None, "mp"),
        ),
        out_specs=(
            P("dp", None, "mp"),
            P("dp", None),
            P(),
            P(),
            P(None, None, "mp"),
            P(None, "mp"),
            P("mp", None),
            P(),
            P(),
            P(),
            P(None, "mp"),
            P("mp"),
            P("mp", None),
            P(),
            P(None, "mp"),
            P("mp"),
            P("mp"),
        ),
        check_vma=False,
    )
```

```python
from functools import partial

import jax
import jax.numpy as jnp
import numpy as np
from jax import lax
from jax.experimental import pallas as pl
from jax.experimental.pallas import tpu as pltpu
from jax.sharding import PartitionSpec as P

HD = 64
EPSILON = 1e-06
NEGATIVE = -1e30
F32 = jnp.float32
BF16 = jnp.bfloat16


def nn(a, b):
    return lax.dot_general(a, b, (((1,), (0,)), ((), ())), preferred_element_type=F32)


def tn(a, b):
    return lax.dot_general(a, b, (((0,), (0,)), ((), ())), preferred_element_type=F32)


def nt(a, b):
    return lax.dot_general(a, b, (((1,), (1,)), ((), ())), preferred_element_type=F32)


def norm_stats(inputs):
    centered = inputs - jnp.mean(inputs, -1, keepdims=True)
    inverse = lax.rsqrt(jnp.mean(centered * centered, -1, keepdims=True) + EPSILON)
    return centered * inverse, inverse


def norm_backward(incoming, normed, inverse, gain_vec):
    weighted = incoming * gain_vec
    inner = (
        weighted
        - jnp.mean(weighted, -1, keepdims=True)
        - normed * jnp.mean(weighted * normed, -1, keepdims=True)
    )
    return inner * inverse, jnp.sum(incoming * normed, 0), jnp.sum(incoming, 0)


def prepare_kernel(held_ref, len_ref, pos_ref, cot_ref, vis_ref, blank_ref, out_ref, mask_ref, bias_ref):
    @pl.when(pl.program_id(0) == 0)
    def _():
        mask_ref[...] = jnp.zeros_like(mask_ref)

    seq = cot_ref.shape[1]
    n, _, chunk, feats = out_ref.shape
    rows = bias_ref.shape[2]
    spot = lax.broadcasted_iota(jnp.int32, (n * chunk, seq), 1)
    chosen = (pos_ref[0] == spot).astype(F32)
    picked = nn(chosen.astype(BF16), cot_ref[0])
    out_ref[...] = picked.astype(BF16).reshape(n, 1, chunk, feats)
    hidden = 1.0 - jnp.sum(chosen, 0, keepdims=True)
    hidden = jnp.broadcast_to(hidden, (8, seq)).astype(BF16)
    mask_ref[...] += nn(hidden, cot_ref[0])
    place = lax.broadcasted_iota(jnp.int32, (1, seq), 1)
    usable = (blank_ref[0] == 0) & (place < len_ref[pl.program_id(0)])
    usable = jnp.broadcast_to(usable.astype(F32), (8, seq)).astype(BF16)
    at = lax.broadcasted_iota(jnp.int32, (seq, rows), 0)
    allowed = nn(usable, (vis_ref[0] == at).astype(F32).astype(BF16))
    bias_ref[0] = jnp.where(allowed[:1] > 0.5, 0.0, NEGATIVE)


def prepare(held_strips, lengths, pos_col, cot, vis, blank, n, chunk):
    held, seq, feats = cot.shape
    rows = vis.shape[2]
    return pl.pallas_call(
        prepare_kernel,
        grid_spec=pltpu.PrefetchScalarGridSpec(
            num_scalar_prefetch=2,
            grid=(held,),
            in_specs=[
                pl.BlockSpec((1, n * chunk, 1), lambda s, h, l: (s, 0, 0)),
                pl.BlockSpec((1, seq, feats), lambda s, h, l: (s, 0, 0)),
                pl.BlockSpec((1, 1, rows), lambda s, h, l: (h[s], 0, 0)),
                pl.BlockSpec((1, 1, seq), lambda s, h, l: (h[s], 0, 0)),
            ],
            out_specs=[
                pl.BlockSpec((n, 1, chunk, feats), lambda s, h, l: (0, s, 0, 0)),
                pl.BlockSpec((8, feats), lambda s, h, l: (0, 0)),
                pl.BlockSpec((1, 1, rows), lambda s, h, l: (s, 0, 0)),
            ],
        ),
        out_shape=[
            jax.ShapeDtypeStruct((n, held, chunk, feats), BF16),
            jax.ShapeDtypeStruct((8, feats), F32),
            jax.ShapeDtypeStruct((held, 1, rows), F32),
        ],
        name="prepare",
        compiler_params=pltpu.CompilerParams(vmem_limit_bytes=24 << 20),
    )(held_strips, lengths, pos_col, cot, vis, blank)


def put_rows_kernel(pos_ref, rows_ref, token_ref, out_ref):
    n, _, chunk, feats = rows_ref.shape
    seq = out_ref.shape[1]
    spot = lax.broadcasted_iota(jnp.int32, (seq, n * chunk), 0)
    chosen = (pos_ref[0] == spot).astype(F32)
    rows = nn(chosen.astype(BF16), rows_ref[...].reshape(n * chunk, feats))
    hidden = 1.0 - jnp.sum(chosen, 1, keepdims=True)
    out_ref[0] = (rows + hidden * token_ref[...].astype(BF16).astype(F32)).astype(BF16)


def put_rows(pos_row, rows, token, seq):
    n, held, chunk, feats = rows.shape
    return pl.pallas_call(
        put_rows_kernel,
        grid=(held,),
        in_specs=[
            pl.BlockSpec((1, 1, n * chunk), lambda s: (s, 0, 0)),
            pl.BlockSpec((n, 1, chunk, feats), lambda s: (0, s, 0, 0)),
            pl.BlockSpec((1, feats), lambda s: (0, 0)),
        ],
        out_specs=pl.BlockSpec((1, seq, feats), lambda s: (s, 0, 0)),
        out_shape=jax.ShapeDtypeStruct((held, seq, feats), BF16),
        name="put_rows",
        compiler_params=pltpu.CompilerParams(vmem_limit_bytes=24 << 20),
    )(pos_row, rows, token.reshape(1, feats))


MESH = pl.DeviceIdType.MESH


class Wires:
    def __init__(self, send, recv):
        self.send, self.recv, self.used = send, recv, 0

    def take(self, count=1):
        first = self.used
        self.used += count
        return first

    def copy(self, src, dst, index, target):
        return pltpu.make_async_remote_copy(
            src_ref=src,
            dst_ref=dst,
            send_sem=self.send.at[index],
            recv_sem=self.recv.at[index],
            device_id=target,
            device_id_type=MESH,
        )

    def start(self, src, dst, target):
        made = self.copy(src, dst, self.take(), target)
        made.start()
        return made


class Place:
    def __init__(self, n):
        self.n = n
        self.d = lax.axis_index("dp")
        self.m = lax.axis_index("mp")
        self.core, self.y = self.m % 2, self.m // 2
        self.core_peer = (self.d, self.m + 1 - 2 * self.core)
        self.y_peer = (self.d, (self.m + 2) % 4)
        self.y_strip = (self.m + 2) % 4
        oc, oy = 1 - self.core, 1 - self.y
        self.order = [2 * oy + oc, 2 * oy + self.core, 2 * self.y + oc, self.m]

    def dp_peer(self, k):
        return ((self.d + k) % self.n, self.m)


def meet(peers):
    barrier = pltpu.get_barrier_semaphore()
    for peer in peers:
        pl.semaphore_signal(barrier, inc=1, device_id=peer, device_id_type=MESH)
    return barrier


def meet_all(place):
    barrier = pltpu.get_barrier_semaphore()
    for peer in (place.core_peer, place.y_peer):
        pl.semaphore_signal(barrier, inc=1, device_id=peer, device_id_type=MESH)

    def greet(k, carry):
        pl.semaphore_signal(barrier, inc=1, device_id=place.dp_peer(k), device_id_type=MESH)
        return carry

    lax.fori_loop(1, place.n, greet, 0)
    pl.semaphore_wait(barrier, place.n + 1)


class Spread:
    def __init__(self, wires, place, src, dst):
        self.wires, self.place, self.src, self.dst = wires, place, src, dst
        self.base = wires.take(place.n)

    def made(self, k):
        peer = self.place.dp_peer(k)
        return self.wires.copy(
            self.src.at[peer[0]], self.dst.at[self.place.d], self.base + k, peer
        )

    def start(self):
        def one(k, carry):
            self.made(k).start()
            return carry

        lax.fori_loop(1, self.place.n, one, 0)
        self.dst[self.place.d] = self.src[self.place.d]

    def wait(self):
        def one(k, carry):
            self.made(k).wait()
            return carry

        lax.fori_loop(1, self.place.n, one, 0)


class Scatter:
    def __init__(self, wires, place, core_send, core_recv, y_send, y_recv):
        self.wires, self.place = wires, place
        self.core_send, self.core_recv, self.y_send, self.y_recv = core_send, core_recv, y_send, y_recv
        self.core = [None, None]

    def give_core(self, i, value):
        self.core_send[i] = value.astype(BF16)
        self.core[i] = self.wires.start(
            self.core_send.at[i], self.core_recv.at[i], self.place.core_peer
        )

    def give_y(self, value):
        self.core[0].wait_recv()
        self.y_send[...] = (value + self.core_recv[0].astype(F32)).astype(BF16)
        self.start_y()

    def start_y(self):
        self.away = self.wires.start(self.y_send, self.y_recv, self.place.y_peer)

    def own(self, value):
        self.core[1].wait_recv()
        self.away.wait_recv()
        return value + self.core_recv[1].astype(F32) + self.y_recv[...].astype(F32)

    def close(self):
        for made in (*self.core, self.away):
            made.wait_send()


class Gather:
    def __init__(self, wires, place, full, src=None):
        self.wires, self.place, self.full = wires, place, full
        self.src = full.at[place.m] if src is None else src

    def start(self):
        p = self.place
        spot = self.full.at[p.m]
        self.over_y = self.wires.start(self.src, spot, p.y_peer)
        self.over_core = self.wires.start(self.src, spot, p.core_peer)

    def forward(self):
        p = self.place
        self.over_y.wait_recv()
        spot = self.full.at[p.y_strip]
        self.passed = self.wires.start(spot, spot, p.core_peer)

    def wait(self):
        self.over_core.wait_recv()
        self.passed.wait_recv()

    def close(self):
        for made in (self.over_y, self.over_core, self.passed):
            made.wait_send()


def softmax_heads(qkv_ref, s, bias, lw):
    stats, outs = [], []
    for h in range(lw // HD):
        q = qkv_ref[s, :, h * HD : (h + 1) * HD]
        k = qkv_ref[s, :, lw + h * HD : lw + (h + 1) * HD]
        v = qkv_ref[s, :, 2 * lw + h * HD : 2 * lw + (h + 1) * HD]
        scores = nt(q, k) + bias
        top = jnp.max(scores, -1, keepdims=True)
        e = jnp.exp(scores - top)
        total = jnp.sum(e, -1, keepdims=True)
        outs.append((nn(e.astype(BF16), v) / total).astype(BF16))
        stats.append(top + jnp.log(total))
    lane = lax.broadcasted_iota(jnp.int32, (bias_rows(qkv_ref), 128), 1)
    stat = jnp.zeros((bias_rows(qkv_ref), 128), F32)
    for h, column in enumerate(stats):
        stat = jnp.where(lane == h, column, stat)
    return jnp.concatenate(outs, -1), stat


def bias_rows(qkv_ref):
    return qkv_ref.shape[1]


def forward_kernel(
    n,
    order_ref,
    x_ref,
    gain1_ref,
    shift1_ref,
    qkv_w_ref,
    qkv_b_ref,
    qkv_s_ref,
    out_w_ref,
    out_b_ref,
    gain2_ref,
    shift2_ref,
    bias_ref,
    cot_ref,
    col_ref,
    dec_w_ref,
    low_ref,
    qkv_ref,
    att_ref,
    stat_ref,
    mid_ref,
    low2_ref,
    g_ref,
    dec_ref,
    core_send,
    core_recv,
    y_send,
    y_recv,
    hop1,
    send2,
    hop2,
    send_sem,
    recv_sem,
):
    place = Place(n)
    wires = Wires(send_sem, recv_sem)
    lw = att_ref.shape[2]
    held, rows, width = x_ref.shape
    chunk, feats = hop1.shape[2:]
    meet_all(place)

    decs = Gather(wires, place, dec_ref, dec_w_ref)
    decs.start()
    dec_ref[place.m] = dec_w_ref[...]
    first = Spread(wires, place, cot_ref, hop1)
    first.start()

    def strip(s):
        normed, _ = norm_stats(x_ref[s].astype(F32))
        low_ref[s] = (normed * gain1_ref[...] + shift1_ref[...]).astype(BF16)
        proj = (nn(low_ref[s], qkv_w_ref[...]) + qkv_b_ref[...]) * qkv_s_ref[...]
        qkv_ref[s] = proj.astype(BF16)
        att, stat = softmax_heads(qkv_ref, s, bias_ref[s], lw)
        att_ref[s] = att
        stat_ref[s] = stat
        return nn(att_ref[s], out_w_ref[...])

    summed = Scatter(wires, place, core_send, core_recv, y_send, y_recv)
    summed.give_core(0, strip(place.order[0]))
    summed.give_y(strip(place.order[1]))
    decs.forward()
    summed.give_core(1, strip(place.order[2]))
    first.wait()
    second = Spread(wires, place, send2, hop2)

    def regroup(k, carry):
        j = order_ref[k]
        send2[k // held, k % held] = hop1[j // held, j % held]
        return carry

    lax.fori_loop(0, n * held, regroup, 0)
    second.start()
    own = strip(place.order[3])
    mid = x_ref[place.m].astype(F32) + out_b_ref[...] + summed.own(own)
    mid_ref[...] = mid
    normed, _ = norm_stats(mid)
    low2_ref[place.m] = (normed * gain2_ref[...] + shift2_ref[...]).astype(BF16)
    rows2 = Gather(wires, place, low2_ref)
    rows2.start()
    second.wait()
    t = lax.broadcasted_iota(jnp.int32, (rows, n * chunk), 0)
    sel = (t == col_ref[...]).astype(F32).astype(BF16)
    for s in range(held):
        g_ref[s] = nn(sel, hop2[:, s].reshape(n * chunk, feats)).astype(BF16)
    decs.wait()
    rows2.forward()
    rows2.wait()
    decs.close()
    rows2.close()
    summed.close()


def vmem(count):
    return [pl.BlockSpec(memory_space=pltpu.VMEM)] * count


def forward(n, order, x, *rest):
    held, rows, width = x.shape
    qkv_w, out_w = rest[2], rest[5]
    cot, dec_w = rest[10], rest[12]
    wide, lw = qkv_w.shape[1], out_w.shape[0]
    _, _, chunk, feats = cot.shape
    shape = jax.ShapeDtypeStruct
    sems = 3 * n + 16
    return pl.pallas_call(
        partial(forward_kernel, n),
        in_specs=[pl.BlockSpec(memory_space=pltpu.SMEM)] + vmem(1 + len(rest)),
        out_specs=vmem(8),
        out_shape=[
            shape((held, rows, width), BF16),
            shape((held, rows, wide), BF16),
            shape((held, rows, lw), BF16),
            shape((held, rows, 128), F32),
            shape((rows, width), F32),
            shape((held, rows, width), BF16),
            shape((held, rows, feats), BF16),
            shape((4, *dec_w.shape), BF16),
        ],
        scratch_shapes=[
            pltpu.VMEM((2, rows, width), BF16),
            pltpu.VMEM((2, rows, width), BF16),
            pltpu.VMEM((rows, width), BF16),
            pltpu.VMEM((rows, width), BF16),
            pltpu.VMEM((n, held, chunk, feats), BF16),
            pltpu.VMEM((n, held, chunk, feats), BF16),
            pltpu.VMEM((n, held, chunk, feats), BF16),
            pltpu.SemaphoreType.DMA((sems,)),
            pltpu.SemaphoreType.DMA((sems,)),
        ],
        name="forward",
        compiler_params=pltpu.CompilerParams(
            collective_id=0, has_side_effects=True, vmem_limit_bytes=56 << 20
        ),
    )(order, x, *rest)


def attention_backward_kernel(qkv_ref, bias_ref, att_ref, stat_ref, grad_ref, out_ref):
    lw = att_ref.shape[2]
    scale = HD ** (-0.5)
    bias = bias_ref[0]
    dq, dk, dv = [], [], []
    for h in range(lw // HD):
        q = qkv_ref[0, :, h * HD : (h + 1) * HD]
        k = qkv_ref[0, :, lw + h * HD : lw + (h + 1) * HD]
        v = qkv_ref[0, :, 2 * lw + h * HD : 2 * lw + (h + 1) * HD]
        g = grad_ref[0, :, h * HD : (h + 1) * HD]
        o = att_ref[0, :, h * HD : (h + 1) * HD]
        s = nt(q, k) + bias
        p = jnp.exp(s - stat_ref[0, :, h : h + 1])
        dv.append(tn(p.astype(BF16), g).astype(BF16))
        inner = jnp.sum(g.astype(F32) * o.astype(F32), -1, keepdims=True)
        ds = (p * (nt(g, v) - inner)).astype(BF16)
        dq.append((nn(ds, k) * scale).astype(BF16))
        dk.append(tn(ds, q).astype(BF16))
    out_ref[0] = jnp.concatenate(dq + dk + dv, -1)


def attention_backward(qkv, bias, att, stat, grad):
    held, rows, wide = qkv.shape
    lw = wide // 3
    block = lambda w: pl.BlockSpec((1, rows, w), lambda s: (s, 0, 0))
    return pl.pallas_call(
        attention_backward_kernel,
        grid=(held,),
        in_specs=[
            block(wide),
            pl.BlockSpec((1, 1, rows), lambda s: (s, 0, 0)),
            block(lw),
            block(128),
            block(lw),
        ],
        out_specs=block(wide),
        out_shape=jax.ShapeDtypeStruct((held, rows, wide), BF16),
        name="attention_backward",
        compiler_params=pltpu.CompilerParams(vmem_limit_bytes=32 << 20),
    )(qkv, bias, att, stat, grad)


def over_core(x):
    return lax.ppermute(x, "mp", [(i, i ^ 1) for i in range(lax.axis_size("mp"))])


def over_y(x):
    return lax.ppermute(x, "mp", [(i, i ^ 2) for i in range(lax.axis_size("mp"))])


def pick(x, index, axis):
    return lax.dynamic_index_in_dim(x, index, axis, keepdims=False)


def scatter_mp(parts):
    m = lax.axis_index("mp")
    core, y = m % 2, m // 2
    square = parts.reshape(2, 2, *parts.shape[1:])
    got = over_core(pick(square, 1 - core, 1))
    total = pick(square, core, 1).astype(F32) + got.astype(F32)
    away = over_y(pick(total, 1 - y, 0).astype(BF16))
    return pick(total, y, 0) + away.astype(F32)


def gather_mp(own):
    m = lax.axis_index("mp")
    core, y = m % 2, m // 2
    other = over_y(own)
    pair = jnp.stack([jnp.where(y == 0, own, other), jnp.where(y == 0, other, own)])
    twin = over_core(pair)
    square = jnp.stack([jnp.where(core == 0, pair, twin), jnp.where(core == 0, twin, pair)], 1)
    return square.reshape(4, *own.shape)


def sum_dp(x):
    count = lax.axis_size("dp")
    d = lax.axis_index("dp")
    bits = count.bit_length() - 1
    swap = lambda v, b: lax.ppermute(v, "dp", [(i, i ^ (1 << b)) for i in range(count)])
    for b in range(bits):
        half = x.shape[0] // 2
        up = (d >> b) % 2 == 1
        low_half, high_half = x[:half], x[half:]
        send = jnp.where(up, low_half, high_half).astype(BF16)
        x = jnp.where(up, high_half, low_half) + swap(send, b).astype(F32)
    x = x.astype(BF16)
    for b in reversed(range(bits)):
        up = (d >> b) % 2 == 1
        got = swap(x, b)
        x = jnp.where(up, jnp.concatenate([got, x]), jnp.concatenate([x, got]))
    return x.astype(F32)


def high_low(vec):
    high = vec.astype(BF16)
    return high, (vec - high.astype(F32)).astype(BF16)


def shards(
    patches,
    norm1_gain,
    norm1_bias,
    qkv_weight,
    qv_bias,
    out_weight,
    out_bias,
    norm2_gain,
    norm2_bias,
    up_weight,
    up_bias,
    down_weight,
    down_bias,
    dec_weight,
    dec_bias,
    mask_token,
    lengths,
    blank,
    visible,
    plan,
    dec_cot,
):
    n = lax.axis_size("dp")
    d = lax.axis_index("dp")
    m = lax.axis_index("mp")
    held, seq, feats = dec_cot.shape
    vis = visible.shape[1]
    strips = plan.shape[0]
    width = patches.shape[1]
    lw = qkv_weight.shape[2]
    rows = -(-vis // 16) * 16
    real = -(-vis // n)
    chunk = -(-real // 8) * 8
    scale = HD ** (-0.5)

    strip_ids = jnp.arange(strips, dtype=jnp.int32)
    earlier = (plan[None, :] == plan[:, None]) & (strip_ids[None, :] < strip_ids[:, None])
    packed_at = plan * held + jnp.sum(earlier.astype(jnp.int32), 1)
    strip_at = jnp.sum(
        jnp.where(packed_at[None, :] == strip_ids[:, None], strip_ids[None, :], 0), 1
    )
    held_strips = lax.dynamic_slice_in_dim(strip_at, d * held, held)
    owned_pos = lax.dynamic_slice_in_dim(visible, d * held, held)
    owned_pos = jnp.pad(owned_pos, ((0, 0), (0, n * real - vis)), constant_values=-1)
    owned_pos = jnp.pad(
        owned_pos.reshape(held, n, real), ((0, 0), (0, 0), (0, chunk - real)), constant_values=-1
    )

    def exchange(spread, order):
        swap = partial(lax.all_to_all, axis_name="dp", split_axis=0, concat_axis=0, tiled=True)
        midway = swap(spread).reshape(strips, chunk, feats)
        return swap(midway[order].reshape(n, held, chunk, feats))

    vis_rows = jnp.pad(visible, ((0, 0), (0, rows - vis)), constant_values=-1)
    spread_cot, mask_grad, key_bias = prepare(
        held_strips,
        lengths[held_strips],
        owned_pos.reshape(held, n * chunk, 1),
        dec_cot,
        vis_rows.reshape(strips, 1, rows),
        blank.reshape(strips, 1, seq),
        n,
        chunk,
    )
    spot = np.arange(n * chunk)
    spot = np.where(spot % chunk < real, spot // chunk * real + spot % chunk, -1)
    x_all = jnp.pad(patches.reshape(held, vis, width), ((0, 0), (0, rows - vis), (0, 0)))
    row = lambda v: v.reshape(1, -1)
    flat_qkv = qkv_weight.reshape(width, 3 * lw)
    qkv_shift = jnp.concatenate([qv_bias[0], jnp.zeros((lw,), F32), qv_bias[1]])
    qkv_scale = np.where(np.arange(3 * lw) < lw, scale, 1.0).astype(np.float32)
    low_one, qkv, attended, stat, mid, low_two, g_rows, dec_all = forward(
        n,
        strip_at,
        x_all,
        row(norm1_gain),
        row(norm1_bias),
        flat_qkv,
        row(qkv_shift),
        row(jnp.asarray(qkv_scale)),
        out_weight,
        row(out_bias),
        row(norm2_gain),
        row(norm2_bias),
        key_bias,
        spread_cot,
        row(jnp.asarray(spot, jnp.int32)),
        dec_weight,
    )
    low_one = low_one.reshape(held * rows, width)
    low_two = low_two.reshape(held * rows, width)
    g_rows = g_rows.reshape(held * rows, feats)
    att_flat = attended.reshape(held * rows, lw)
    x_own = pick(x_all, m, 0).astype(F32)
    normed_two, inverse_two = norm_stats(mid)
    dec_bias_grad = jnp.sum(g_rows.astype(F32), 0)
    g_all = gather_mp(g_rows)
    parts = range(4)
    g_three = nt(
        jnp.concatenate([g_all[i] for i in parts], 1),
        jnp.concatenate([dec_all[i] for i in parts], 1),
    )
    g_three_low = g_three.astype(BF16)
    down_bias_grad = jnp.sum(g_three, 0)

    before = nn(low_two, up_weight) + up_bias
    half = 0.5 * (1.0 + lax.erf(before * np.float32(0.5**0.5)))
    act = (before * half).astype(BF16)
    slope = half + before * jnp.exp(-0.5 * before * before) * np.float32((2 * np.pi) ** -0.5)
    slope = lax.optimization_barrier(slope)
    g_before = (nt(g_three_low, down_weight) * slope).astype(BF16)
    h_two_parts = nt(g_before, up_weight).astype(BF16).reshape(held, rows, width)
    g_h_two = scatter_mp(h_two_parts)
    g_norm_two, gain_two, bias_two = norm_backward(g_h_two, normed_two, inverse_two, norm2_gain)
    g_mid = pick(g_three.reshape(held, rows, width), m, 0) + g_norm_two
    extra = jnp.stack([*high_low(gain_two), *high_low(bias_two)])
    extra = jnp.pad(extra, ((0, 4), (0, 0)))
    mid_all = gather_mp(jnp.concatenate([g_mid.astype(BF16), extra]))
    mid_low = mid_all[:, :rows].reshape(held * rows, width)
    extra_two = jnp.sum(mid_all[:, rows:].astype(F32), 0)

    up_bias_grad = jnp.sum(g_before.astype(F32), 0)
    up_grad = tn(low_two, g_before)
    down_grad = tn(act, g_three_low)
    ff_grads = sum_dp(jnp.concatenate([up_grad, down_grad]))

    ffn_parts = nn(act, down_weight).astype(BF16).reshape(held, rows, width)
    final = mid + scatter_mp(ffn_parts) + down_bias
    final_low = gather_mp(final.astype(BF16)).reshape(held * rows, width)
    projected = (nn(final_low, dec_weight) + dec_bias).astype(BF16).reshape(held, rows, feats)
    if n * real > rows:
        projected = jnp.pad(projected, ((0, 0), (0, n * real - rows), (0, 0)))
    spread = projected[:, : n * real].reshape(held, n, real, feats)
    spread = jnp.pad(spread, ((0, 0), (0, 0), (0, chunk - real), (0, 0))).transpose(1, 0, 2, 3)
    arrived = exchange(spread, packed_at)
    decoded = put_rows(owned_pos.reshape(held, 1, n * chunk), arrived, mask_token, seq)
    dec_grad = tn(g_rows, final_low)

    out_bias_grad = jnp.sum(mid_low.astype(F32), 0)
    out_grad = tn(att_flat, mid_low)
    g_att = nt(mid_low, out_weight).astype(BF16).reshape(held, rows, lw)
    g_qkv = attention_backward(qkv, key_bias, attended, stat, g_att)
    g_qkv = g_qkv.reshape(held * rows, 3 * lw)
    qkv_grad = tn(g_qkv, low_one)
    column_sums = jnp.sum(g_qkv.astype(F32), 0)
    h_one_parts = nt(g_qkv, flat_qkv).astype(BF16).reshape(held, rows, width)
    g_h_one = scatter_mp(h_one_parts)
    normed_one, inverse_one = norm_stats(x_own)
    g_norm_one, gain_one, bias_one = norm_backward(g_h_one, normed_one, inverse_one, norm1_gain)
    extra = jnp.stack([*high_low(gain_one), *high_low(bias_one)])
    extra = jnp.pad(extra, ((0, 4), (0, 0)))
    patch_all = gather_mp(jnp.concatenate([(g_mid + g_norm_one).astype(BF16), extra]))
    patches_grad = patch_all[:, :vis].reshape(held * vis, width).astype(F32)
    extra_one = jnp.sum(patch_all[:, rows:].astype(F32), 0)

    mixed = jnp.concatenate(
        [
            column_sums[:lw],
            column_sums[2 * lw :],
            dec_bias_grad,
            mask_grad[0],
            jnp.zeros((width - 2 * lw - 2 * feats,), F32),
        ]
    )
    vectors = jnp.stack(
        [
            extra_one[0] + extra_one[1],
            extra_one[2] + extra_one[3],
            extra_two[0] + extra_two[1],
            extra_two[2] + extra_two[3],
            out_bias_grad,
            down_bias_grad,
            up_bias_grad,
            mixed,
        ]
    )
    rest = jnp.concatenate([out_grad, qkv_grad, dec_grad, vectors])
    rest = jnp.pad(rest, ((0, -rest.shape[0] % (8 * n)), (0, 0)))
    rest = sum_dp(rest)
    out_grad = rest[:lw]
    qkv_grad = rest[lw : 4 * lw].T.reshape(width, 3, lw)
    dec_grad = rest[4 * lw : 4 * lw + feats].T
    vectors = rest[4 * lw + feats : 4 * lw + feats + 8]
    mixed = vectors[7]
    return (
        decoded,
        patches_grad,
        vectors[0],
        vectors[1],
        qkv_grad,
        mixed[: 2 * lw].reshape(2, lw),
        out_grad,
        vectors[4],
        vectors[2],
        vectors[3],
        ff_grads[:width],
        vectors[6],
        ff_grads[width:],
        vectors[5],
        dec_grad,
        mixed[2 * lw : 2 * lw + feats],
        mixed[2 * lw + feats : 2 * lw + 2 * feats],
    )


def solution(mesh):
    return jax.shard_map(
        shards,
        mesh=mesh,
        in_specs=(
            P("dp", None),
            P(),
            P(),
            P(None, None, "mp"),
            P(None, "mp"),
            P("mp", None),
            P(),
            P(),
            P(),
            P(None, "mp"),
            P("mp"),
            P("mp", None),
            P(),
            P(None, "mp"),
            P("mp"),
            P("mp"),
            P(),
            P(),
            P(),
            P(),
            P("dp", None, "mp"),
        ),
        out_specs=(
            P("dp", None, "mp"),
            P("dp", None),
            P(),
            P(),
            P(None, None, "mp"),
            P(None, "mp"),
            P("mp", None),
            P(),
            P(),
            P(),
            P(None, "mp"),
            P("mp"),
            P("mp", None),
            P(),
            P(None, "mp"),
            P("mp"),
            P("mp"),
        ),
        check_vma=False,
    )
```

```python
from functools import partial

import jax
import jax.numpy as jnp
import numpy as np
from jax import lax
from jax.experimental import pallas as pl
from jax.experimental.pallas import tpu as pltpu
from jax.sharding import PartitionSpec as P

HD = 64
EPSILON = 1e-06
NEGATIVE = -1e30
F32 = jnp.float32
BF16 = jnp.bfloat16


def nn(a, b):
    return lax.dot_general(a, b, (((1,), (0,)), ((), ())), preferred_element_type=F32)


def tn(a, b):
    return lax.dot_general(a, b, (((0,), (0,)), ((), ())), preferred_element_type=F32)


def nt(a, b):
    return lax.dot_general(a, b, (((1,), (1,)), ((), ())), preferred_element_type=F32)


def norm_stats(inputs):
    centered = inputs - jnp.mean(inputs, -1, keepdims=True)
    inverse = lax.rsqrt(jnp.mean(centered * centered, -1, keepdims=True) + EPSILON)
    return centered * inverse, inverse


def norm_backward(incoming, normed, inverse, gain_vec):
    weighted = incoming * gain_vec
    inner = (
        weighted
        - jnp.mean(weighted, -1, keepdims=True)
        - normed * jnp.mean(weighted * normed, -1, keepdims=True)
    )
    return inner * inverse, jnp.sum(incoming * normed, 0), jnp.sum(incoming, 0)


def prepare_kernel(held_ref, len_ref, pos_ref, cot_ref, vis_ref, blank_ref, out_ref, mask_ref, bias_ref):
    @pl.when(pl.program_id(0) == 0)
    def _():
        mask_ref[...] = jnp.zeros_like(mask_ref)

    seq = cot_ref.shape[1]
    n, _, chunk, feats = out_ref.shape
    rows = bias_ref.shape[2]
    spot = lax.broadcasted_iota(jnp.int32, (n * chunk, seq), 1)
    chosen = (pos_ref[0] == spot).astype(F32)
    picked = nn(chosen.astype(BF16), cot_ref[0])
    out_ref[...] = picked.astype(BF16).reshape(n, 1, chunk, feats)
    hidden = 1.0 - jnp.sum(chosen, 0, keepdims=True)
    hidden = jnp.broadcast_to(hidden, (8, seq)).astype(BF16)
    mask_ref[...] += nn(hidden, cot_ref[0])
    place = lax.broadcasted_iota(jnp.int32, (1, seq), 1)
    usable = (blank_ref[0] == 0) & (place < len_ref[pl.program_id(0)])
    usable = jnp.broadcast_to(usable.astype(F32), (8, seq)).astype(BF16)
    at = lax.broadcasted_iota(jnp.int32, (seq, rows), 0)
    allowed = nn(usable, (vis_ref[0] == at).astype(F32).astype(BF16))
    bias_ref[0] = jnp.where(allowed[:1] > 0.5, 0.0, NEGATIVE)


def prepare(held_strips, lengths, pos_col, cot, vis, blank, n, chunk):
    held, seq, feats = cot.shape
    rows = vis.shape[2]
    return pl.pallas_call(
        prepare_kernel,
        grid_spec=pltpu.PrefetchScalarGridSpec(
            num_scalar_prefetch=2,
            grid=(held,),
            in_specs=[
                pl.BlockSpec((1, n * chunk, 1), lambda s, h, l: (s, 0, 0)),
                pl.BlockSpec((1, seq, feats), lambda s, h, l: (s, 0, 0)),
                pl.BlockSpec((1, 1, rows), lambda s, h, l: (h[s], 0, 0)),
                pl.BlockSpec((1, 1, seq), lambda s, h, l: (h[s], 0, 0)),
            ],
            out_specs=[
                pl.BlockSpec((n, 1, chunk, feats), lambda s, h, l: (0, s, 0, 0)),
                pl.BlockSpec((8, feats), lambda s, h, l: (0, 0)),
                pl.BlockSpec((1, 1, rows), lambda s, h, l: (s, 0, 0)),
            ],
        ),
        out_shape=[
            jax.ShapeDtypeStruct((n, held, chunk, feats), BF16),
            jax.ShapeDtypeStruct((8, feats), F32),
            jax.ShapeDtypeStruct((held, 1, rows), F32),
        ],
        name="prepare",
        compiler_params=pltpu.CompilerParams(vmem_limit_bytes=24 << 20),
    )(held_strips, lengths, pos_col, cot, vis, blank)


def put_rows_kernel(pos_ref, rows_ref, token_ref, out_ref):
    n, _, chunk, feats = rows_ref.shape
    seq = out_ref.shape[1]
    spot = lax.broadcasted_iota(jnp.int32, (seq, n * chunk), 0)
    chosen = (pos_ref[0] == spot).astype(F32)
    rows = nn(chosen.astype(BF16), rows_ref[...].reshape(n * chunk, feats))
    hidden = 1.0 - jnp.sum(chosen, 1, keepdims=True)
    out_ref[0] = (rows + hidden * token_ref[...].astype(BF16).astype(F32)).astype(BF16)


def put_rows(pos_row, rows, token, seq):
    n, held, chunk, feats = rows.shape
    return pl.pallas_call(
        put_rows_kernel,
        grid=(held,),
        in_specs=[
            pl.BlockSpec((1, 1, n * chunk), lambda s: (s, 0, 0)),
            pl.BlockSpec((n, 1, chunk, feats), lambda s: (0, s, 0, 0)),
            pl.BlockSpec((1, feats), lambda s: (0, 0)),
        ],
        out_specs=pl.BlockSpec((1, seq, feats), lambda s: (s, 0, 0)),
        out_shape=jax.ShapeDtypeStruct((held, seq, feats), BF16),
        name="put_rows",
        compiler_params=pltpu.CompilerParams(vmem_limit_bytes=24 << 20),
    )(pos_row, rows, token.reshape(1, feats))


MESH = pl.DeviceIdType.MESH


class Wires:
    def __init__(self, send, recv):
        self.send, self.recv, self.used = send, recv, 0

    def take(self, count=1):
        first = self.used
        self.used += count
        return first

    def copy(self, src, dst, index, target):
        return pltpu.make_async_remote_copy(
            src_ref=src,
            dst_ref=dst,
            send_sem=self.send.at[index],
            recv_sem=self.recv.at[index],
            device_id=target,
            device_id_type=MESH,
        )

    def start(self, src, dst, target):
        made = self.copy(src, dst, self.take(), target)
        made.start()
        return made


class Place:
    def __init__(self, n):
        self.n = n
        self.d = lax.axis_index("dp")
        self.m = lax.axis_index("mp")
        self.core, self.y = self.m % 2, self.m // 2
        self.core_peer = (self.d, self.m + 1 - 2 * self.core)
        self.y_peer = (self.d, (self.m + 2) % 4)
        self.far_peer = (self.d, 3 - self.m)
        self.y_strip = (self.m + 2) % 4
        oc, oy = 1 - self.core, 1 - self.y
        self.order = [2 * oy + oc, 2 * oy + self.core, 2 * self.y + oc, self.m]

    def dp_peer(self, k):
        return ((self.d + k) % self.n, self.m)


def meet_all(place):
    barrier = pltpu.get_barrier_semaphore()
    for peer in (place.core_peer, place.y_peer, place.far_peer):
        pl.semaphore_signal(barrier, inc=1, device_id=peer, device_id_type=MESH)

    def greet(k, carry):
        pl.semaphore_signal(barrier, inc=1, device_id=place.dp_peer(k), device_id_type=MESH)
        return carry

    lax.fori_loop(1, place.n, greet, 0)
    pl.semaphore_wait(barrier, place.n + 2)


class Spread:
    def __init__(self, wires, place, src, dst):
        self.wires, self.place, self.src, self.dst = wires, place, src, dst
        self.base = wires.take(place.n)

    def made(self, k):
        peer = self.place.dp_peer(k)
        return self.wires.copy(
            self.src.at[peer[0]], self.dst.at[self.place.d], self.base + k, peer
        )

    def start(self):
        def one(k, carry):
            self.made(k).start()
            return carry

        lax.fori_loop(1, self.place.n, one, 0)
        self.dst[self.place.d] = self.src[self.place.d]

    def wait(self):
        def one(k, carry):
            self.made(k).wait()
            return carry

        lax.fori_loop(1, self.place.n, one, 0)


class Scatter:
    def __init__(self, wires, place, core_send, core_recv, y_send, y_recv):
        self.wires, self.place = wires, place
        self.core_send, self.core_recv, self.y_send, self.y_recv = core_send, core_recv, y_send, y_recv
        self.core = [None, None]

    def give_core(self, i, value):
        self.core_send[i] = value.astype(BF16)
        self.core[i] = self.wires.start(
            self.core_send.at[i], self.core_recv.at[i], self.place.core_peer
        )

    def give_y(self, value, start=True):
        self.core[0].wait_recv()
        self.y_send[...] = (value + self.core_recv[0].astype(F32)).astype(BF16)
        if start:
            self.start_y()

    def start_y(self):
        self.away = self.wires.start(self.y_send, self.y_recv, self.place.y_peer)

    def own(self, value):
        self.core[1].wait_recv()
        self.away.wait_recv()
        return value + self.core_recv[1].astype(F32) + self.y_recv[...].astype(F32)

    def close(self):
        for made in (*self.core, self.away):
            made.wait_send()


class Gather:
    def __init__(self, wires, place, full, src=None):
        self.wires, self.place, self.full = wires, place, full
        self.src = full.at[place.m] if src is None else src

    def start(self):
        p = self.place
        spot = self.full.at[p.m]
        self.over_y = self.wires.start(self.src, spot, p.y_peer)
        self.over_core = self.wires.start(self.src, spot, p.core_peer)

    def forward(self):
        p = self.place
        self.over_y.wait_recv()
        spot = self.full.at[p.y_strip]
        self.passed = self.wires.start(spot, spot, p.core_peer)

    def wait(self):
        self.over_core.wait_recv()
        self.passed.wait_recv()

    def close(self):
        for made in (self.over_y, self.over_core, self.passed):
            made.wait_send()


def softmax_heads(qkv_ref, s, bias, lw):
    stats, outs = [], []
    for h in range(lw // HD):
        q = qkv_ref[s, :, h * HD : (h + 1) * HD]
        k = qkv_ref[s, :, lw + h * HD : lw + (h + 1) * HD]
        v = qkv_ref[s, :, 2 * lw + h * HD : 2 * lw + (h + 1) * HD]
        scores = nt(q, k) + bias
        top = jnp.max(scores, -1, keepdims=True)
        e = jnp.exp(scores - top)
        total = jnp.sum(e, -1, keepdims=True)
        outs.append((nn(e.astype(BF16), v) / total).astype(BF16))
        stats.append(top + jnp.log(total))
    lane = lax.broadcasted_iota(jnp.int32, (bias_rows(qkv_ref), 128), 1)
    stat = jnp.zeros((bias_rows(qkv_ref), 128), F32)
    for h, column in enumerate(stats):
        stat = jnp.where(lane == h, column, stat)
    return jnp.concatenate(outs, -1), stat


def bias_rows(qkv_ref):
    return qkv_ref.shape[1]


def forward_kernel(
    n,
    order_ref,
    x_ref,
    gain1_ref,
    shift1_ref,
    qkv_w_ref,
    qkv_b_ref,
    qkv_s_ref,
    out_w_ref,
    out_b_ref,
    gain2_ref,
    shift2_ref,
    bias_ref,
    cot_ref,
    col_ref,
    dec_w_ref,
    low_ref,
    qkv_ref,
    att_ref,
    stat_ref,
    mid_ref,
    low2_ref,
    g_ref,
    dec_ref,
    own_ref,
    core_send,
    core_recv,
    y_send,
    y_recv,
    hop1,
    send2,
    hop2,
    send_sem,
    recv_sem,
):
    place = Place(n)
    wires = Wires(send_sem, recv_sem)
    lw = att_ref.shape[2]
    held, rows, width = x_ref.shape
    chunk, feats = hop1.shape[2:]
    meet_all(place)

    decs = Gather(wires, place, dec_ref, dec_w_ref)
    decs.start()
    dec_ref[place.m] = dec_w_ref[...]
    first = Spread(wires, place, cot_ref, hop1)
    first.start()

    def strip(s):
        normed, _ = norm_stats(x_ref[s].astype(F32))
        low_ref[s] = (normed * gain1_ref[...] + shift1_ref[...]).astype(BF16)
        proj = (nn(low_ref[s], qkv_w_ref[...]) + qkv_b_ref[...]) * qkv_s_ref[...]
        qkv_ref[s] = proj.astype(BF16)
        att, stat = softmax_heads(qkv_ref, s, bias_ref[s], lw)
        att_ref[s] = att
        stat_ref[s] = stat
        return nn(att_ref[s], out_w_ref[...])

    summed = Scatter(wires, place, core_send, core_recv, y_send, y_recv)
    summed.give_core(0, strip(place.order[0]))
    summed.give_y(strip(place.order[1]))
    decs.forward()
    summed.give_core(1, strip(place.order[2]))
    first.wait()
    second = Spread(wires, place, send2, hop2)

    def regroup(k, carry):
        j = order_ref[k]
        send2[k // held, k % held] = hop1[j // held, j % held]
        return carry

    lax.fori_loop(0, n * held, regroup, 0)
    second.start()
    own = strip(place.order[3])
    own_ref[...] = x_ref[place.m]
    mid = x_ref[place.m].astype(F32) + out_b_ref[...] + summed.own(own)
    mid_ref[...] = mid
    normed, _ = norm_stats(mid)
    low2_ref[place.m] = (normed * gain2_ref[...] + shift2_ref[...]).astype(BF16)
    rows2 = Gather(wires, place, low2_ref)
    rows2.start()
    second.wait()
    t = lax.broadcasted_iota(jnp.int32, (rows, n * chunk), 0)
    sel = (t == col_ref[...]).astype(F32).astype(BF16)
    for s in range(held):
        g_ref[s] = nn(sel, hop2[:, s].reshape(n * chunk, feats)).astype(BF16)
    decs.wait()
    rows2.forward()
    rows2.wait()
    decs.close()
    rows2.close()
    summed.close()


def vmem(count):
    return [pl.BlockSpec(memory_space=pltpu.VMEM)] * count


def forward(n, order, x, *rest):
    held, rows, width = x.shape
    qkv_w, out_w = rest[2], rest[5]
    cot, dec_w = rest[10], rest[12]
    wide, lw = qkv_w.shape[1], out_w.shape[0]
    _, _, chunk, feats = cot.shape
    shape = jax.ShapeDtypeStruct
    sems = 3 * n + 16
    return pl.pallas_call(
        partial(forward_kernel, n),
        in_specs=[pl.BlockSpec(memory_space=pltpu.SMEM)] + vmem(1 + len(rest)),
        out_specs=vmem(9),
        out_shape=[
            shape((held, rows, width), BF16),
            shape((held, rows, wide), BF16),
            shape((held, rows, lw), BF16),
            shape((held, rows, 128), F32),
            shape((rows, width), F32),
            shape((held, rows, width), BF16),
            shape((held, rows, feats), BF16),
            shape((4, *dec_w.shape), BF16),
            shape((rows, width), BF16),
        ],
        scratch_shapes=[
            pltpu.VMEM((2, rows, width), BF16),
            pltpu.VMEM((2, rows, width), BF16),
            pltpu.VMEM((rows, width), BF16),
            pltpu.VMEM((rows, width), BF16),
            pltpu.VMEM((n, held, chunk, feats), BF16),
            pltpu.VMEM((n, held, chunk, feats), BF16),
            pltpu.VMEM((n, held, chunk, feats), BF16),
            pltpu.SemaphoreType.DMA((sems,)),
            pltpu.SemaphoreType.DMA((sems,)),
        ],
        name="forward",
        compiler_params=pltpu.CompilerParams(
            collective_id=0, has_side_effects=True, vmem_limit_bytes=56 << 20
        ),
    )(order, x, *rest)


class Tell:
    def __init__(self, wires, place, src, dst):
        self.wires, self.place, self.src, self.dst = wires, place, src, dst
        self.base = wires.take(place.n)

    def made(self, k):
        peer = self.place.dp_peer(k)
        return self.wires.copy(self.src, self.dst.at[self.place.d], self.base + k, peer)

    wait = Spread.wait

    def start(self):
        def one(k, carry):
            self.made(k).start()
            return carry

        lax.fori_loop(1, self.place.n, one, 0)
        self.dst[self.place.d] = self.src[...]


def reduce_steps(wires, place, g, recv, h):
    n = place.n
    bits = n.bit_length() - 1
    base, size = 0, n
    path, sent = [], []
    for k in range(bits):
        half = size // 2
        bit = (place.d // (1 << k)) % 2
        peer = (place.d + (1 - 2 * bit) * (1 << k), place.m)
        keep, away, landing = base + bit * half, base + (1 - bit) * half, n - size
        made = wires.start(g.at[pl.ds(away, half)], recv.at[pl.ds(landing, half)], peer)
        sent.append(made)
        yield
        made.wait_recv()

        def add(i, carry):
            total = g[keep + i].astype(F32) + recv[landing + i].astype(F32)
            g[keep + i] = total.astype(BF16)
            return carry

        lax.fori_loop(0, half, add, 0)
        path.append((base, peer))
        base, size = keep, half
    h[base] = g[base]
    for start, peer in reversed(path):
        held = h.at[pl.ds(base, size)]
        made = wires.start(held, held, peer)
        sent.append(made)
        yield
        made.wait_recv()
        base, size = start, size * 2
    for made in sent:
        made.wait_send()


class Pump:
    def __init__(self, bits):
        self.todo = []
        steps = [7.0] + [4.0] * (bits - 1) + [4.0] * (bits - 1) + [7.0]
        self.after = [0.0]
        for step in steps:
            self.after.append(self.after[-1] + step)

    def add(self, when, steps, rate=1.0):
        for i, t in enumerate(self.after):
            self.todo.append((when + rate * t, len(self.todo), steps))
        self.todo.sort(key=lambda item: item[:2])

    def until(self, when):
        while self.todo and self.todo[0][0] <= when:
            next(self.todo.pop(0)[2], None)


def backward_kernel(
    n,
    order_ref,
    x_ref,
    low1_hbm,
    qkv_ref,
    att_ref,
    stat_ref,
    bias_ref,
    mid_ref,
    low2_ref,
    g_ref,
    decs_ref,
    up_w_ref,
    up_b_ref,
    down_w_ref,
    down_b_ref,
    dec_w_ref,
    dec_b_ref,
    out_w_ref,
    qkv_w_ref,
    gain1_ref,
    gain2_ref,
    col_ref,
    mask_ref,
    patch_ref,
    h_up,
    h_down,
    h_at,
    h_dec,
    hop4,
    vec_ref,
    act,
    slope,
    g3_low,
    g_full,
    h2_cs,
    h2_cr,
    h2_ys,
    h2_yr,
    ff_cs,
    ff_cr,
    ff_ys,
    ff_yr,
    own_a,
    own_b,
    own_c,
    acc,
    mid_all,
    dqkv,
    g_up,
    g_down,
    g_at,
    g_dec,
    r_up,
    r_down,
    r_at,
    r_dec,
    send3,
    hop3,
    v_own,
    v_all,
    w_own,
    w_all,
    copy_sem,
    send_sem,
    recv_sem,
):
    place = Place(n)
    wires = Wires(send_sem, recv_sem)
    held, rows, lw = att_ref.shape
    width = x_ref.shape[1]
    chunk, feats = hop4.shape[2:]
    parts = range(4)
    first, second, third, mine = place.order
    temp = acc.at[pl.ds(0, rows)]
    meet_all(place)

    gg = Gather(wires, place, g_full, g_ref)
    gg.start()
    g_full[place.m] = g_ref[...]
    v_own[...] = jnp.zeros_like(v_own)

    tall = 16

    def ff(s, carry):
        temp[...] = nn(low2_ref[s], up_w_ref[...]) + up_b_ref[...]

        def some(r, inner):
            at = pl.ds(pl.multiple_of(r * tall, tall), tall)
            pre = temp[at]
            half = 0.5 * (1.0 + lax.erf(pre * np.float32(0.5**0.5)))
            bell = jnp.exp(-0.5 * pre * pre) * np.float32((2 * np.pi) ** -0.5)
            act[s, at] = (pre * half).astype(BF16)
            slope[s, at] = (half + pre * bell).astype(BF16)
            return inner

        return lax.fori_loop(0, rows // tall, some, carry)

    lax.fori_loop(0, held, ff, 0)
    gg.forward()
    gg.wait()

    def g_three(s):
        weight = jnp.concatenate([decs_ref[i] for i in parts], 1)
        return nt(jnp.concatenate([g_full[i, s] for i in parts], 1), weight)

    def g_strip(s):
        g3_low[s] = g_three(s).astype(BF16)
        g_pre = nt(g3_low[s], down_w_ref[...]) * slope[s].astype(F32)
        slope[s] = g_pre.astype(BF16)
        v_own[6:7] += jnp.sum(g_pre, 0, keepdims=True)
        return nt(slope[s], up_w_ref[...])

    h2 = Scatter(wires, place, h2_cs, h2_cr, h2_ys, h2_yr)
    h2.give_core(0, g_strip(first))
    h2.give_y(g_strip(second))
    h2.give_core(1, g_strip(third))
    own_a[...] = g_strip(mine)

    ff_sum = Scatter(wires, place, ff_cs, ff_cr, ff_ys, ff_yr)
    ff_sum.give_core(0, nn(act[first], down_w_ref[...]))
    ff_sum.give_y(nn(act[second], down_w_ref[...]), start=False)
    ff_sum.give_core(1, nn(act[third], down_w_ref[...]))
    own_b[...] = nn(act[mine], down_w_ref[...]).astype(BF16)

    def weight_grad(left, right, out):
        acc[...] = jnp.zeros_like(acc)

        def add(s, carry):
            acc[...] += tn(left[s], right[s])
            return carry

        lax.fori_loop(0, held, add, 0)
        out[...] = acc[...].reshape(out.shape).astype(BF16)

    pump = Pump(n.bit_length() - 1)
    pieces = g_up.shape[0]
    weight_grad(low2_ref, slope, g_up)
    for i in range(pieces):
        pump.add(34.0 + 6.5 * i, reduce_steps(wires, place, g_up.at[i], r_up.at[i], h_up.at[i]))
    pump.until(35.0)
    weight_grad(act, g3_low, g_down)
    for i in range(pieces):
        pump.add(
            34.0 + 6.5 * (pieces + i),
            reduce_steps(wires, place, g_down.at[i], r_down.at[i], h_down.at[i]),
        )
    low1, fin_all = act, g3_low
    fetch = pltpu.make_async_copy(low1_hbm, low1, copy_sem)
    fetch.start()

    g_h2 = h2.own(own_a[...])
    h2.close()
    normed, inverse = norm_stats(mid_ref[...])
    g_own = g_three(place.m)
    g_norm, gain_sum, bias_sum = norm_backward(g_h2, normed, inverse, gain2_ref[...])
    g_mid = g_own + g_norm
    own_a[...] = g_mid
    mid_all[place.m] = g_mid.astype(BF16)
    gm = Gather(wires, place, mid_all)
    gm.start()
    total = lambda v: jnp.sum(v, 0, keepdims=True)
    v_own[2:3] = gain_sum.reshape(1, width)
    v_own[3:4] = bias_sum.reshape(1, width)
    v_own[4:5] = total(g_mid)
    v_own[5:6] = total(g_own)
    pump.until(41.0)

    scale = HD ** (-0.5)

    def attend(s):
        grad = nt(mid_all[s], out_w_ref[...]).astype(BF16)
        bias = bias_ref[s]
        dq, dk, dv = [], [], []
        for h in range(lw // HD):
            at = slice(h * HD, (h + 1) * HD)
            q = qkv_ref[s, :, h * HD : (h + 1) * HD]
            k = qkv_ref[s, :, lw + h * HD : lw + (h + 1) * HD]
            v = qkv_ref[s, :, 2 * lw + h * HD : 2 * lw + (h + 1) * HD]
            g = grad[:, at]
            o = att_ref[s, :, at]
            p = jnp.exp(nt(q, k) + bias - stat_ref[s, :, h : h + 1])
            dv.append(tn(p.astype(BF16), g).astype(BF16))
            inner = jnp.sum(g.astype(F32) * o.astype(F32), -1, keepdims=True)
            ds = (p * (nt(g, v) - inner)).astype(BF16)
            dq.append((nn(ds, k) * scale).astype(BF16))
            dk.append(tn(ds, q).astype(BF16))
        dqkv[s] = jnp.concatenate(dq + dk + dv, -1)
        return nt(dqkv[s], qkv_w_ref[...])

    h1 = Scatter(wires, place, h2_cs, h2_cr, h2_ys, h2_yr)
    own_c[...] = attend(mine).astype(BF16)
    pump.until(45.0)
    gm.over_core.wait_recv()
    h1.give_core(1, attend(third))
    pump.until(51.0)
    gm.forward()
    ff_sum.start_y()
    temp[...] = attend(second)
    pump.until(56.0)
    gm.passed.wait_recv()
    h1.give_core(0, attend(first))
    h1.give_y(temp[...], start=False)
    pump.until(60.0)

    fetch.wait()
    acc[...] = jnp.zeros_like(acc)

    def attention_grads(s, carry):
        acc[...] += jnp.concatenate([tn(low1[s], dqkv[s]), tn(mid_all[s], att_ref[s])], 1)
        return carry

    lax.fori_loop(0, held, attention_grads, 0)
    g_at[...] = acc[...].reshape(g_at.shape).astype(BF16)
    for i in range(pieces):
        pump.add(66.0 + 6.5 * i, reduce_steps(wires, place, g_at.at[i], r_at.at[i], h_at.at[i]), 1.3)
    columns = jnp.zeros((1, 3 * lw), F32)
    dec_sum = jnp.zeros((1, feats), F32)
    for s in range(held):
        columns += total(dqkv[s].astype(F32))
        dec_sum += total(g_ref[s].astype(F32))
    blank = jnp.zeros((1, width - 2 * lw - 2 * feats), F32)
    v_own[7:8] = jnp.concatenate(
        [columns[:, :lw], columns[:, 2 * lw :], dec_sum, mask_ref[0:1], blank], 1
    )
    pump.until(65.0)

    final = mid_ref[...] + ff_sum.own(own_b[...].astype(F32)) + down_b_ref[...]
    fin_all[place.m] = final.astype(BF16)
    gf = Gather(wires, place, fin_all)
    gf.start()
    pump.until(79.0)
    gf.forward()
    h1.start_y()
    gf.wait()
    t = lax.broadcasted_iota(jnp.int32, (n * chunk, rows), 1)
    sel = (t == col_ref[...]).astype(F32).astype(BF16)
    for s in range(held):
        projected = (nn(fin_all[s], dec_w_ref[...]) + dec_b_ref[...]).astype(BF16)
        send3[:, s] = nn(sel, projected).astype(BF16).reshape(n, chunk, feats)
    out_one = Spread(wires, place, send3, hop3)
    out_one.start()
    dec_grad = jnp.zeros((width, feats), F32)
    for s in range(held):
        dec_grad += tn(fin_all[s], g_ref[s])
    g_dec[...] = dec_grad.reshape(g_dec.shape).astype(BF16)
    pump.add(84.0, reduce_steps(wires, place, g_dec, r_dec, h_dec), 0.5)
    pump.until(92.0)

    g_h1 = h1.own(own_c[...].astype(F32))
    normed, inverse = norm_stats(x_ref[...].astype(F32))
    g_norm, gain_sum, bias_sum = norm_backward(g_h1, normed, inverse, gain1_ref[...])
    patch_ref[place.m] = (own_a[...] + g_norm).astype(BF16)
    gp = Gather(wires, place, patch_ref)
    gp.start()
    v_own[0:1] = gain_sum.reshape(1, width)
    v_own[1:2] = bias_sum.reshape(1, width)
    told = Tell(wires, place, v_own, v_all)
    told.start()
    out_one.wait()

    def regroup(k, carry):
        j = order_ref[k]
        send3[k // held, k % held] = hop3[j // held, j % held]
        return carry

    lax.fori_loop(0, n * held, regroup, 0)
    out_two = Spread(wires, place, send3, hop4)
    out_two.start()
    pump.until(96.0)
    told.wait()
    w_own[...] = lax.fori_loop(1, n, lambda i, v: v + v_all[i], v_all[0])
    shared = []
    for peer in (place.core_peer, place.y_peer, place.far_peer):
        shared.append(wires.start(w_own, w_all.at[place.m], peer))
    w_all[place.m] = w_own[...]
    pump.until(104.0)
    out_two.wait()
    for made in shared:
        made.wait()
    summed = w_all[0] + w_all[1] + w_all[2] + w_all[3]
    vec_ref[...] = jnp.concatenate([summed[:6], w_own[6:8]], 0)
    gp.forward()
    pump.until(1e9)
    gp.wait()
    for made in (gg, ff_sum, gm, h1, gf, gp):
        made.close()


def backward(n, pieces, order, x, low1, *rest):
    qkv, att = rest[0], rest[1]
    held, rows, lw = att.shape
    width = x.shape[1]
    feats = rest[6].shape[2]
    chunk = rest[-2].shape[0] // n
    each = width // (pieces * n)
    shape = jax.ShapeDtypeStruct
    low = lambda *dims: pltpu.VMEM(dims, BF16)
    full = lambda *dims: pltpu.VMEM(dims, F32)
    sems = 5 * n + 64 + 2 * (3 * pieces + 1) * (n.bit_length() - 1)
    part = (pieces, n, each, width)
    got = (pieces, n - 1, each, width)
    links = [low(2, rows, width), low(2, rows, width), low(rows, width), low(rows, width)]
    every = pl.BlockSpec(memory_space=pl.ANY)
    return pl.pallas_call(
        partial(backward_kernel, n),
        in_specs=[pl.BlockSpec(memory_space=pltpu.SMEM)] + vmem(1) + [every] + vmem(len(rest)),
        out_specs=vmem(7),
        out_shape=[
            shape((held, rows, width), BF16),
            shape(part, BF16),
            shape(part, BF16),
            shape(part, BF16),
            shape((n, width // n, feats), BF16),
            shape((n, held, chunk, feats), BF16),
            shape((8, width), F32),
        ],
        scratch_shapes=[low(held, rows, width)] * 3
        + [low(4, held, rows, feats)]
        + links
        + links
        + [full(rows, width), low(rows, width), low(rows, width)]
        + [full(width, width)]
        + [low(held, rows, width)]
        + [low(*qkv.shape)]
        + [low(*part)] * 3
        + [low(n, width // n, feats)]
        + [low(*got)] * 3
        + [low(n - 1, width // n, feats)]
        + [low(n, held, chunk, feats)] * 2
        + [full(8, width), full(n, 8, width), full(8, width), full(4, 8, width)]
        + [
            pltpu.SemaphoreType.DMA,
            pltpu.SemaphoreType.DMA((sems,)),
            pltpu.SemaphoreType.DMA((sems,)),
        ],
        name="backward",
        compiler_params=pltpu.CompilerParams(
            collective_id=1, has_side_effects=True, vmem_limit_bytes=62 << 20
        ),
    )(order, x, low1, *rest)


def shards(
    patches,
    norm1_gain,
    norm1_bias,
    qkv_weight,
    qv_bias,
    out_weight,
    out_bias,
    norm2_gain,
    norm2_bias,
    up_weight,
    up_bias,
    down_weight,
    down_bias,
    dec_weight,
    dec_bias,
    mask_token,
    lengths,
    blank,
    visible,
    plan,
    dec_cot,
):
    n = lax.axis_size("dp")
    d = lax.axis_index("dp")
    m = lax.axis_index("mp")
    held, seq, feats = dec_cot.shape
    vis = visible.shape[1]
    strips = plan.shape[0]
    width = patches.shape[1]
    lw = qkv_weight.shape[2]
    rows = -(-vis // 16) * 16
    real = -(-vis // n)
    chunk = -(-real // 8) * 8
    scale = HD ** (-0.5)

    strip_ids = jnp.arange(strips, dtype=jnp.int32)
    earlier = (plan[None, :] == plan[:, None]) & (strip_ids[None, :] < strip_ids[:, None])
    packed_at = plan * held + jnp.sum(earlier.astype(jnp.int32), 1)
    strip_at = jnp.sum(
        jnp.where(packed_at[None, :] == strip_ids[:, None], strip_ids[None, :], 0), 1
    )
    held_strips = lax.dynamic_slice_in_dim(strip_at, d * held, held)
    owned_pos = lax.dynamic_slice_in_dim(visible, d * held, held)
    owned_pos = jnp.pad(owned_pos, ((0, 0), (0, n * real - vis)), constant_values=-1)
    owned_pos = jnp.pad(
        owned_pos.reshape(held, n, real), ((0, 0), (0, 0), (0, chunk - real)), constant_values=-1
    )

    vis_rows = jnp.pad(visible, ((0, 0), (0, rows - vis)), constant_values=-1)
    spread_cot, mask_grad, key_bias = prepare(
        held_strips,
        lengths[held_strips],
        owned_pos.reshape(held, n * chunk, 1),
        dec_cot,
        vis_rows.reshape(strips, 1, rows),
        blank.reshape(strips, 1, seq),
        n,
        chunk,
    )
    spot = np.arange(n * chunk)
    spot = np.where(spot % chunk < real, spot // chunk * real + spot % chunk, -1)
    x_all = jnp.pad(patches.reshape(held, vis, width), ((0, 0), (0, rows - vis), (0, 0)))
    row = lambda v: v.reshape(1, -1)
    flat_qkv = qkv_weight.reshape(width, 3 * lw)
    qkv_shift = jnp.concatenate([qv_bias[0], jnp.zeros((lw,), F32), qv_bias[1]])
    qkv_scale = np.where(np.arange(3 * lw) < lw, scale, 1.0).astype(np.float32)
    low_one, qkv, attended, stat, mid, low_two, g_rows, dec_all, x_own = forward(
        n,
        strip_at,
        x_all,
        row(norm1_gain),
        row(norm1_bias),
        flat_qkv,
        row(qkv_shift),
        row(jnp.asarray(qkv_scale)),
        out_weight,
        row(out_bias),
        row(norm2_gain),
        row(norm2_bias),
        key_bias,
        spread_cot,
        row(jnp.asarray(spot, jnp.int32)),
        dec_weight,
    )
    pieces = 2 if width // n % 32 == 0 else 1
    patch_all, up_grad, down_grad, at_grad, dec_grad, arrived, vectors = backward(
        n,
        pieces,
        packed_at,
        x_own,
        low_one,
        qkv,
        attended,
        stat,
        key_bias,
        mid,
        low_two,
        g_rows,
        dec_all,
        up_weight,
        row(up_bias),
        down_weight,
        row(down_bias),
        dec_weight,
        row(dec_bias),
        out_weight,
        flat_qkv,
        row(norm1_gain),
        row(norm2_gain),
        jnp.asarray(spot, jnp.int32).reshape(n * chunk, 1),
        mask_grad,
    )
    decoded = put_rows(owned_pos.reshape(held, 1, n * chunk), arrived, mask_token, seq)
    patches_grad = patch_all[:, :vis].reshape(held * vis, width).astype(F32)
    at_grad = at_grad.reshape(width, width)
    qkv_grad = at_grad[:, : 3 * lw].astype(F32).reshape(width, 3, lw)
    out_grad = at_grad[:, 3 * lw :].astype(F32).T
    mixed = vectors[7]
    return (
        decoded,
        patches_grad,
        vectors[0],
        vectors[1],
        qkv_grad,
        mixed[: 2 * lw].reshape(2, lw),
        out_grad,
        vectors[4],
        vectors[2],
        vectors[3],
        up_grad.reshape(width, width).astype(F32),
        vectors[6],
        down_grad.reshape(width, width).astype(F32),
        vectors[5],
        dec_grad.reshape(width, feats).astype(F32),
        mixed[2 * lw : 2 * lw + feats],
        mixed[2 * lw + feats : 2 * lw + 2 * feats],
    )


def solution(mesh):
    return jax.shard_map(
        shards,
        mesh=mesh,
        in_specs=(
            P("dp", None),
            P(),
            P(),
            P(None, None, "mp"),
            P(None, "mp"),
            P("mp", None),
            P(),
            P(),
            P(),
            P(None, "mp"),
            P("mp"),
            P("mp", None),
            P(),
            P(None, "mp"),
            P("mp"),
            P("mp"),
            P(),
            P(),
            P(),
            P(),
            P("dp", None, "mp"),
        ),
        out_specs=(
            P("dp", None, "mp"),
            P("dp", None),
            P(),
            P(),
            P(None, None, "mp"),
            P(None, "mp"),
            P("mp", None),
            P(),
            P(),
            P(),
            P(None, "mp"),
            P("mp"),
            P("mp", None),
            P(),
            P(None, "mp"),
            P("mp"),
            P("mp"),
        ),
        check_vma=False,
    )
```

```python
from functools import partial

import jax
import jax.numpy as jnp
import numpy as np
from jax import lax
from jax.experimental import pallas as pl
from jax.experimental.pallas import tpu as pltpu
from jax.sharding import PartitionSpec as P

HD = 64
EPSILON = 1e-06
NEGATIVE = -1e30
F32 = jnp.float32
BF16 = jnp.bfloat16


def nn(a, b):
    return lax.dot_general(a, b, (((1,), (0,)), ((), ())), preferred_element_type=F32)


def tn(a, b):
    return lax.dot_general(a, b, (((0,), (0,)), ((), ())), preferred_element_type=F32)


def nt(a, b):
    return lax.dot_general(a, b, (((1,), (1,)), ((), ())), preferred_element_type=F32)


def norm_stats(inputs):
    centered = inputs - jnp.mean(inputs, -1, keepdims=True)
    inverse = lax.rsqrt(jnp.mean(centered * centered, -1, keepdims=True) + EPSILON)
    return centered * inverse, inverse


def norm_backward(incoming, normed, inverse, gain_vec):
    weighted = incoming * gain_vec
    inner = (
        weighted
        - jnp.mean(weighted, -1, keepdims=True)
        - normed * jnp.mean(weighted * normed, -1, keepdims=True)
    )
    return inner * inverse, jnp.sum(incoming * normed, 0), jnp.sum(incoming, 0)


def prepare_kernel(count, held_ref, len_ref, *refs):
    pos_ref, cot_ref, vis_ref, blank_ref, patches_ref, out_ref, mask_ref, bias_ref, x_ref = refs

    @pl.when(pl.program_id(0) == 0)
    def _():
        mask_ref[...] = jnp.zeros_like(mask_ref)

    seq = cot_ref.shape[1]
    n, _, chunk, feats = out_ref.shape
    rows = bias_ref.shape[2]
    spot = lax.broadcasted_iota(jnp.int32, (n * chunk, seq), 1)
    chosen = (pos_ref[0] == spot).astype(F32)
    picked = nn(chosen.astype(BF16), cot_ref[0])
    out_ref[...] = picked.astype(BF16).reshape(n, 1, chunk, feats)
    hidden = 1.0 - jnp.sum(chosen, 0, keepdims=True)
    hidden = jnp.broadcast_to(hidden, (8, seq)).astype(BF16)
    mask_ref[...] += nn(hidden, cot_ref[0])
    place = lax.broadcasted_iota(jnp.int32, (1, seq), 1)
    usable = (blank_ref[0] == 0) & (place < len_ref[pl.program_id(0)])
    usable = jnp.broadcast_to(usable.astype(F32), (8, seq)).astype(BF16)
    at = lax.broadcasted_iota(jnp.int32, (seq, rows), 0)
    allowed = nn(usable, (vis_ref[0] == at).astype(F32).astype(BF16))
    bias_ref[0] = jnp.where(allowed[:1] > 0.5, 0.0, NEGATIVE)
    for s in range(patches_ref.shape[0] // count):

        @pl.when(pl.program_id(0) == s)
        def _():
            first, last = s * count, (s + 1) * count
            start = first // 16 * 16
            block = patches_ref[start:last].astype(F32)[first - start :]
            filler = jnp.zeros((rows - count, block.shape[1]), F32)
            x_ref[0] = jnp.concatenate([block, filler]).astype(BF16)


def prepare(held_strips, lengths, pos_col, cot, vis, blank, patches, n, chunk):
    held, seq, feats = cot.shape
    rows = vis.shape[2]
    width = patches.shape[1]
    return pl.pallas_call(
        partial(prepare_kernel, patches.shape[0] // held),
        grid_spec=pltpu.PrefetchScalarGridSpec(
            num_scalar_prefetch=2,
            grid=(held,),
            in_specs=[
                pl.BlockSpec((1, n * chunk, 1), lambda s, h, l: (s, 0, 0)),
                pl.BlockSpec((1, seq, feats), lambda s, h, l: (s, 0, 0)),
                pl.BlockSpec((1, 1, rows), lambda s, h, l: (h[s], 0, 0)),
                pl.BlockSpec((1, 1, seq), lambda s, h, l: (h[s], 0, 0)),
                pl.BlockSpec(patches.shape, lambda s, h, l: (0, 0)),
            ],
            out_specs=[
                pl.BlockSpec((n, 1, chunk, feats), lambda s, h, l: (0, s, 0, 0)),
                pl.BlockSpec((8, feats), lambda s, h, l: (0, 0)),
                pl.BlockSpec((1, 1, rows), lambda s, h, l: (s, 0, 0)),
                pl.BlockSpec((1, rows, width), lambda s, h, l: (s, 0, 0)),
            ],
        ),
        out_shape=[
            jax.ShapeDtypeStruct((n, held, chunk, feats), BF16),
            jax.ShapeDtypeStruct((8, feats), F32),
            jax.ShapeDtypeStruct((held, 1, rows), F32),
            jax.ShapeDtypeStruct((held, rows, width), BF16),
        ],
        name="prepare",
        compiler_params=pltpu.CompilerParams(vmem_limit_bytes=24 << 20),
    )(held_strips, lengths, pos_col, cot, vis, blank, patches)


def finish_kernel(vis, pos_ref, rows_ref, token_ref, patch_ref, up_ref, down_ref, *outs):
    out_ref, patches_ref, up_out, down_out = outs
    n, _, chunk, feats = rows_ref.shape
    seq = out_ref.shape[1]
    spot = lax.broadcasted_iota(jnp.int32, (seq, n * chunk), 0)
    chosen = (pos_ref[0] == spot).astype(F32)
    rows = nn(chosen.astype(BF16), rows_ref[...].reshape(n * chunk, feats))
    hidden = 1.0 - jnp.sum(chosen, 1, keepdims=True)
    token = token_ref[...].reshape(1, feats).astype(BF16).astype(F32)
    out_ref[0] = (rows + hidden * token).astype(BF16)
    up_out[...] = up_ref[...].astype(F32)
    down_out[...] = down_ref[...].astype(F32)
    for s in range(patches_ref.shape[0] // vis):

        @pl.when(pl.program_id(0) == s)
        def _():
            patches_ref[s * vis : (s + 1) * vis] = patch_ref[0, :vis].astype(F32)


def finish(pos_row, rows, token, patch_all, up_grad, down_grad, seq, vis):
    n, held, chunk, feats = rows.shape
    _, each, width = patch_all.shape
    tall = width // held
    whole = pl.BlockSpec((held * vis, width), lambda s: (0, 0))
    tile = pl.BlockSpec((tall, width), lambda s: (s, 0))
    shape = jax.ShapeDtypeStruct
    return pl.pallas_call(
        partial(finish_kernel, vis),
        grid=(held,),
        in_specs=[
            pl.BlockSpec((1, 1, n * chunk), lambda s: (s, 0, 0)),
            pl.BlockSpec((n, 1, chunk, feats), lambda s: (0, s, 0, 0)),
            pl.BlockSpec(memory_space=pltpu.VMEM),
            pl.BlockSpec((1, each, width), lambda s: (s, 0, 0)),
            tile,
            tile,
        ],
        out_specs=[pl.BlockSpec((1, seq, feats), lambda s: (s, 0, 0)), whole, tile, tile],
        out_shape=[
            shape((held, seq, feats), BF16),
            shape((held * vis, width), F32),
            shape((width, width), F32),
            shape((width, width), F32),
        ],
        name="finish",
        compiler_params=pltpu.CompilerParams(vmem_limit_bytes=32 << 20),
    )(pos_row, rows, token, patch_all, up_grad, down_grad)


MESH = pl.DeviceIdType.MESH


class Wires:
    def __init__(self, send, recv):
        self.send, self.recv, self.used = send, recv, 0

    def take(self, count=1):
        first = self.used
        self.used += count
        return first

    def copy(self, src, dst, target, index=None):
        index = self.take() if index is None else index
        return pltpu.make_async_remote_copy(
            src_ref=src,
            dst_ref=dst,
            send_sem=self.send.at[index],
            recv_sem=self.recv.at[index],
            device_id=target,
            device_id_type=MESH,
        )


class Place:
    def __init__(self, n):
        self.n = n
        self.d = lax.axis_index("dp")
        self.m = lax.axis_index("mp")
        self.core, self.y = self.m % 2, self.m // 2
        self.core_peer = (self.d, self.m + 1 - 2 * self.core)
        self.y_peer = (self.d, (self.m + 2) % 4)
        self.far_peer = (self.d, 3 - self.m)
        self.y_strip = (self.m + 2) % 4

    def strip(self, i):
        y = self.y + (1 - 2 * self.y) * (1 - i // 2)
        core = self.core + (1 - 2 * self.core) * (1 - i % 2)
        return 2 * y + core

    def dp_peer(self, k):
        return ((self.d + k) % self.n, self.m)


def meet_all(place):
    barrier = pltpu.get_barrier_semaphore()
    for peer in (place.core_peer, place.y_peer, place.far_peer):
        pl.semaphore_signal(barrier, inc=1, device_id=peer, device_id_type=MESH)

    def greet(k, carry):
        pl.semaphore_signal(barrier, inc=1, device_id=place.dp_peer(k), device_id_type=MESH)
        return carry

    lax.fori_loop(1, place.n, greet, 0)
    pl.semaphore_wait(barrier, place.n + 2)


class Spread:
    def __init__(self, wires, place, src, dst, blocks=True, local=True, tall=None):
        self.wires, self.place, self.src, self.blocks, self.local = wires, place, src, blocks, local
        d = place.d
        self.slot = dst.at[d] if tall is None else dst.at[pl.ds(pl.multiple_of(d * tall, tall), tall)]
        self.base = wires.take(place.n)

    def made(self, k):
        peer = self.place.dp_peer(k)
        src = self.src.at[peer[0]] if self.blocks else self.src
        return self.wires.copy(src, self.slot, peer, self.base + k)

    def start(self):
        def one(k, carry):
            self.made(k).start()
            return carry

        lax.fori_loop(1, self.place.n, one, 0)
        if self.local:
            self.slot[...] = self.src[self.place.d] if self.blocks else self.src[...]

    def wait(self):
        def one(k, carry):
            self.made(k).wait()
            return carry

        lax.fori_loop(1, self.place.n, one, 0)


class Scatter:
    def __init__(self, wires, place, core_send, core_recv, y_send, y_recv):
        self.core_send, self.core_recv, self.y_send, self.y_recv = core_send, core_recv, y_send, y_recv
        self.core = [
            wires.copy(core_send.at[i], core_recv.at[i], place.core_peer) for i in range(2)
        ]
        self.away = wires.copy(y_send, y_recv, place.y_peer)

    def give_core(self, i, value):
        self.core_send[i] = value.astype(BF16)
        self.core[i].start()

    def give_y(self, value):
        self.core[0].wait_recv()
        self.y_send[...] = (value + self.core_recv[0].astype(F32)).astype(BF16)

    def own(self, value, arrived=False):
        self.core[1].wait_recv()
        if not arrived:
            self.away.wait_recv()
        return value + self.core_recv[1].astype(F32) + self.y_recv[...].astype(F32)

    def close(self):
        for made in (*self.core, self.away):
            made.wait_send()


class Gather:
    def __init__(self, wires, place, full, src=None):
        spot, passing = full.at[place.m], full.at[place.y_strip]
        src = spot if src is None else src
        self.over_y = wires.copy(src, spot, place.y_peer)
        self.over_core = wires.copy(src, spot, place.core_peer)
        self.passed = wires.copy(passing, passing, place.core_peer)

    def start(self):
        self.over_y.start()
        self.over_core.start()

    def forward(self):
        self.over_y.wait_recv()
        self.passed.start()

    def wait(self):
        self.over_core.wait_recv()
        self.passed.wait_recv()

    def close(self):
        for made in (self.over_y, self.over_core, self.passed):
            made.wait_send()


class Reduce:
    def __init__(self, wires, place, g, recv, h, bits):
        self.g, self.recv, self.h = g, recv, h
        n = place.n
        base, size = 0, n
        self.halves, self.doubles, path = [], [], []
        for k in bits:
            half = size // 2
            bit = (place.d // (1 << k)) % 2
            peer = (place.d + (1 - 2 * bit) * (1 << k), place.m)
            keep, away, landing = base + bit * half, base + (1 - bit) * half, n - size
            made = wires.copy(g.at[pl.ds(away, half)], recv.at[pl.ds(landing, half)], peer)
            self.halves.append((made, keep, landing, half))
            path.append((base, peer))
            base, size = keep, half
        self.mine = base
        for start, peer in reversed(path):
            held = h.at[pl.ds(base, size)]
            self.doubles.append(wires.copy(held, held, peer))
            base, size = start, size * 2

    def steps(self):
        g, recv, h = self.g, self.recv, self.h
        for made, keep, landing, half in self.halves:
            made.start()
            yield
            made.wait_recv()

            def add(i, carry):
                total = g[keep + i].astype(F32) + recv[landing + i].astype(F32)
                g[keep + i] = total.astype(BF16)
                return carry

            lax.fori_loop(0, half, add, 0)
        h[self.mine] = g[self.mine]
        for made in self.doubles:
            made.start()
            yield
            made.wait_recv()
        for made in [half[0] for half in self.halves] + self.doubles:
            made.wait_send()


class Group:
    def __init__(self, sums):
        self.todo = [one.steps() for one in sums]

    def go(self):
        self.todo = [steps for steps in self.todo if next(steps, self) is not self]
        return bool(self.todo)


def layer_kernel(
    n,
    order_in,
    order_out,
    x_ref,
    gain1_ref,
    shift1_ref,
    qkv_w_ref,
    qv_b_ref,
    out_w_ref,
    out_b_ref,
    gain2_ref,
    shift2_ref,
    up_w_ref,
    up_b_ref,
    down_w_ref,
    down_b_ref,
    dec_w_ref,
    dec_b_ref,
    bias_ref,
    cot_ref,
    spot_row,
    spot_col,
    mask_ref,
    patch_hbm,
    h_up,
    h_down,
    h_at,
    h_dec,
    hop4,
    vec_ref,
    qkv,
    att,
    stat,
    mid,
    low2,
    act,
    slope,
    g3_low,
    mid_all,
    g_full,
    decs,
    a_cs,
    a_cr,
    a_ys,
    a_yr,
    b_cs,
    b_cr,
    b_ys,
    b_yr,
    own_a,
    own_b,
    own_c,
    acc,
    g_up,
    g_down,
    g_at,
    g_dec,
    r_up,
    r_down,
    r_at,
    r_dec,
    hop1,
    send2,
    hop2,
    v_own,
    w_own,
    w_all,
    copy_sem,
    send_sem,
    recv_sem,
):
    place = Place(n)
    wires = Wires(send_sem, recv_sem)
    held, rows, width = x_ref.shape
    lw = att.shape[2]
    chunk, feats = hop4.shape[2:]
    scale = HD ** (-0.5)
    row = lambda ref: ref[...].reshape(1, -1)
    total = lambda v: jnp.sum(v, 0, keepdims=True)
    m = place.m
    temp = acc.at[pl.ds(0, rows)]
    fin_all, patch_all, send3, hop3 = g3_low, act, send2, hop1

    decs_in = Gather(wires, place, decs, dec_w_ref)
    cot_one = Spread(wires, place, cot_ref, hop1)
    cot_two = Spread(wires, place, send2, hop2)
    att_sum = Scatter(wires, place, a_cs, a_cr, a_ys, a_yr)
    low2_in = Gather(wires, place, low2)
    g_in = Gather(wires, place, g_full)
    ff_sum = Scatter(wires, place, b_cs, b_cr, b_ys, b_yr)
    h2_sum = Scatter(wires, place, a_cs, a_cr, a_ys, a_yr)
    mid_in = Gather(wires, place, mid_all)
    fin_in = Gather(wires, place, fin_all)
    h1_sum = Scatter(wires, place, a_cs, a_cr, a_ys, a_yr)
    patch_in = Gather(wires, place, patch_all)
    out_one = Spread(wires, place, send3, hop3)
    out_two = Spread(wires, place, send3, hop4)
    told = Spread(wires, place, v_own, acc, blocks=False, tall=v_own.shape[0])
    shared = [
        wires.copy(w_own, w_all.at[m], peer)
        for peer in (place.core_peer, place.y_peer, place.far_peer)
    ]
    bits = list(range(n.bit_length() - 1))
    turned = [bits[1], bits[0], *bits[2:]]
    pieces = g_up.shape[0]
    ways = [bits, turned] if pieces > 1 else [bits]


    def group(g, recv, h):
        return Group(
            [Reduce(wires, place, g.at[i], recv.at[i], h.at[i], ways[i]) for i in range(pieces)]
        )

    up, down, at = group(g_up, r_up, h_up), group(g_down, r_down, h_down), group(g_at, r_at, h_at)
    dec = Group([Reduce(wires, place, g_dec, r_dec, h_dec, bits)])

    meet_all(place)
    decs_in.start()
    decs[m] = dec_w_ref[...]
    cot_one.start()

    def regroup(order_ref, src, dst):
        def one(k, carry):
            j = order_ref[k]
            dst[k // held, k % held] = src[j // held, j % held]
            return carry

        lax.fori_loop(0, n * held, one, 0)

    qkv_shift = jnp.concatenate([qv_b_ref[0:1], jnp.zeros((1, lw), F32), qv_b_ref[1:2]], 1)
    lane = lax.broadcasted_iota(jnp.int32, (1, 3 * lw), 1)
    qkv_scale = jnp.where(lane < lw, scale, 1.0)

    def low_one(s):
        normed, _ = norm_stats(x_ref[s].astype(F32))
        return (normed * row(gain1_ref) + row(shift1_ref)).astype(BF16)

    def attention(i, carry):
        s = place.strip(i)
        proj = (nn(low_one(s), qkv_w_ref[...]) + qkv_shift) * qkv_scale
        qkv[s] = proj.astype(BF16)
        bias = bias_ref[s]
        outs = []
        spot = lax.broadcasted_iota(jnp.int32, (rows, 128), 1)
        stats = jnp.zeros((rows, 128), F32)
        for h in range(lw // HD):
            q = qkv[s, :, h * HD : (h + 1) * HD]
            k = qkv[s, :, lw + h * HD : lw + (h + 1) * HD]
            v = qkv[s, :, 2 * lw + h * HD : 2 * lw + (h + 1) * HD]
            scores = nt(q, k) + bias
            top = jnp.max(scores, -1, keepdims=True)
            e = jnp.exp(scores - top)
            norm = jnp.sum(e, -1, keepdims=True)
            outs.append((nn(e.astype(BF16), v) / norm).astype(BF16))
            stats = jnp.where(spot == h, top + jnp.log(norm), stats)
        att[s] = jnp.concatenate(outs, -1)
        stat[s] = stats
        temp[...] = nn(att[s], out_w_ref[...])

        @pl.when(i == 0)
        def _():
            att_sum.give_core(0, temp[...])

        @pl.when(i == 1)
        def _():
            att_sum.give_y(temp[...])
            decs_in.forward()
            att_sum.away.start()

        @pl.when(i == 2)
        def _():
            att_sum.give_core(1, temp[...])
            cot_one.wait()
            regroup(order_in, hop1, send2)
            cot_two.start()

        return carry

    lax.fori_loop(0, held, attention, 0)
    mid[...] = x_ref[m].astype(F32) + row(out_b_ref) + att_sum.own(temp[...])
    normed, _ = norm_stats(mid[...])
    low2[m] = (normed * row(gain2_ref) + row(shift2_ref)).astype(BF16)
    low2_in.start()
    att_sum.close()
    cot_two.wait()
    t = lax.broadcasted_iota(jnp.int32, (rows, n * chunk), 0)
    sel = (t == spot_row[...]).astype(F32).astype(BF16)
    for s in range(held):
        g_full[m, s] = nn(sel, hop2[:, s].reshape(n * chunk, feats)).astype(BF16)
    decs_in.wait()
    v_own[...] = jnp.zeros_like(v_own)
    low2_in.forward()
    g_in.start()
    low2_in.wait()

    tall = 16

    def feed_forward(i, carry):
        s = place.strip(i)
        temp[...] = nn(low2[s], up_w_ref[...]) + row(up_b_ref)

        def some(r, inner):
            at = pl.ds(pl.multiple_of(r * tall, tall), tall)
            pre = temp[at]
            half = 0.5 * (1.0 + lax.erf(pre * np.float32(0.5**0.5)))
            bell = jnp.exp(-0.5 * pre * pre) * np.float32((2 * np.pi) ** -0.5)
            act[s, at] = (pre * half).astype(BF16)
            slope[s, at] = (half + pre * bell).astype(BF16)
            return inner

        lax.fori_loop(0, rows // tall, some, 0)
        temp[...] = nn(act[s], down_w_ref[...])

        @pl.when(i == 0)
        def _():
            ff_sum.give_core(0, temp[...])

        @pl.when(i == 1)
        def _():
            ff_sum.give_y(temp[...])
            g_in.forward()
            ff_sum.away.start()

        @pl.when(i == 2)
        def _():
            ff_sum.give_core(1, temp[...])

        @pl.when(i == 3)
        def _():
            own_b[...] = temp[...].astype(BF16)

        return carry

    lax.fori_loop(0, held, feed_forward, 0)
    g_in.wait()

    def g_three(s):
        weight = jnp.concatenate([decs[i] for i in range(4)], 1)
        return nt(jnp.concatenate([g_full[i, s] for i in range(4)], 1), weight)

    def g_low(s, carry):
        g3_low[s] = g_three(s).astype(BF16)
        return carry

    lax.fori_loop(0, held, g_low, 0)

    def weight_grad(left, right, out):
        acc[...] = jnp.zeros_like(acc)

        def add(s, carry):
            acc[...] += tn(left[s], right[s])
            return carry

        lax.fori_loop(0, held, add, 0)
        out[...] = acc[...].reshape(out.shape).astype(BF16)

    weight_grad(act, g3_low, g_down)
    down.go()

    def backward_ff(i, carry):
        s = place.strip(i)
        g_pre = nt(g3_low[s], down_w_ref[...]) * slope[s].astype(F32)
        slope[s] = g_pre.astype(BF16)
        v_own[6:7] += total(g_pre)
        temp[...] = nt(slope[s], up_w_ref[...])

        @pl.when(i == 0)
        def _():
            h2_sum.give_core(0, temp[...])

        @pl.when(i == 1)
        def _():
            h2_sum.give_y(temp[...])
            ff_sum.away.wait_recv()
            h2_sum.away.start()
            down.go()

        @pl.when(i == 2)
        def _():
            h2_sum.give_core(1, temp[...])

        @pl.when(i == 3)
        def _():
            own_a[...] = temp[...]
            down.go()

        return carry

    lax.fori_loop(0, held, backward_ff, 0)
    weight_grad(low2, slope, g_up)
    up.go()
    final = mid[...] + ff_sum.own(own_b[...].astype(F32), arrived=True) + row(down_b_ref)
    fin_all[m] = final.astype(BF16)
    g_own = g_three(m)
    v_own[5:6] = total(g_own)

    g_h2 = h2_sum.own(own_a[...])
    normed, inverse = norm_stats(mid[...])
    g_norm, gain_sum, bias_sum = norm_backward(g_h2, normed, inverse, row(gain2_ref))
    g_mid = g_own + g_norm
    own_a[...] = g_mid
    mid_all[m] = g_mid.astype(BF16)
    mid_in.start()
    h2_sum.close()
    v_own[2:3] = gain_sum.reshape(1, width)
    v_own[3:4] = bias_sum.reshape(1, width)
    v_own[4:5] = total(g_mid)
    down.go()

    def dqkv(s):
        return slope[s, :, : 3 * lw]

    def attention_back(i, carry):
        s = place.strip(3 - i)

        @pl.when(i == 1)
        def _():
            mid_in.over_core.wait_recv()

        @pl.when(i == 2)
        def _():
            mid_in.forward()
            fin_in.start()

        @pl.when(i == 3)
        def _():
            mid_in.passed.wait_recv()

        grad = nt(mid_all[s], out_w_ref[...]).astype(BF16)
        bias = bias_ref[s]
        dq, dk, dv = [], [], []
        for h in range(lw // HD):
            q = qkv[s, :, h * HD : (h + 1) * HD]
            k = qkv[s, :, lw + h * HD : lw + (h + 1) * HD]
            v = qkv[s, :, 2 * lw + h * HD : 2 * lw + (h + 1) * HD]
            g = grad[:, h * HD : (h + 1) * HD]
            o = att[s, :, h * HD : (h + 1) * HD]
            p = jnp.exp(nt(q, k) + bias - stat[s, :, h : h + 1])
            dv.append(tn(p.astype(BF16), g).astype(BF16))
            inner = jnp.sum(g.astype(F32) * o.astype(F32), -1, keepdims=True)
            ds = (p * (nt(g, v) - inner)).astype(BF16)
            dq.append((nn(ds, k) * scale).astype(BF16))
            dk.append(tn(ds, q).astype(BF16))
        slope[s, :, : 3 * lw] = jnp.concatenate(dq + dk + dv, -1)
        temp[...] = nt(dqkv(s), qkv_w_ref[...])

        @pl.when(i == 0)
        def _():
            own_c[...] = temp[...].astype(BF16)
            up.go()

        @pl.when(i == 1)
        def _():
            h1_sum.give_core(1, temp[...])
            down.go()
            up.go()
            down.go()

        @pl.when(i == 2)
        def _():
            a_ys[...] = temp[...].astype(BF16)
            up.go()

        @pl.when(i == 3)
        def _():
            h1_sum.give_core(0, temp[...])
            h1_sum.give_y(a_ys[...].astype(F32))
            down.go()

        return carry

    lax.fori_loop(0, held, attention_back, 0)

    acc[...] = jnp.zeros_like(acc)

    def attention_grads(s, carry):
        acc[:lw] += tn(att[s], mid_all[s])
        acc[lw:] += tn(dqkv(s), low_one(s))
        return carry

    lax.fori_loop(0, held, attention_grads, 0)
    g_at[...] = acc[...].reshape(g_at.shape).astype(BF16)
    at.go()
    up.go()
    columns = jnp.zeros((1, 3 * lw), F32)
    dec_rows = jnp.zeros((1, feats), F32)
    for s in range(held):
        columns += total(dqkv(s).astype(F32))
        dec_rows += total(g_full[m, s].astype(F32))
    blank = jnp.zeros((1, width - 2 * lw - 2 * feats), F32)
    v_own[7:8] = jnp.concatenate(
        [columns[:, :lw], columns[:, 2 * lw :], dec_rows, mask_ref[0:1], blank], 1
    )

    fin_in.forward()
    h1_sum.away.start()
    fin_in.wait()
    t = lax.broadcasted_iota(jnp.int32, (n * chunk, rows), 1)
    sel = (t == spot_col[...]).astype(F32).astype(BF16)
    for s in range(held):
        projected = (nn(fin_all[s], dec_w_ref[...]) + row(dec_b_ref)).astype(BF16)
        send3[:, s] = nn(sel, projected).astype(BF16).reshape(n, chunk, feats)
    out_one.start()
    dec_grad = jnp.zeros((width, feats), F32)
    for s in range(held):
        dec_grad += tn(fin_all[s], g_full[m, s])
    g_dec[...] = dec_grad.reshape(g_dec.shape).astype(BF16)
    up.go()
    dec.go()
    at.go()
    up.go()

    g_h1 = h1_sum.own(own_c[...].astype(F32))
    normed, inverse = norm_stats(x_ref[m].astype(F32))
    g_norm, gain_sum, bias_sum = norm_backward(g_h1, normed, inverse, row(gain1_ref))
    patch_all[m] = (own_a[...] + g_norm).astype(BF16)
    patch_in.start()
    v_own[0:1] = gain_sum.reshape(1, width)
    v_own[1:2] = bias_sum.reshape(1, width)
    at.go()
    dec.go()
    out_one.wait()
    told.start()
    regroup(order_out, hop3, send3)
    out_two.start()
    at.go()
    dec.go()
    told.wait()
    w_own[...] = lax.fori_loop(
        1, n, lambda i, v: v + acc[pl.ds(pl.multiple_of(8 * i, 8), 8)], acc[0:8]
    )
    for made in shared:
        made.start()
    w_all[m] = w_own[...]
    at.go()
    dec.go()
    out_two.wait()
    for made in shared:
        made.wait()
    summed = w_all[0] + w_all[1] + w_all[2] + w_all[3]
    vec_ref[...] = jnp.concatenate([summed[:6], w_own[6:8]], 0)
    patch_in.forward()
    while any([group.go() for group in (down, up, at, dec)]):
        pass
    patch_in.wait()
    store = pltpu.make_async_copy(patch_all, patch_hbm, copy_sem)
    store.start()
    for made in (decs_in, low2_in, g_in, ff_sum, mid_in, fin_in, h1_sum, patch_in):
        made.close()
    store.wait()


def vmem(count):
    return [pl.BlockSpec(memory_space=pltpu.VMEM)] * count


def layer(n, pieces, order_in, order_out, x, *rest):
    held, rows, width = x.shape
    lw = rest[4].shape[0]
    _, _, chunk, feats = rest[-4].shape
    each = width // (pieces * n)
    shape = jax.ShapeDtypeStruct
    low = lambda *dims: pltpu.VMEM(dims, BF16)
    full = lambda *dims: pltpu.VMEM(dims, F32)
    bits = n.bit_length() - 1
    sems = 5 * n + 64 + 2 * (3 * pieces + 1) * bits
    part = (pieces, n, each, width)
    got = (pieces, n - 1, each, width)
    strips = low(held, rows, width)
    links = [low(2, rows, width), low(2, rows, width), low(rows, width), low(rows, width)]
    hop = low(n, held, chunk, feats)
    smem = pl.BlockSpec(memory_space=pltpu.SMEM)
    return pl.pallas_call(
        partial(layer_kernel, n),
        in_specs=[smem, smem] + vmem(1 + len(rest)),
        out_specs=[pl.BlockSpec(memory_space=pl.ANY)] + vmem(6),
        out_shape=[
            shape((held, rows, width), BF16),
            shape(part, BF16),
            shape(part, BF16),
            shape(part, BF16),
            shape((n, width // n, feats), BF16),
            shape((n, held, chunk, feats), BF16),
            shape((8, width), F32),
        ],
        scratch_shapes=[
            low(held, rows, 3 * lw),
            low(held, rows, lw),
            full(held, rows, 128),
            full(rows, width),
            strips,
            strips,
            strips,
            strips,
            strips,
            low(4, held, rows, feats),
            low(4, width, feats),
            *links,
            *links,
            full(rows, width),
            low(rows, width),
            low(rows, width),
            full(width, width),
            low(*part),
            low(*part),
            low(*part),
            low(n, width // n, feats),
            low(*got),
            low(*got),
            low(*got),
            low(n - 1, width // n, feats),
            hop,
            hop,
            hop,
            full(8, width),
            full(8, width),
            full(4, 8, width),
            pltpu.SemaphoreType.DMA,
            pltpu.SemaphoreType.DMA((sems,)),
            pltpu.SemaphoreType.DMA((sems,)),
        ],
        name="layer",
        compiler_params=pltpu.CompilerParams(
            collective_id=0, has_side_effects=True, vmem_limit_bytes=62 << 20
        ),
    )(order_in, order_out, x, *rest)


def shards(
    patches,
    norm1_gain,
    norm1_bias,
    qkv_weight,
    qv_bias,
    out_weight,
    out_bias,
    norm2_gain,
    norm2_bias,
    up_weight,
    up_bias,
    down_weight,
    down_bias,
    dec_weight,
    dec_bias,
    mask_token,
    lengths,
    blank,
    visible,
    plan,
    dec_cot,
):
    n = lax.axis_size("dp")
    d = lax.axis_index("dp")
    held, seq, feats = dec_cot.shape
    vis = visible.shape[1]
    strips = plan.shape[0]
    width = patches.shape[1]
    lw = qkv_weight.shape[2]
    rows = -(-vis // 16) * 16
    real = -(-vis // n)
    chunk = -(-real // 8) * 8

    strip_ids = jnp.arange(strips, dtype=jnp.int32)
    earlier = (plan[None, :] == plan[:, None]) & (strip_ids[None, :] < strip_ids[:, None])
    packed_at = plan * held + jnp.sum(earlier.astype(jnp.int32), 1)
    strip_at = jnp.sum(
        jnp.where(packed_at[None, :] == strip_ids[:, None], strip_ids[None, :], 0), 1
    )
    held_strips = lax.dynamic_slice_in_dim(strip_at, d * held, held)
    owned_pos = lax.dynamic_slice_in_dim(visible, d * held, held)
    owned_pos = jnp.pad(owned_pos, ((0, 0), (0, n * real - vis)), constant_values=-1)
    owned_pos = jnp.pad(
        owned_pos.reshape(held, n, real), ((0, 0), (0, 0), (0, chunk - real)), constant_values=-1
    )

    vis_rows = jnp.pad(visible, ((0, 0), (0, rows - vis)), constant_values=-1)
    spread_cot, mask_grad, key_bias, x_all = prepare(
        held_strips,
        lengths[held_strips],
        owned_pos.reshape(held, n * chunk, 1),
        dec_cot,
        vis_rows.reshape(strips, 1, rows),
        blank.reshape(strips, 1, seq),
        patches,
        n,
        chunk,
    )
    spot = np.arange(n * chunk)
    spot = np.where(spot % chunk < real, spot // chunk * real + spot % chunk, -1)
    pieces = 2 if width // n % 32 == 0 else 1
    patch_all, up_grad, down_grad, at_grad, dec_grad, arrived, vectors = layer(
        n,
        pieces,
        strip_at,
        packed_at,
        x_all,
        norm1_gain,
        norm1_bias,
        qkv_weight.reshape(width, 3 * lw),
        qv_bias,
        out_weight,
        out_bias,
        norm2_gain,
        norm2_bias,
        up_weight,
        up_bias,
        down_weight,
        down_bias,
        dec_weight,
        dec_bias,
        key_bias,
        spread_cot,
        jnp.asarray(spot, jnp.int32).reshape(1, n * chunk),
        jnp.asarray(spot, jnp.int32).reshape(n * chunk, 1),
        mask_grad,
    )
    decoded, patches_grad, up_grad, down_grad = finish(
        owned_pos.reshape(held, 1, n * chunk),
        arrived,
        mask_token,
        patch_all,
        up_grad.reshape(width, width),
        down_grad.reshape(width, width),
        seq,
        vis,
    )
    at_grad = at_grad.reshape(width, width)
    out_grad = at_grad[:lw].astype(F32)
    qkv_grad = at_grad[lw:].T.astype(F32).reshape(width, 3, lw)
    mixed = vectors[7]
    return (
        decoded,
        patches_grad,
        vectors[0],
        vectors[1],
        qkv_grad,
        mixed[: 2 * lw].reshape(2, lw),
        out_grad,
        vectors[4],
        vectors[2],
        vectors[3],
        up_grad,
        vectors[6],
        down_grad,
        vectors[5],
        dec_grad.reshape(width, feats).astype(F32),
        mixed[2 * lw : 2 * lw + feats],
        mixed[2 * lw + feats : 2 * lw + 2 * feats],
    )


def solution(mesh):
    return jax.shard_map(
        shards,
        mesh=mesh,
        in_specs=(
            P("dp", None),
            P(),
            P(),
            P(None, None, "mp"),
            P(None, "mp"),
            P("mp", None),
            P(),
            P(),
            P(),
            P(None, "mp"),
            P("mp"),
            P("mp", None),
            P(),
            P(None, "mp"),
            P("mp"),
            P("mp"),
            P(),
            P(),
            P(),
            P(),
            P("dp", None, "mp"),
        ),
        out_specs=(
            P("dp", None, "mp"),
            P("dp", None),
            P(),
            P(),
            P(None, None, "mp"),
            P(None, "mp"),
            P("mp", None),
            P(),
            P(),
            P(),
            P(None, "mp"),
            P("mp"),
            P("mp", None),
            P(),
            P(None, "mp"),
            P("mp"),
            P("mp"),
        ),
        check_vma=False,
    )
```

```python
from functools import partial

import jax
import jax.numpy as jnp
import numpy as np
from jax import lax
from jax.experimental import pallas as pl
from jax.experimental.pallas import tpu as pltpu
from jax.sharding import PartitionSpec as P

HD = 64
EPSILON = 1e-06
NEGATIVE = -1e30
F32 = jnp.float32
BF16 = jnp.bfloat16


def nn(a, b):
    return lax.dot_general(a, b, (((1,), (0,)), ((), ())), preferred_element_type=F32)


def tn(a, b):
    return lax.dot_general(a, b, (((0,), (0,)), ((), ())), preferred_element_type=F32)


def nt(a, b):
    return lax.dot_general(a, b, (((1,), (1,)), ((), ())), preferred_element_type=F32)


def norm_stats(inputs):
    centered = inputs - jnp.mean(inputs, -1, keepdims=True)
    inverse = lax.rsqrt(jnp.mean(centered * centered, -1, keepdims=True) + EPSILON)
    return centered * inverse, inverse


def norm_backward(incoming, normed, inverse, gain_vec):
    weighted = incoming * gain_vec
    inner = (
        weighted
        - jnp.mean(weighted, -1, keepdims=True)
        - normed * jnp.mean(weighted * normed, -1, keepdims=True)
    )
    return inner * inverse, jnp.sum(incoming * normed, 0), jnp.sum(incoming, 0)


def prepare_kernel(count, held_ref, len_ref, *refs):
    pos_ref, cot_ref, vis_ref, blank_ref, patches_ref, out_ref, mask_ref, bias_ref, x_ref = refs

    @pl.when(pl.program_id(0) == 0)
    def _():
        mask_ref[...] = jnp.zeros_like(mask_ref)

    seq = cot_ref.shape[1]
    n, _, chunk, feats = out_ref.shape
    rows = bias_ref.shape[2]
    spot = lax.broadcasted_iota(jnp.int32, (n * chunk, seq), 1)
    chosen = (pos_ref[0] == spot).astype(F32)
    picked = nn(chosen.astype(BF16), cot_ref[0])
    out_ref[...] = picked.astype(BF16).reshape(n, 1, chunk, feats)
    hidden = 1.0 - jnp.sum(chosen, 0, keepdims=True)
    hidden = jnp.broadcast_to(hidden, (8, seq)).astype(BF16)
    mask_ref[...] += nn(hidden, cot_ref[0])
    place = lax.broadcasted_iota(jnp.int32, (1, seq), 1)
    usable = (blank_ref[0] == 0) & (place < len_ref[pl.program_id(0)])
    usable = jnp.broadcast_to(usable.astype(F32), (8, seq)).astype(BF16)
    at = lax.broadcasted_iota(jnp.int32, (seq, rows), 0)
    allowed = nn(usable, (vis_ref[0] == at).astype(F32).astype(BF16))
    bias_ref[0] = jnp.where(allowed[:1] > 0.5, 0.0, NEGATIVE)
    for s in range(patches_ref.shape[0] // count):

        @pl.when(pl.program_id(0) == s)
        def _():
            first, last = s * count, (s + 1) * count
            start = first // 16 * 16
            block = patches_ref[start:last].astype(F32)[first - start :]
            filler = jnp.zeros((rows - count, block.shape[1]), F32)
            x_ref[0] = jnp.concatenate([block, filler]).astype(BF16)


def prepare(held_strips, lengths, pos_col, cot, vis, blank, patches, n, chunk):
    held, seq, feats = cot.shape
    rows = vis.shape[2]
    width = patches.shape[1]
    return pl.pallas_call(
        partial(prepare_kernel, patches.shape[0] // held),
        grid_spec=pltpu.PrefetchScalarGridSpec(
            num_scalar_prefetch=2,
            grid=(held,),
            in_specs=[
                pl.BlockSpec((1, n * chunk, 1), lambda s, h, l: (s, 0, 0)),
                pl.BlockSpec((1, seq, feats), lambda s, h, l: (s, 0, 0)),
                pl.BlockSpec((1, 1, rows), lambda s, h, l: (h[s], 0, 0)),
                pl.BlockSpec((1, 1, seq), lambda s, h, l: (h[s], 0, 0)),
                pl.BlockSpec(patches.shape, lambda s, h, l: (0, 0)),
            ],
            out_specs=[
                pl.BlockSpec((n, 1, chunk, feats), lambda s, h, l: (0, s, 0, 0)),
                pl.BlockSpec((8, feats), lambda s, h, l: (0, 0)),
                pl.BlockSpec((1, 1, rows), lambda s, h, l: (s, 0, 0)),
                pl.BlockSpec((1, rows, width), lambda s, h, l: (s, 0, 0)),
            ],
        ),
        out_shape=[
            jax.ShapeDtypeStruct((n, held, chunk, feats), BF16),
            jax.ShapeDtypeStruct((8, feats), F32),
            jax.ShapeDtypeStruct((held, 1, rows), F32),
            jax.ShapeDtypeStruct((held, rows, width), BF16),
        ],
        name="prepare",
        compiler_params=pltpu.CompilerParams(vmem_limit_bytes=24 << 20),
    )(held_strips, lengths, pos_col, cot, vis, blank, patches)


def finish_kernel(vis, pos_ref, rows_ref, token_ref, patch_ref, *refs):
    up_ref, down_ref, at_ref, dec_ref = refs[:4]
    out_ref, patches_ref, up_out, down_out, out_out, qkv_out, dec_out = refs[4:]
    n, _, chunk, feats = rows_ref.shape
    seq = out_ref.shape[1]
    spot = lax.broadcasted_iota(jnp.int32, (seq, n * chunk), 0)
    chosen = (pos_ref[0] == spot).astype(F32)
    rows = nn(chosen.astype(BF16), rows_ref[...].reshape(n * chunk, feats))
    hidden = 1.0 - jnp.sum(chosen, 1, keepdims=True)
    token = token_ref[...].reshape(1, feats).astype(BF16).astype(F32)
    out_ref[0] = (rows + hidden * token).astype(BF16)
    up_out[...] = up_ref[...].astype(F32)
    down_out[...] = down_ref[...].astype(F32)
    dec_out[...] = dec_ref[...].astype(F32)

    @pl.when(pl.program_id(0) == 0)
    def _():
        out_out[...] = at_ref[...].astype(F32)

    @pl.when(pl.program_id(0) > 0)
    def _():
        qkv_out[...] = at_ref[...].astype(F32)

    for s in range(patches_ref.shape[0] // vis):

        @pl.when(pl.program_id(0) == s)
        def _():
            patches_ref[s * vis : (s + 1) * vis] = patch_ref[0, :vis].astype(F32)


def finish(pos_row, rows, token, patch_all, up_grad, down_grad, at_grad, dec_grad, seq, vis):
    n, held, chunk, feats = rows.shape
    _, each, width = patch_all.shape
    tall = width // held
    whole = pl.BlockSpec((held * vis, width), lambda s: (0, 0))
    tile = pl.BlockSpec((tall, width), lambda s: (s, 0))
    shape = jax.ShapeDtypeStruct
    return pl.pallas_call(
        partial(finish_kernel, vis),
        grid=(held,),
        in_specs=[
            pl.BlockSpec((1, 1, n * chunk), lambda s: (s, 0, 0)),
            pl.BlockSpec((n, 1, chunk, feats), lambda s: (0, s, 0, 0)),
            pl.BlockSpec(memory_space=pltpu.VMEM),
            pl.BlockSpec((1, each, width), lambda s: (s, 0, 0)),
            tile,
            tile,
            tile,
            pl.BlockSpec((tall, feats), lambda s: (s, 0)),
        ],
        out_specs=[
            pl.BlockSpec((1, seq, feats), lambda s: (s, 0, 0)),
            whole,
            tile,
            tile,
            pl.BlockSpec((tall, width), lambda s: (0, 0)),
            pl.BlockSpec((tall, width), lambda s: (jnp.maximum(s - 1, 0), 0)),
            pl.BlockSpec((tall, feats), lambda s: (s, 0)),
        ],
        out_shape=[
            shape((held, seq, feats), BF16),
            shape((held * vis, width), F32),
            shape((width, width), F32),
            shape((width, width), F32),
            shape((tall, width), F32),
            shape((width - tall, width), F32),
            shape((width, feats), F32),
        ],
        name="finish",
        compiler_params=pltpu.CompilerParams(vmem_limit_bytes=61 << 20),
    )(pos_row, rows, token, patch_all, up_grad, down_grad, at_grad, dec_grad)


MESH = pl.DeviceIdType.MESH


class Wires:
    def __init__(self, send, recv):
        self.send, self.recv, self.used = send, recv, 0

    def take(self, count=1):
        first = self.used
        self.used += count
        return first

    def copy(self, src, dst, target, index=None):
        index = self.take() if index is None else index
        return pltpu.make_async_remote_copy(
            src_ref=src,
            dst_ref=dst,
            send_sem=self.send.at[index],
            recv_sem=self.recv.at[index],
            device_id=target,
            device_id_type=MESH,
        )


class Place:
    def __init__(self, n):
        self.n = n
        self.d = lax.axis_index("dp")
        self.m = lax.axis_index("mp")
        self.core, self.y = self.m % 2, self.m // 2
        self.core_peer = (self.d, self.m + 1 - 2 * self.core)
        self.y_peer = (self.d, (self.m + 2) % 4)
        self.far_peer = (self.d, 3 - self.m)
        self.y_strip = (self.m + 2) % 4

    def strip(self, i):
        y = self.y + (1 - 2 * self.y) * (1 - i // 2)
        core = self.core + (1 - 2 * self.core) * (1 - i % 2)
        return 2 * y + core

    def dp_peer(self, k):
        return ((self.d + k) % self.n, self.m)


def meet_all(place):
    barrier = pltpu.get_barrier_semaphore()
    for peer in (place.core_peer, place.y_peer, place.far_peer):
        pl.semaphore_signal(barrier, inc=1, device_id=peer, device_id_type=MESH)

    def greet(k, carry):
        pl.semaphore_signal(barrier, inc=1, device_id=place.dp_peer(k), device_id_type=MESH)
        return carry

    lax.fori_loop(1, place.n, greet, 0)
    pl.semaphore_wait(barrier, place.n + 2)


class Spread:
    def __init__(self, wires, place, src, dst, blocks=True, local=True, tall=None):
        self.wires, self.place, self.src, self.blocks, self.local = wires, place, src, blocks, local
        d = place.d
        self.slot = dst.at[d] if tall is None else dst.at[pl.ds(pl.multiple_of(d * tall, tall), tall)]
        self.base = wires.take(place.n)

    def made(self, k):
        peer = self.place.dp_peer(k)
        src = self.src.at[peer[0]] if self.blocks else self.src
        return self.wires.copy(src, self.slot, peer, self.base + k)

    def start(self):
        def one(k, carry):
            self.made(k).start()
            return carry

        lax.fori_loop(1, self.place.n, one, 0)
        if self.local:
            self.slot[...] = self.src[self.place.d] if self.blocks else self.src[...]

    def wait(self):
        def one(k, carry):
            self.made(k).wait()
            return carry

        lax.fori_loop(1, self.place.n, one, 0)


class Scatter:
    def __init__(self, wires, place, core_send, core_recv, y_send, y_recv):
        self.core_send, self.core_recv, self.y_send, self.y_recv = core_send, core_recv, y_send, y_recv
        self.core = [
            wires.copy(core_send.at[i], core_recv.at[i], place.core_peer) for i in range(2)
        ]
        self.away = wires.copy(y_send, y_recv, place.y_peer)

    def give_core(self, i, value):
        self.core_send[i] = value.astype(BF16)
        self.core[i].start()

    def give_y(self, value):
        self.core[0].wait_recv()
        self.y_send[...] = (value + self.core_recv[0].astype(F32)).astype(BF16)

    def own(self, value, arrived=False):
        self.core[1].wait_recv()
        if not arrived:
            self.away.wait_recv()
        return value + self.core_recv[1].astype(F32) + self.y_recv[...].astype(F32)

    def close(self):
        for made in (*self.core, self.away):
            made.wait_send()


class Gather:
    def __init__(self, wires, place, full, src=None):
        spot, passing = full.at[place.m], full.at[place.y_strip]
        src = spot if src is None else src
        self.over_y = wires.copy(src, spot, place.y_peer)
        self.over_core = wires.copy(src, spot, place.core_peer)
        self.passed = wires.copy(passing, passing, place.core_peer)

    def start(self):
        self.over_y.start()
        self.over_core.start()

    def forward(self):
        self.over_y.wait_recv()
        self.passed.start()

    def wait(self):
        self.over_core.wait_recv()
        self.passed.wait_recv()

    def close(self):
        for made in (self.over_y, self.over_core, self.passed):
            made.wait_send()


class Reduce:
    def __init__(self, wires, place, g, recv, h, bits):
        self.g, self.recv, self.h = g, recv, h
        n = place.n
        base, size = 0, n
        self.halves, self.doubles, path = [], [], []
        for k in bits:
            half = size // 2
            bit = (place.d // (1 << k)) % 2
            peer = (place.d + (1 - 2 * bit) * (1 << k), place.m)
            keep, away, landing = base + bit * half, base + (1 - bit) * half, n - size
            made = wires.copy(g.at[pl.ds(away, half)], recv.at[pl.ds(landing, half)], peer)
            self.halves.append((made, keep, landing, half))
            path.append((base, peer))
            base, size = keep, half
        self.mine = base
        for start, peer in reversed(path):
            held = h.at[pl.ds(base, size)]
            self.doubles.append(wires.copy(held, held, peer))
            base, size = start, size * 2

    def steps(self):
        g, recv, h = self.g, self.recv, self.h
        for made, keep, landing, half in self.halves:
            made.start()
            yield
            made.wait_recv()

            def add(i, carry):
                total = g[keep + i].astype(F32) + recv[landing + i].astype(F32)
                g[keep + i] = total.astype(BF16)
                return carry

            lax.fori_loop(0, half, add, 0)
        h[self.mine] = g[self.mine]
        for made in self.doubles:
            made.start()
            yield
            made.wait_recv()
        for made in [half[0] for half in self.halves] + self.doubles:
            made.wait_send()


class Group:
    def __init__(self, sums):
        self.todo = [one.steps() for one in sums]

    def go(self):
        self.todo = [steps for steps in self.todo if next(steps, self) is not self]
        return bool(self.todo)


def layer_kernel(
    n,
    order_in,
    order_out,
    x_ref,
    gain1_ref,
    shift1_ref,
    qkv_w_ref,
    qv_b_ref,
    out_w_ref,
    out_b_ref,
    gain2_ref,
    shift2_ref,
    up_w_ref,
    up_b_ref,
    down_w_ref,
    down_b_ref,
    dec_w_ref,
    dec_b_ref,
    bias_ref,
    cot_ref,
    spot_row,
    spot_col,
    mask_ref,
    patch_hbm,
    h_up,
    h_down,
    h_at,
    h_dec,
    hop4,
    vec_ref,
    qkv,
    att,
    stat,
    mid,
    low2,
    act,
    slope,
    g3_low,
    mid_all,
    g_full,
    decs,
    a_cs,
    a_cr,
    a_ys,
    a_yr,
    b_cs,
    b_cr,
    b_ys,
    b_yr,
    own_a,
    own_b,
    own_c,
    acc,
    g_up,
    g_down,
    g_at,
    g_dec,
    r_up,
    r_down,
    r_at,
    r_dec,
    hop1,
    send2,
    hop2,
    v_own,
    w_own,
    w_all,
    copy_sem,
    send_sem,
    recv_sem,
):
    place = Place(n)
    wires = Wires(send_sem, recv_sem)
    held, rows, width = x_ref.shape
    lw = att.shape[2]
    chunk, feats = hop4.shape[2:]
    scale = HD ** (-0.5)
    row = lambda ref: ref[...].reshape(1, -1)
    total = lambda v: jnp.sum(v, 0, keepdims=True)
    m = place.m
    temp = acc.at[pl.ds(0, rows)]
    fin_all, patch_all, send3, hop3 = g3_low, act, send2, hop1

    decs_in = Gather(wires, place, decs, dec_w_ref)
    cot_one = Spread(wires, place, cot_ref, hop1)
    cot_two = Spread(wires, place, send2, hop2)
    att_sum = Scatter(wires, place, a_cs, a_cr, a_ys, a_yr)
    low2_in = Gather(wires, place, low2)
    g_in = Gather(wires, place, g_full)
    ff_sum = Scatter(wires, place, b_cs, b_cr, b_ys, b_yr)
    h2_sum = Scatter(wires, place, a_cs, a_cr, a_ys, a_yr)
    mid_in = Gather(wires, place, mid_all)
    fin_in = Gather(wires, place, fin_all)
    h1_sum = Scatter(wires, place, a_cs, a_cr, a_ys, a_yr)
    patch_in = Gather(wires, place, patch_all)
    out_one = Spread(wires, place, send3, hop3)
    out_two = Spread(wires, place, send3, hop4)
    told = Spread(wires, place, v_own, acc, blocks=False, tall=v_own.shape[0])
    shared = [
        wires.copy(w_own, w_all.at[m], peer)
        for peer in (place.core_peer, place.y_peer, place.far_peer)
    ]
    bits = list(range(n.bit_length() - 1))
    turned = [bits[1], bits[0], *bits[2:]]
    pieces = g_up.shape[0]
    ways = [bits, turned] if pieces > 1 else [bits]


    def group(g, recv, h):
        return Group(
            [Reduce(wires, place, g.at[i], recv.at[i], h.at[i], ways[i]) for i in range(pieces)]
        )

    up, down, at = group(g_up, r_up, h_up), group(g_down, r_down, h_down), group(g_at, r_at, h_at)
    dec_one = Spread(wires, place, g_dec, r_dec)
    dec_two = Spread(wires, place, h_dec.at[place.d], h_dec, blocks=False, local=False)

    meet_all(place)
    decs_in.start()
    decs[m] = dec_w_ref[...]
    cot_one.start()

    def regroup(order_ref, src, dst):
        def one(k, carry):
            j = order_ref[k]
            dst[k // held, k % held] = src[j // held, j % held]
            return carry

        lax.fori_loop(0, n * held, one, 0)

    qkv_shift = jnp.concatenate([qv_b_ref[0:1], jnp.zeros((1, lw), F32), qv_b_ref[1:2]], 1)
    lane = lax.broadcasted_iota(jnp.int32, (1, 3 * lw), 1)
    qkv_scale = jnp.where(lane < lw, scale, 1.0)

    def low_one(s):
        normed, _ = norm_stats(x_ref[s].astype(F32))
        return (normed * row(gain1_ref) + row(shift1_ref)).astype(BF16)

    def attention(i, carry):
        s = place.strip(i)
        proj = (nt(low_one(s), qkv_w_ref[...]) + qkv_shift) * qkv_scale
        qkv[s] = proj.astype(BF16)
        bias = bias_ref[s]
        outs = []
        spot = lax.broadcasted_iota(jnp.int32, (rows, 128), 1)
        stats = jnp.zeros((rows, 128), F32)
        for h in range(lw // HD):
            q = qkv[s, :, h * HD : (h + 1) * HD]
            k = qkv[s, :, lw + h * HD : lw + (h + 1) * HD]
            v = qkv[s, :, 2 * lw + h * HD : 2 * lw + (h + 1) * HD]
            scores = nt(q, k) + bias
            top = jnp.max(scores, -1, keepdims=True)
            e = jnp.exp(scores - top)
            norm = jnp.sum(e, -1, keepdims=True)
            outs.append((nn(e.astype(BF16), v) / norm).astype(BF16))
            stats = jnp.where(spot == h, top + jnp.log(norm), stats)
        att[s] = jnp.concatenate(outs, -1)
        stat[s] = stats
        temp[...] = nn(att[s], out_w_ref[...])

        @pl.when(i == 0)
        def _():
            att_sum.give_core(0, temp[...])

        @pl.when(i == 1)
        def _():
            att_sum.give_y(temp[...])
            decs_in.forward()
            att_sum.away.start()

        @pl.when(i == 2)
        def _():
            att_sum.give_core(1, temp[...])
            cot_one.wait()
            regroup(order_in, hop1, send2)
            cot_two.start()

        return carry

    lax.fori_loop(0, held, attention, 0)
    mid[...] = x_ref[m].astype(F32) + row(out_b_ref) + att_sum.own(temp[...])
    normed, _ = norm_stats(mid[...])
    low2[m] = (normed * row(gain2_ref) + row(shift2_ref)).astype(BF16)
    low2_in.start()
    att_sum.close()
    cot_two.wait()
    t = lax.broadcasted_iota(jnp.int32, (rows, n * chunk), 0)
    sel = (t == spot_row[...]).astype(F32).astype(BF16)
    for s in range(held):
        g_full[m, s] = nn(sel, hop2[:, s].reshape(n * chunk, feats)).astype(BF16)
    decs_in.wait()
    v_own[...] = jnp.zeros_like(v_own)
    low2_in.forward()
    g_in.start()
    low2_in.wait()

    tall = 16

    def feed_forward(i, carry):
        s = place.strip(i)
        temp[...] = nn(low2[s], up_w_ref[...]) + row(up_b_ref)

        def some(r, inner):
            at = pl.ds(pl.multiple_of(r * tall, tall), tall)
            pre = temp[at]
            half = 0.5 * (1.0 + lax.erf(pre * np.float32(0.5**0.5)))
            bell = jnp.exp(-0.5 * pre * pre) * np.float32((2 * np.pi) ** -0.5)
            act[s, at] = (pre * half).astype(BF16)
            slope[s, at] = (half + pre * bell).astype(BF16)
            return inner

        lax.fori_loop(0, rows // tall, some, 0)
        temp[...] = nn(act[s], down_w_ref[...])

        @pl.when(i == 0)
        def _():
            ff_sum.give_core(0, temp[...])

        @pl.when(i == 1)
        def _():
            ff_sum.give_y(temp[...])
            g_in.forward()
            ff_sum.away.start()

        @pl.when(i == 2)
        def _():
            ff_sum.give_core(1, temp[...])

        @pl.when(i == 3)
        def _():
            own_b[...] = temp[...].astype(BF16)

        return carry

    lax.fori_loop(0, held, feed_forward, 0)
    g_in.wait()

    def g_three(s):
        weight = jnp.concatenate([decs[i] for i in range(4)], 1)
        return nt(jnp.concatenate([g_full[i, s] for i in range(4)], 1), weight)

    def g_low(s, carry):
        g3_low[s] = g_three(s).astype(BF16)
        return carry

    lax.fori_loop(0, held, g_low, 0)

    def weight_grad(left, right, out):
        acc[...] = jnp.zeros_like(acc)

        def add(s, carry):
            acc[...] += tn(left[s], right[s])
            return carry

        lax.fori_loop(0, held, add, 0)
        out[...] = acc[...].reshape(out.shape).astype(BF16)

    weight_grad(act, g3_low, g_down)
    down.go()

    def backward_ff(i, carry):
        s = place.strip(i)
        g_pre = nt(g3_low[s], down_w_ref[...]) * slope[s].astype(F32)
        slope[s] = g_pre.astype(BF16)
        v_own[6:7] += total(g_pre)
        temp[...] = nt(slope[s], up_w_ref[...])

        @pl.when(i == 0)
        def _():
            h2_sum.give_core(0, temp[...])

        @pl.when(i == 1)
        def _():
            h2_sum.give_y(temp[...])
            ff_sum.away.wait_recv()
            h2_sum.away.start()
            down.go()

        @pl.when(i == 2)
        def _():
            h2_sum.give_core(1, temp[...])

        @pl.when(i == 3)
        def _():
            own_a[...] = temp[...]
            down.go()

        return carry

    lax.fori_loop(0, held, backward_ff, 0)
    weight_grad(low2, slope, g_up)
    up.go()
    final = mid[...] + ff_sum.own(own_b[...].astype(F32), arrived=True) + row(down_b_ref)
    fin_all[m] = final.astype(BF16)
    g_own = g_three(m)
    v_own[5:6] = total(g_own)

    g_h2 = h2_sum.own(own_a[...])
    normed, inverse = norm_stats(mid[...])
    g_norm, gain_sum, bias_sum = norm_backward(g_h2, normed, inverse, row(gain2_ref))
    g_mid = g_own + g_norm
    own_a[...] = g_mid
    mid_all[m] = g_mid.astype(BF16)
    mid_in.start()
    h2_sum.close()
    v_own[2:3] = gain_sum.reshape(1, width)
    v_own[3:4] = bias_sum.reshape(1, width)
    v_own[4:5] = total(g_mid)
    down.go()

    def dqkv(s):
        return slope[s, :, : 3 * lw]

    def attention_back(i, carry):
        s = place.strip(3 - i)

        @pl.when(i == 1)
        def _():
            mid_in.over_core.wait_recv()

        @pl.when(i == 2)
        def _():
            mid_in.forward()
            fin_in.start()

        @pl.when(i == 3)
        def _():
            mid_in.passed.wait_recv()

        grad = nt(mid_all[s], out_w_ref[...]).astype(BF16)
        bias = bias_ref[s]
        dq, dk, dv = [], [], []
        for h in range(lw // HD):
            q = qkv[s, :, h * HD : (h + 1) * HD]
            k = qkv[s, :, lw + h * HD : lw + (h + 1) * HD]
            v = qkv[s, :, 2 * lw + h * HD : 2 * lw + (h + 1) * HD]
            g = grad[:, h * HD : (h + 1) * HD]
            o = att[s, :, h * HD : (h + 1) * HD]
            p = jnp.exp(nt(q, k) + bias - stat[s, :, h : h + 1])
            dv.append(tn(p.astype(BF16), g).astype(BF16))
            inner = jnp.sum(g.astype(F32) * o.astype(F32), -1, keepdims=True)
            ds = (p * (nt(g, v) - inner)).astype(BF16)
            dq.append((nn(ds, k) * scale).astype(BF16))
            dk.append(tn(ds, q).astype(BF16))
        slope[s, :, : 3 * lw] = jnp.concatenate(dq + dk + dv, -1)
        temp[...] = nn(dqkv(s), qkv_w_ref[...])

        @pl.when(i == 0)
        def _():
            own_c[...] = temp[...].astype(BF16)
            up.go()

        @pl.when(i == 1)
        def _():
            h1_sum.give_core(1, temp[...])
            down.go()
            up.go()
            down.go()

        @pl.when(i == 2)
        def _():
            a_ys[...] = temp[...].astype(BF16)
            up.go()

        @pl.when(i == 3)
        def _():
            h1_sum.give_core(0, temp[...])
            h1_sum.give_y(a_ys[...].astype(F32))
            down.go()

        return carry

    lax.fori_loop(0, held, attention_back, 0)

    acc[...] = jnp.zeros_like(acc)

    def attention_grads(s, carry):
        acc[:lw] += tn(att[s], mid_all[s])
        acc[lw:] += tn(dqkv(s), low_one(s))
        return carry

    lax.fori_loop(0, held, attention_grads, 0)
    g_at[...] = acc[...].reshape(g_at.shape).astype(BF16)
    at.go()
    up.go()
    columns = jnp.zeros((1, 3 * lw), F32)
    dec_rows = jnp.zeros((1, feats), F32)
    for s in range(held):
        columns += total(dqkv(s).astype(F32))
        dec_rows += total(g_full[m, s].astype(F32))
    blank = jnp.zeros((1, width - 2 * lw - 2 * feats), F32)
    v_own[7:8] = jnp.concatenate(
        [columns[:, :lw], columns[:, 2 * lw :], dec_rows, mask_ref[0:1], blank], 1
    )

    fin_in.forward()
    h1_sum.away.start()
    fin_in.wait()
    t = lax.broadcasted_iota(jnp.int32, (n * chunk, rows), 1)
    sel = (t == spot_col[...]).astype(F32).astype(BF16)
    for s in range(held):
        projected = (nn(fin_all[s], dec_w_ref[...]) + row(dec_b_ref)).astype(BF16)
        send3[:, s] = nn(sel, projected).astype(BF16).reshape(n, chunk, feats)
    out_one.start()
    dec_grad = jnp.zeros((width, feats), F32)
    for s in range(held):
        dec_grad += tn(fin_all[s], g_full[m, s])
    g_dec[...] = dec_grad.reshape(g_dec.shape).astype(BF16)
    up.go()
    at.go()
    up.go()
    dec_one.start()
    at.go()

    g_h1 = h1_sum.own(own_c[...].astype(F32))
    normed, inverse = norm_stats(x_ref[m].astype(F32))
    g_norm, gain_sum, bias_sum = norm_backward(g_h1, normed, inverse, row(gain1_ref))
    patch_all[m] = (own_a[...] + g_norm).astype(BF16)
    patch_in.start()
    v_own[0:1] = gain_sum.reshape(1, width)
    v_own[1:2] = bias_sum.reshape(1, width)
    at.go()
    out_one.wait()
    regroup(order_out, hop3, send3)
    out_two.start()
    told.start()
    at.go()
    at.go()
    dec_one.wait()
    dec_total = lax.fori_loop(1, n, lambda i, v: v + r_dec[i].astype(F32), r_dec[0].astype(F32))
    h_dec[place.d] = dec_total.astype(BF16)
    dec_two.start()
    told.wait()
    w_own[...] = lax.fori_loop(
        1, n, lambda i, v: v + acc[pl.ds(pl.multiple_of(8 * i, 8), 8)], acc[0:8]
    )
    for made in shared:
        made.start()
    w_all[m] = w_own[...]
    out_two.wait()
    for made in shared:
        made.wait()
    summed = w_all[0] + w_all[1] + w_all[2] + w_all[3]
    vec_ref[...] = jnp.concatenate([summed[:6], w_own[6:8]], 0)
    patch_in.forward()
    while any([group.go() for group in (down, up, at)]):
        pass
    dec_two.wait()
    patch_in.wait()
    store = pltpu.make_async_copy(patch_all, patch_hbm, copy_sem)
    store.start()
    for made in (decs_in, low2_in, g_in, ff_sum, mid_in, fin_in, h1_sum, patch_in):
        made.close()
    store.wait()


def vmem(count):
    return [pl.BlockSpec(memory_space=pltpu.VMEM)] * count


def layer(n, pieces, order_in, order_out, x, *rest):
    held, rows, width = x.shape
    lw = rest[4].shape[0]
    _, _, chunk, feats = rest[-4].shape
    each = width // (pieces * n)
    shape = jax.ShapeDtypeStruct
    low = lambda *dims: pltpu.VMEM(dims, BF16)
    full = lambda *dims: pltpu.VMEM(dims, F32)
    bits = n.bit_length() - 1
    sems = 7 * n + 64 + 2 * (3 * pieces + 1) * bits
    part = (pieces, n, each, width)
    got = (pieces, n - 1, each, width)
    strips = low(held, rows, width)
    links = [low(2, rows, width), low(2, rows, width), low(rows, width), low(rows, width)]
    hop = low(n, held, chunk, feats)
    smem = pl.BlockSpec(memory_space=pltpu.SMEM)
    return pl.pallas_call(
        partial(layer_kernel, n),
        in_specs=[smem, smem] + vmem(1 + len(rest)),
        out_specs=[pl.BlockSpec(memory_space=pl.ANY)] + vmem(6),
        out_shape=[
            shape((held, rows, width), BF16),
            shape(part, BF16),
            shape(part, BF16),
            shape(part, BF16),
            shape((n, width // n, feats), BF16),
            shape((n, held, chunk, feats), BF16),
            shape((8, width), F32),
        ],
        scratch_shapes=[
            low(held, rows, 3 * lw),
            low(held, rows, lw),
            full(held, rows, 128),
            full(rows, width),
            strips,
            strips,
            strips,
            strips,
            strips,
            low(4, held, rows, feats),
            low(4, width, feats),
            *links,
            *links,
            full(rows, width),
            low(rows, width),
            low(rows, width),
            full(width, width),
            low(*part),
            low(*part),
            low(*part),
            low(n, width // n, feats),
            low(*got),
            low(*got),
            low(*got),
            low(n, width // n, feats),
            hop,
            hop,
            hop,
            full(8, width),
            full(8, width),
            full(4, 8, width),
            pltpu.SemaphoreType.DMA,
            pltpu.SemaphoreType.DMA((sems,)),
            pltpu.SemaphoreType.DMA((sems,)),
        ],
        name="layer",
        compiler_params=pltpu.CompilerParams(
            collective_id=0, has_side_effects=True, vmem_limit_bytes=62 << 20
        ),
    )(order_in, order_out, x, *rest)


def shards(
    patches,
    norm1_gain,
    norm1_bias,
    qkv_weight,
    qv_bias,
    out_weight,
    out_bias,
    norm2_gain,
    norm2_bias,
    up_weight,
    up_bias,
    down_weight,
    down_bias,
    dec_weight,
    dec_bias,
    mask_token,
    lengths,
    blank,
    visible,
    plan,
    dec_cot,
):
    n = lax.axis_size("dp")
    d = lax.axis_index("dp")
    held, seq, feats = dec_cot.shape
    vis = visible.shape[1]
    strips = plan.shape[0]
    width = patches.shape[1]
    lw = qkv_weight.shape[2]
    rows = -(-vis // 16) * 16
    real = -(-vis // n)
    chunk = -(-real // 8) * 8

    strip_ids = jnp.arange(strips, dtype=jnp.int32)
    earlier = (plan[None, :] == plan[:, None]) & (strip_ids[None, :] < strip_ids[:, None])
    packed_at = plan * held + jnp.sum(earlier.astype(jnp.int32), 1)
    strip_at = jnp.sum(
        jnp.where(packed_at[None, :] == strip_ids[:, None], strip_ids[None, :], 0), 1
    )
    held_strips = lax.dynamic_slice_in_dim(strip_at, d * held, held)
    owned_pos = lax.dynamic_slice_in_dim(visible, d * held, held)
    owned_pos = jnp.pad(owned_pos, ((0, 0), (0, n * real - vis)), constant_values=-1)
    owned_pos = jnp.pad(
        owned_pos.reshape(held, n, real), ((0, 0), (0, 0), (0, chunk - real)), constant_values=-1
    )

    vis_rows = jnp.pad(visible, ((0, 0), (0, rows - vis)), constant_values=-1)
    spread_cot, mask_grad, key_bias, x_all = prepare(
        held_strips,
        lengths[held_strips],
        owned_pos.reshape(held, n * chunk, 1),
        dec_cot,
        vis_rows.reshape(strips, 1, rows),
        blank.reshape(strips, 1, seq),
        patches,
        n,
        chunk,
    )
    spot = np.arange(n * chunk)
    spot = np.where(spot % chunk < real, spot // chunk * real + spot % chunk, -1)
    pieces = 2 if width // n % 32 == 0 else 1
    patch_all, up_grad, down_grad, at_grad, dec_grad, arrived, vectors = layer(
        n,
        pieces,
        strip_at,
        packed_at,
        x_all,
        norm1_gain,
        norm1_bias,
        qkv_weight.reshape(width, 3 * lw).T,
        qv_bias,
        out_weight,
        out_bias,
        norm2_gain,
        norm2_bias,
        up_weight,
        up_bias,
        down_weight,
        down_bias,
        dec_weight,
        dec_bias,
        key_bias,
        spread_cot,
        jnp.asarray(spot, jnp.int32).reshape(1, n * chunk),
        jnp.asarray(spot, jnp.int32).reshape(n * chunk, 1),
        mask_grad,
    )
    decoded, patches_grad, up_grad, down_grad, out_grad, qkv_grad, dec_grad = finish(
        owned_pos.reshape(held, 1, n * chunk),
        arrived,
        mask_token,
        patch_all,
        up_grad.reshape(width, width),
        down_grad.reshape(width, width),
        at_grad.reshape(width, width),
        dec_grad.reshape(width, feats),
        seq,
        vis,
    )
    qkv_grad = qkv_grad.T.reshape(width, 3, lw)
    mixed = vectors[7]
    return (
        decoded,
        patches_grad,
        vectors[0],
        vectors[1],
        qkv_grad,
        mixed[: 2 * lw].reshape(2, lw),
        out_grad,
        vectors[4],
        vectors[2],
        vectors[3],
        up_grad,
        vectors[6],
        down_grad,
        vectors[5],
        dec_grad,
        mixed[2 * lw : 2 * lw + feats],
        mixed[2 * lw + feats : 2 * lw + 2 * feats],
    )


def solution(mesh):
    return jax.shard_map(
        shards,
        mesh=mesh,
        in_specs=(
            P("dp", None),
            P(),
            P(),
            P(None, None, "mp"),
            P(None, "mp"),
            P("mp", None),
            P(),
            P(),
            P(),
            P(None, "mp"),
            P("mp"),
            P("mp", None),
            P(),
            P(None, "mp"),
            P("mp"),
            P("mp"),
            P(),
            P(),
            P(),
            P(),
            P("dp", None, "mp"),
        ),
        out_specs=(
            P("dp", None, "mp"),
            P("dp", None),
            P(),
            P(),
            P(None, None, "mp"),
            P(None, "mp"),
            P("mp", None),
            P(),
            P(),
            P(),
            P(None, "mp"),
            P("mp"),
            P("mp", None),
            P(),
            P(None, "mp"),
            P("mp"),
            P("mp"),
        ),
        check_vma=False,
    )
```

```python
from functools import partial

import jax
import jax.numpy as jnp
import numpy as np
from jax import lax
from jax.experimental import pallas as pl
from jax.experimental.pallas import tpu as pltpu
from jax.sharding import PartitionSpec as P

HD = 64
EPSILON = 1e-06
NEGATIVE = -1e30
F32 = jnp.float32
BF16 = jnp.bfloat16


def nn(a, b):
    return lax.dot_general(a, b, (((1,), (0,)), ((), ())), preferred_element_type=F32)


def tn(a, b):
    return lax.dot_general(a, b, (((0,), (0,)), ((), ())), preferred_element_type=F32)


def nt(a, b):
    return lax.dot_general(a, b, (((1,), (1,)), ((), ())), preferred_element_type=F32)


def norm_stats(inputs):
    centered = inputs - jnp.mean(inputs, -1, keepdims=True)
    inverse = lax.rsqrt(jnp.mean(centered * centered, -1, keepdims=True) + EPSILON)
    return centered * inverse, inverse


def norm_backward(incoming, normed, inverse, gain_vec):
    weighted = incoming * gain_vec
    inner = (
        weighted
        - jnp.mean(weighted, -1, keepdims=True)
        - normed * jnp.mean(weighted * normed, -1, keepdims=True)
    )
    return inner * inverse, jnp.sum(incoming * normed, 0), jnp.sum(incoming, 0)


def prepare_kernel(count, held_ref, len_ref, *refs):
    pos_ref, cot_ref, vis_ref, blank_ref, patches_ref, out_ref, mask_ref, bias_ref, x_ref = refs

    @pl.when(pl.program_id(0) == 0)
    def _():
        mask_ref[...] = jnp.zeros_like(mask_ref)

    seq = cot_ref.shape[1]
    n, _, chunk, feats = out_ref.shape
    rows = bias_ref.shape[2]
    spot = lax.broadcasted_iota(jnp.int32, (n * chunk, seq), 1)
    chosen = (pos_ref[0] == spot).astype(F32)
    picked = nn(chosen.astype(BF16), cot_ref[0])
    out_ref[...] = picked.astype(BF16).reshape(n, 1, chunk, feats)
    hidden = 1.0 - jnp.sum(chosen, 0, keepdims=True)
    hidden = jnp.broadcast_to(hidden, (8, seq)).astype(BF16)
    mask_ref[...] += nn(hidden, cot_ref[0])
    place = lax.broadcasted_iota(jnp.int32, (1, seq), 1)
    strip = held_ref[pl.program_id(0)]
    usable = (blank_ref[pl.ds(strip, 1)] == 0) & (place < len_ref[strip])
    usable = jnp.broadcast_to(usable.astype(F32), (8, seq)).astype(BF16)
    at = lax.broadcasted_iota(jnp.int32, (seq, rows), 0)
    allowed = nn(usable, (vis_ref[pl.ds(strip, 1)] == at).astype(F32).astype(BF16))
    bias_ref[0] = jnp.where(allowed[:1] > 0.5, 0.0, NEGATIVE)
    for s in range(patches_ref.shape[0] // count):

        @pl.when(pl.program_id(0) == s)
        def _():
            first, last = s * count, (s + 1) * count
            start = first // 16 * 16
            block = patches_ref[start:last].astype(F32)[first - start :]
            filler = jnp.zeros((rows - count, block.shape[1]), F32)
            x_ref[0] = jnp.concatenate([block, filler]).astype(BF16)


def prepare(held_strips, lengths, pos_col, cot, vis, blank, patches, n, chunk):
    held, seq, feats = cot.shape
    rows = vis.shape[1]
    width = patches.shape[1]
    return pl.pallas_call(
        partial(prepare_kernel, patches.shape[0] // held),
        grid_spec=pltpu.PrefetchScalarGridSpec(
            num_scalar_prefetch=2,
            grid=(held,),
            in_specs=[
                pl.BlockSpec((1, n * chunk, 1), lambda s, h, l: (s, 0, 0)),
                pl.BlockSpec((1, seq, feats), lambda s, h, l: (s, 0, 0)),
                pl.BlockSpec(vis.shape, lambda s, h, l: (0, 0)),
                pl.BlockSpec(blank.shape, lambda s, h, l: (0, 0)),
                pl.BlockSpec(patches.shape, lambda s, h, l: (0, 0)),
            ],
            out_specs=[
                pl.BlockSpec((n, 1, chunk, feats), lambda s, h, l: (0, s, 0, 0)),
                pl.BlockSpec((8, feats), lambda s, h, l: (0, 0)),
                pl.BlockSpec((1, 1, rows), lambda s, h, l: (s, 0, 0)),
                pl.BlockSpec((1, rows, width), lambda s, h, l: (s, 0, 0)),
            ],
        ),
        out_shape=[
            jax.ShapeDtypeStruct((n, held, chunk, feats), BF16),
            jax.ShapeDtypeStruct((8, feats), F32),
            jax.ShapeDtypeStruct((held, 1, rows), F32),
            jax.ShapeDtypeStruct((held, rows, width), BF16),
        ],
        name="prepare",
        compiler_params=pltpu.CompilerParams(vmem_limit_bytes=24 << 20),
    )(held_strips, lengths, pos_col, cot, vis, blank, patches)


def finish_kernel(vis, pos_ref, rows_ref, token_ref, patch_ref, *refs):
    up_ref, down_ref, at_ref, dec_ref = refs[:4]
    out_ref, patches_ref, up_out, down_out, out_out, qkv_out, dec_out = refs[4:]
    n, _, chunk, feats = rows_ref.shape
    seq = out_ref.shape[1]
    spot = lax.broadcasted_iota(jnp.int32, (seq, n * chunk), 0)
    chosen = (pos_ref[0] == spot).astype(F32)
    rows = nn(chosen.astype(BF16), rows_ref[...].reshape(n * chunk, feats))
    hidden = 1.0 - jnp.sum(chosen, 1, keepdims=True)
    token = token_ref[...].reshape(1, feats).astype(BF16).astype(F32)
    out_ref[0] = (rows + hidden * token).astype(BF16)
    up_out[...] = up_ref[...].astype(F32)
    down_out[...] = down_ref[...].astype(F32)
    dec_out[...] = dec_ref[...].astype(F32)

    @pl.when(pl.program_id(0) == 0)
    def _():
        out_out[...] = at_ref[...].astype(F32)

    @pl.when(pl.program_id(0) > 0)
    def _():
        qkv_out[...] = at_ref[...].astype(F32)

    for s in range(patches_ref.shape[0] // vis):

        @pl.when(pl.program_id(0) == s)
        def _():
            patches_ref[s * vis : (s + 1) * vis] = patch_ref[0, :vis].astype(F32)


def finish(pos_row, rows, token, patch_all, up_grad, down_grad, at_grad, dec_grad, seq, vis):
    n, held, chunk, feats = rows.shape
    _, each, width = patch_all.shape
    tall = width // held
    whole = pl.BlockSpec((held * vis, width), lambda s: (0, 0))
    tile = pl.BlockSpec((tall, width), lambda s: (s, 0))
    shape = jax.ShapeDtypeStruct
    return pl.pallas_call(
        partial(finish_kernel, vis),
        grid=(held,),
        in_specs=[
            pl.BlockSpec((1, 1, n * chunk), lambda s: (s, 0, 0)),
            pl.BlockSpec((n, 1, chunk, feats), lambda s: (0, s, 0, 0)),
            pl.BlockSpec(memory_space=pltpu.VMEM),
            pl.BlockSpec((1, each, width), lambda s: (s, 0, 0)),
            tile,
            tile,
            tile,
            pl.BlockSpec((tall, feats), lambda s: (s, 0)),
        ],
        out_specs=[
            pl.BlockSpec((1, seq, feats), lambda s: (s, 0, 0)),
            whole,
            tile,
            tile,
            pl.BlockSpec((tall, width), lambda s: (0, 0)),
            pl.BlockSpec((tall, width), lambda s: (jnp.maximum(s - 1, 0), 0)),
            pl.BlockSpec((tall, feats), lambda s: (s, 0)),
        ],
        out_shape=[
            shape((held, seq, feats), BF16),
            shape((held * vis, width), F32),
            shape((width, width), F32),
            shape((width, width), F32),
            shape((tall, width), F32),
            shape((width - tall, width), F32),
            shape((width, feats), F32),
        ],
        name="finish",
        compiler_params=pltpu.CompilerParams(vmem_limit_bytes=61 << 20),
    )(pos_row, rows, token, patch_all, up_grad, down_grad, at_grad, dec_grad)


MESH = pl.DeviceIdType.MESH


class Wires:
    def __init__(self, send, recv):
        self.send, self.recv, self.used = send, recv, 0

    def take(self, count=1):
        first = self.used
        self.used += count
        return first

    def copy(self, src, dst, target, index=None):
        index = self.take() if index is None else index
        return pltpu.make_async_remote_copy(
            src_ref=src,
            dst_ref=dst,
            send_sem=self.send.at[index],
            recv_sem=self.recv.at[index],
            device_id=target,
            device_id_type=MESH,
        )


class Place:
    def __init__(self, n):
        self.n = n
        self.d = lax.axis_index("dp")
        self.m = lax.axis_index("mp")
        self.core, self.y = self.m % 2, self.m // 2
        self.core_peer = (self.d, self.m + 1 - 2 * self.core)
        self.y_peer = (self.d, (self.m + 2) % 4)
        self.far_peer = (self.d, 3 - self.m)
        self.y_strip = (self.m + 2) % 4

    def strip(self, i):
        y = self.y + (1 - 2 * self.y) * (1 - i // 2)
        core = self.core + (1 - 2 * self.core) * (1 - i % 2)
        return 2 * y + core

    def dp_peer(self, k):
        return ((self.d + k) % self.n, self.m)


def meet_all(place):
    barrier = pltpu.get_barrier_semaphore()
    for peer in (place.core_peer, place.y_peer, place.far_peer):
        pl.semaphore_signal(barrier, inc=1, device_id=peer, device_id_type=MESH)

    def greet(k, carry):
        pl.semaphore_signal(barrier, inc=1, device_id=place.dp_peer(k), device_id_type=MESH)
        return carry

    lax.fori_loop(1, place.n, greet, 0)
    pl.semaphore_wait(barrier, place.n + 2)


class Spread:
    def __init__(self, wires, place, src, dst, blocks=True, local=True, tall=None):
        self.wires, self.place, self.src, self.blocks, self.local = wires, place, src, blocks, local
        d = place.d
        self.slot = dst.at[d] if tall is None else dst.at[pl.ds(pl.multiple_of(d * tall, tall), tall)]
        self.base = wires.take(place.n)

    def made(self, k):
        peer = self.place.dp_peer(k)
        src = self.src.at[peer[0]] if self.blocks else self.src
        return self.wires.copy(src, self.slot, peer, self.base + k)

    def start(self):
        def one(k, carry):
            self.made(k).start()
            return carry

        lax.fori_loop(1, self.place.n, one, 0)
        if self.local:
            self.slot[...] = self.src[self.place.d] if self.blocks else self.src[...]

    def wait(self):
        def one(k, carry):
            self.made(k).wait()
            return carry

        lax.fori_loop(1, self.place.n, one, 0)


class Scatter:
    def __init__(self, wires, place, core_send, core_recv, y_send, y_recv):
        self.core_send, self.core_recv, self.y_send, self.y_recv = core_send, core_recv, y_send, y_recv
        self.core = [
            wires.copy(core_send.at[i], core_recv.at[i], place.core_peer) for i in range(2)
        ]
        self.away = wires.copy(y_send, y_recv, place.y_peer)

    def give_core(self, i, value):
        self.core_send[i] = value.astype(BF16)
        self.core[i].start()

    def give_y(self, value):
        self.core[0].wait_recv()
        self.y_send[...] = (value + self.core_recv[0].astype(F32)).astype(BF16)

    def own(self, value, arrived=False):
        self.core[1].wait_recv()
        if not arrived:
            self.away.wait_recv()
        return value + self.core_recv[1].astype(F32) + self.y_recv[...].astype(F32)

    def close(self):
        for made in (*self.core, self.away):
            made.wait_send()


class Gather:
    def __init__(self, wires, place, full, src=None):
        spot, passing = full.at[place.m], full.at[place.y_strip]
        src = spot if src is None else src
        self.over_y = wires.copy(src, spot, place.y_peer)
        self.over_core = wires.copy(src, spot, place.core_peer)
        self.passed = wires.copy(passing, passing, place.core_peer)

    def start(self):
        self.over_y.start()
        self.over_core.start()

    def forward(self):
        self.over_y.wait_recv()
        self.passed.start()

    def wait(self):
        self.over_core.wait_recv()
        self.passed.wait_recv()

    def close(self):
        for made in (self.over_y, self.over_core, self.passed):
            made.wait_send()


class Reduce:
    def __init__(self, wires, place, g, recv, h, bits):
        self.g, self.recv, self.h = g, recv, h
        n = place.n
        base, size = 0, n
        self.halves, self.doubles, path = [], [], []
        for k in bits:
            half = size // 2
            bit = (place.d // (1 << k)) % 2
            peer = (place.d + (1 - 2 * bit) * (1 << k), place.m)
            keep, away, landing = base + bit * half, base + (1 - bit) * half, n - size
            made = wires.copy(g.at[pl.ds(away, half)], recv.at[pl.ds(landing, half)], peer)
            self.halves.append((made, keep, landing, half))
            path.append((base, peer))
            base, size = keep, half
        self.mine = base
        for start, peer in reversed(path):
            held = h.at[pl.ds(base, size)]
            self.doubles.append(wires.copy(held, held, peer))
            base, size = start, size * 2

    def steps(self):
        g, recv, h = self.g, self.recv, self.h
        for made, keep, landing, half in self.halves:
            made.start()
            yield
            made.wait_recv()

            def add(i, carry):
                total = g[keep + i].astype(F32) + recv[landing + i].astype(F32)
                g[keep + i] = total.astype(BF16)
                return carry

            lax.fori_loop(0, half, add, 0)
        h[self.mine] = g[self.mine]
        for made in self.doubles:
            made.start()
            yield
            made.wait_recv()
        for made in [half[0] for half in self.halves] + self.doubles:
            made.wait_send()


class Group:
    def __init__(self, sums):
        self.todo = [one.steps() for one in sums]

    def go(self):
        self.todo = [steps for steps in self.todo if next(steps, self) is not self]
        return bool(self.todo)


def layer_kernel(
    n,
    order_in,
    order_out,
    x_ref,
    gain1_ref,
    shift1_ref,
    qkv_w_ref,
    qv_b_ref,
    out_w_ref,
    out_b_ref,
    gain2_ref,
    shift2_ref,
    up_w_ref,
    up_b_ref,
    down_w_ref,
    down_b_ref,
    dec_w_ref,
    dec_b_ref,
    bias_ref,
    cot_ref,
    spot_row,
    spot_col,
    mask_ref,
    patch_hbm,
    h_up,
    h_down,
    h_at,
    h_dec,
    hop4,
    vec_ref,
    qkv,
    att,
    stat,
    mid,
    low2,
    act,
    slope,
    g3_low,
    mid_all,
    g_full,
    decs,
    a_cs,
    a_cr,
    a_ys,
    a_yr,
    b_cs,
    b_cr,
    b_ys,
    b_yr,
    own_a,
    own_b,
    own_c,
    acc,
    g_up,
    g_down,
    g_at,
    g_dec,
    r_up,
    r_down,
    r_at,
    r_dec,
    hop1,
    send2,
    hop2,
    v_own,
    w_own,
    w_all,
    copy_sem,
    send_sem,
    recv_sem,
):
    place = Place(n)
    wires = Wires(send_sem, recv_sem)
    held, rows, width = x_ref.shape
    lw = att.shape[2]
    chunk, feats = hop4.shape[2:]
    scale = HD ** (-0.5)
    row = lambda ref: ref[...].reshape(1, -1)
    total = lambda v: jnp.sum(v, 0, keepdims=True)
    m = place.m
    temp = acc.at[pl.ds(0, rows)]
    fin_all, patch_all, send3, hop3 = g3_low, act, send2, hop1

    decs_in = Gather(wires, place, decs, dec_w_ref)
    cot_one = Spread(wires, place, cot_ref, hop1)
    cot_two = Spread(wires, place, send2, hop2)
    att_sum = Scatter(wires, place, a_cs, a_cr, a_ys, a_yr)
    low2_in = Gather(wires, place, low2)
    g_in = Gather(wires, place, g_full)
    ff_sum = Scatter(wires, place, b_cs, b_cr, b_ys, b_yr)
    h2_sum = Scatter(wires, place, a_cs, a_cr, a_ys, a_yr)
    mid_in = Gather(wires, place, mid_all)
    fin_in = Gather(wires, place, fin_all)
    h1_sum = Scatter(wires, place, a_cs, a_cr, a_ys, a_yr)
    patch_in = Gather(wires, place, patch_all)
    out_one = Spread(wires, place, send3, hop3)
    out_two = Spread(wires, place, send3, hop4)
    told = Spread(wires, place, v_own, acc, blocks=False, tall=v_own.shape[0])
    shared = [
        wires.copy(w_own, w_all.at[m], peer)
        for peer in (place.core_peer, place.y_peer, place.far_peer)
    ]
    bits = list(range(n.bit_length() - 1))
    turned = [bits[1], bits[0], *bits[2:]]
    pieces = g_up.shape[0]
    ways = [bits, turned] if pieces > 1 else [bits]


    def group(g, recv, h):
        return Group(
            [Reduce(wires, place, g.at[i], recv.at[i], h.at[i], ways[i]) for i in range(pieces)]
        )

    up, down, at = group(g_up, r_up, h_up), group(g_down, r_down, h_down), group(g_at, r_at, h_at)
    dec_one = Spread(wires, place, g_dec, r_dec)
    dec_two = Spread(wires, place, h_dec.at[place.d], h_dec, blocks=False, local=False)

    meet_all(place)
    decs_in.start()
    decs[m] = dec_w_ref[...]
    cot_one.start()

    def regroup(order_ref, src, dst):
        def one(k, carry):
            j = order_ref[k]
            dst[k // held, k % held] = src[j // held, j % held]
            return carry

        lax.fori_loop(0, n * held, one, 0)

    qkv_shift = jnp.concatenate([qv_b_ref[0:1], jnp.zeros((1, lw), F32), qv_b_ref[1:2]], 1)
    lane = lax.broadcasted_iota(jnp.int32, (1, 3 * lw), 1)
    qkv_scale = jnp.where(lane < lw, scale, 1.0)

    def low_one(s):
        normed, _ = norm_stats(x_ref[s].astype(F32))
        return (normed * row(gain1_ref) + row(shift1_ref)).astype(BF16)

    def attention(i, carry):
        s = place.strip(i)
        proj = (nt(low_one(s), qkv_w_ref[...]) + qkv_shift) * qkv_scale
        qkv[s] = proj.astype(BF16)
        bias = bias_ref[s]
        outs = []
        spot = lax.broadcasted_iota(jnp.int32, (rows, 128), 1)
        stats = jnp.zeros((rows, 128), F32)
        for h in range(lw // HD):
            q = qkv[s, :, h * HD : (h + 1) * HD]
            k = qkv[s, :, lw + h * HD : lw + (h + 1) * HD]
            v = qkv[s, :, 2 * lw + h * HD : 2 * lw + (h + 1) * HD]
            scores = nt(q, k) + bias
            top = jnp.max(scores, -1, keepdims=True)
            e = jnp.exp(scores - top)
            norm = jnp.sum(e, -1, keepdims=True)
            outs.append((nn(e.astype(BF16), v) / norm).astype(BF16))
            stats = jnp.where(spot == h, top + jnp.log(norm), stats)
        att[s] = jnp.concatenate(outs, -1)
        stat[s] = stats
        temp[...] = nn(att[s], out_w_ref[...])

        @pl.when(i == 0)
        def _():
            att_sum.give_core(0, temp[...])

        @pl.when(i == 1)
        def _():
            att_sum.give_y(temp[...])
            decs_in.forward()
            att_sum.away.start()

        @pl.when(i == 2)
        def _():
            att_sum.give_core(1, temp[...])
            cot_one.wait()
            regroup(order_in, hop1, send2)
            cot_two.start()

        return carry

    lax.fori_loop(0, held, attention, 0)
    mid[...] = x_ref[m].astype(F32) + row(out_b_ref) + att_sum.own(temp[...])
    normed, _ = norm_stats(mid[...])
    low2[m] = (normed * row(gain2_ref) + row(shift2_ref)).astype(BF16)
    low2_in.start()
    att_sum.close()
    cot_two.wait()
    t = lax.broadcasted_iota(jnp.int32, (rows, n * chunk), 0)
    sel = (t == spot_row[...]).astype(F32).astype(BF16)
    for s in range(held):
        g_full[m, s] = nn(sel, hop2[:, s].reshape(n * chunk, feats)).astype(BF16)
    decs_in.wait()
    v_own[...] = jnp.zeros_like(v_own)
    low2_in.forward()
    g_in.start()
    low2_in.wait()

    tall = 16

    def feed_forward(i, carry):
        s = place.strip(i)
        temp[...] = nn(low2[s], up_w_ref[...]) + row(up_b_ref)

        def some(r, inner):
            at = pl.ds(pl.multiple_of(r * tall, tall), tall)
            pre = temp[at]
            half = 0.5 * (1.0 + lax.erf(pre * np.float32(0.5**0.5)))
            bell = jnp.exp(-0.5 * pre * pre) * np.float32((2 * np.pi) ** -0.5)
            act[s, at] = (pre * half).astype(BF16)
            slope[s, at] = (half + pre * bell).astype(BF16)
            return inner

        lax.fori_loop(0, rows // tall, some, 0)
        temp[...] = nn(act[s], down_w_ref[...])

        @pl.when(i == 0)
        def _():
            ff_sum.give_core(0, temp[...])

        @pl.when(i == 1)
        def _():
            ff_sum.give_y(temp[...])
            g_in.forward()
            ff_sum.away.start()

        @pl.when(i == 2)
        def _():
            ff_sum.give_core(1, temp[...])

        @pl.when(i == 3)
        def _():
            own_b[...] = temp[...].astype(BF16)

        return carry

    lax.fori_loop(0, held, feed_forward, 0)
    g_in.wait()

    def g_three(s):
        weight = jnp.concatenate([decs[i] for i in range(4)], 1)
        return nt(jnp.concatenate([g_full[i, s] for i in range(4)], 1), weight)

    def g_low(s, carry):
        g3_low[s] = g_three(s).astype(BF16)
        return carry

    lax.fori_loop(0, held, g_low, 0)

    def weight_grad(left, right, out):
        acc[...] = jnp.zeros_like(acc)

        def add(s, carry):
            acc[...] += tn(left[s], right[s])
            return carry

        lax.fori_loop(0, held, add, 0)
        out[...] = acc[...].reshape(out.shape).astype(BF16)

    weight_grad(act, g3_low, g_down)
    down.go()

    def backward_ff(i, carry):
        s = place.strip(i)
        g_pre = nt(g3_low[s], down_w_ref[...]) * slope[s].astype(F32)
        slope[s] = g_pre.astype(BF16)
        v_own[6:7] += total(g_pre)
        temp[...] = nt(slope[s], up_w_ref[...])

        @pl.when(i == 0)
        def _():
            h2_sum.give_core(0, temp[...])

        @pl.when(i == 1)
        def _():
            h2_sum.give_y(temp[...])
            ff_sum.away.wait_recv()
            h2_sum.away.start()
            down.go()

        @pl.when(i == 2)
        def _():
            h2_sum.give_core(1, temp[...])

        @pl.when(i == 3)
        def _():
            own_a[...] = temp[...]
            down.go()

        return carry

    lax.fori_loop(0, held, backward_ff, 0)
    weight_grad(low2, slope, g_up)
    up.go()
    final = mid[...] + ff_sum.own(own_b[...].astype(F32), arrived=True) + row(down_b_ref)
    fin_all[m] = final.astype(BF16)
    g_own = g_three(m)
    v_own[5:6] = total(g_own)

    g_h2 = h2_sum.own(own_a[...])
    normed, inverse = norm_stats(mid[...])
    g_norm, gain_sum, bias_sum = norm_backward(g_h2, normed, inverse, row(gain2_ref))
    g_mid = g_own + g_norm
    own_a[...] = g_mid
    mid_all[m] = g_mid.astype(BF16)
    mid_in.start()
    h2_sum.close()
    v_own[2:3] = gain_sum.reshape(1, width)
    v_own[3:4] = bias_sum.reshape(1, width)
    v_own[4:5] = total(g_mid)
    down.go()

    def dqkv(s):
        return slope[s, :, : 3 * lw]

    def attention_back(i, carry):
        s = place.strip(3 - i)

        @pl.when(i == 1)
        def _():
            mid_in.over_core.wait_recv()

        @pl.when(i == 2)
        def _():
            mid_in.forward()
            fin_in.start()

        @pl.when(i == 3)
        def _():
            mid_in.passed.wait_recv()

        grad = nt(mid_all[s], out_w_ref[...]).astype(BF16)
        bias = bias_ref[s]
        dq, dk, dv = [], [], []
        for h in range(lw // HD):
            q = qkv[s, :, h * HD : (h + 1) * HD]
            k = qkv[s, :, lw + h * HD : lw + (h + 1) * HD]
            v = qkv[s, :, 2 * lw + h * HD : 2 * lw + (h + 1) * HD]
            g = grad[:, h * HD : (h + 1) * HD]
            o = att[s, :, h * HD : (h + 1) * HD]
            p = jnp.exp(nt(q, k) + bias - stat[s, :, h : h + 1])
            dv.append(tn(p.astype(BF16), g).astype(BF16))
            inner = jnp.sum(g.astype(F32) * o.astype(F32), -1, keepdims=True)
            ds = (p * (nt(g, v) - inner)).astype(BF16)
            dq.append((nn(ds, k) * scale).astype(BF16))
            dk.append(tn(ds, q).astype(BF16))
        slope[s, :, : 3 * lw] = jnp.concatenate(dq + dk + dv, -1)
        temp[...] = nn(dqkv(s), qkv_w_ref[...])

        @pl.when(i == 0)
        def _():
            own_c[...] = temp[...].astype(BF16)
            up.go()

        @pl.when(i == 1)
        def _():
            h1_sum.give_core(1, temp[...])
            down.go()
            up.go()

        @pl.when(i == 2)
        def _():
            a_ys[...] = temp[...].astype(BF16)
            down.go()
            up.go()

        @pl.when(i == 3)
        def _():
            h1_sum.give_core(0, temp[...])
            h1_sum.give_y(a_ys[...].astype(F32))
            down.go()
            up.go()

        return carry

    lax.fori_loop(0, held, attention_back, 0)

    acc[...] = jnp.zeros_like(acc)

    def attention_grads(s, carry):
        acc[:lw] += tn(att[s], mid_all[s])
        acc[lw:] += tn(dqkv(s), low_one(s))
        return carry

    lax.fori_loop(0, held, attention_grads, 0)
    g_at[...] = acc[...].reshape(g_at.shape).astype(BF16)
    at.go()
    up.go()
    columns = jnp.zeros((1, 3 * lw), F32)
    dec_rows = jnp.zeros((1, feats), F32)
    for s in range(held):
        columns += total(dqkv(s).astype(F32))
        dec_rows += total(g_full[m, s].astype(F32))
    blank = jnp.zeros((1, width - 2 * lw - 2 * feats), F32)
    v_own[7:8] = jnp.concatenate(
        [columns[:, :lw], columns[:, 2 * lw :], dec_rows, mask_ref[0:1], blank], 1
    )

    fin_in.forward()
    h1_sum.away.start()
    fin_in.wait()
    t = lax.broadcasted_iota(jnp.int32, (n * chunk, rows), 1)
    sel = (t == spot_col[...]).astype(F32).astype(BF16)
    for s in range(held):
        projected = (nn(fin_all[s], dec_w_ref[...]) + row(dec_b_ref)).astype(BF16)
        send3[:, s] = nn(sel, projected).astype(BF16).reshape(n, chunk, feats)
    out_one.start()
    dec_grad = jnp.zeros((width, feats), F32)
    for s in range(held):
        dec_grad += tn(fin_all[s], g_full[m, s])
    g_dec[...] = dec_grad.reshape(g_dec.shape).astype(BF16)
    up.go()
    at.go()
    up.go()
    dec_one.start()
    at.go()

    g_h1 = h1_sum.own(own_c[...].astype(F32))
    normed, inverse = norm_stats(x_ref[m].astype(F32))
    g_norm, gain_sum, bias_sum = norm_backward(g_h1, normed, inverse, row(gain1_ref))
    patch_all[m] = (own_a[...] + g_norm).astype(BF16)
    patch_in.start()
    v_own[0:1] = gain_sum.reshape(1, width)
    v_own[1:2] = bias_sum.reshape(1, width)
    at.go()
    out_one.wait()
    regroup(order_out, hop3, send3)
    out_two.start()
    told.start()
    at.go()
    at.go()
    dec_one.wait()
    dec_total = lax.fori_loop(1, n, lambda i, v: v + r_dec[i].astype(F32), r_dec[0].astype(F32))
    h_dec[place.d] = dec_total.astype(BF16)
    dec_two.start()
    told.wait()
    w_own[...] = lax.fori_loop(
        1, n, lambda i, v: v + acc[pl.ds(pl.multiple_of(8 * i, 8), 8)], acc[0:8]
    )
    for made in shared:
        made.start()
    w_all[m] = w_own[...]
    out_two.wait()
    for made in shared:
        made.wait()
    summed = w_all[0] + w_all[1] + w_all[2] + w_all[3]
    vec_ref[...] = jnp.concatenate([summed[:6], w_own[6:8]], 0)
    patch_in.forward()
    while any([group.go() for group in (down, up, at)]):
        pass
    dec_two.wait()
    patch_in.wait()
    store = pltpu.make_async_copy(patch_all, patch_hbm, copy_sem)
    store.start()
    for made in (decs_in, low2_in, g_in, ff_sum, mid_in, fin_in, h1_sum, patch_in):
        made.close()
    store.wait()


def vmem(count):
    return [pl.BlockSpec(memory_space=pltpu.VMEM)] * count


def layer(n, pieces, order_in, order_out, x, *rest):
    held, rows, width = x.shape
    lw = rest[4].shape[0]
    _, _, chunk, feats = rest[-4].shape
    each = width // (pieces * n)
    shape = jax.ShapeDtypeStruct
    low = lambda *dims: pltpu.VMEM(dims, BF16)
    full = lambda *dims: pltpu.VMEM(dims, F32)
    bits = n.bit_length() - 1
    sems = 7 * n + 64 + 2 * (3 * pieces + 1) * bits
    part = (pieces, n, each, width)
    got = (pieces, n - 1, each, width)
    strips = low(held, rows, width)
    links = [low(2, rows, width), low(2, rows, width), low(rows, width), low(rows, width)]
    hop = low(n, held, chunk, feats)
    smem = pl.BlockSpec(memory_space=pltpu.SMEM)
    return pl.pallas_call(
        partial(layer_kernel, n),
        in_specs=[smem, smem] + vmem(1 + len(rest)),
        out_specs=[pl.BlockSpec(memory_space=pl.ANY)] + vmem(6),
        out_shape=[
            shape((held, rows, width), BF16),
            shape(part, BF16),
            shape(part, BF16),
            shape(part, BF16),
            shape((n, width // n, feats), BF16),
            shape((n, held, chunk, feats), BF16),
            shape((8, width), F32),
        ],
        scratch_shapes=[
            low(held, rows, 3 * lw),
            low(held, rows, lw),
            full(held, rows, 128),
            full(rows, width),
            strips,
            strips,
            strips,
            strips,
            strips,
            low(4, held, rows, feats),
            low(4, width, feats),
            *links,
            *links,
            full(rows, width),
            low(rows, width),
            low(rows, width),
            full(width, width),
            low(*part),
            low(*part),
            low(*part),
            low(n, width // n, feats),
            low(*got),
            low(*got),
            low(*got),
            low(n, width // n, feats),
            hop,
            hop,
            hop,
            full(8, width),
            full(8, width),
            full(4, 8, width),
            pltpu.SemaphoreType.DMA,
            pltpu.SemaphoreType.DMA((sems,)),
            pltpu.SemaphoreType.DMA((sems,)),
        ],
        name="layer",
        compiler_params=pltpu.CompilerParams(
            collective_id=0, has_side_effects=True, vmem_limit_bytes=62 << 20
        ),
    )(order_in, order_out, x, *rest)


def shards(
    patches,
    norm1_gain,
    norm1_bias,
    qkv_weight,
    qv_bias,
    out_weight,
    out_bias,
    norm2_gain,
    norm2_bias,
    up_weight,
    up_bias,
    down_weight,
    down_bias,
    dec_weight,
    dec_bias,
    mask_token,
    lengths,
    blank,
    visible,
    plan,
    dec_cot,
):
    n = lax.axis_size("dp")
    d = lax.axis_index("dp")
    held, seq, feats = dec_cot.shape
    vis = visible.shape[1]
    strips = plan.shape[0]
    width = patches.shape[1]
    lw = qkv_weight.shape[2]
    rows = -(-vis // 16) * 16
    real = -(-vis // n)
    chunk = -(-real // 8) * 8

    strip_ids = jnp.arange(strips, dtype=jnp.int32)
    earlier = (plan[None, :] == plan[:, None]) & (strip_ids[None, :] < strip_ids[:, None])
    packed_at = plan * held + jnp.sum(earlier.astype(jnp.int32), 1)
    strip_at = jnp.sum(
        jnp.where(packed_at[None, :] == strip_ids[:, None], strip_ids[None, :], 0), 1
    )
    held_strips = lax.dynamic_slice_in_dim(strip_at, d * held, held)
    owned_pos = lax.dynamic_slice_in_dim(visible, d * held, held)
    owned_pos = jnp.pad(owned_pos, ((0, 0), (0, n * real - vis)), constant_values=-1)
    owned_pos = jnp.pad(
        owned_pos.reshape(held, n, real), ((0, 0), (0, 0), (0, chunk - real)), constant_values=-1
    )

    vis_rows = jnp.pad(visible, ((0, 0), (0, rows - vis)), constant_values=-1)
    spread_cot, mask_grad, key_bias, x_all = prepare(
        held_strips,
        lengths,
        owned_pos.reshape(held, n * chunk, 1),
        dec_cot,
        vis_rows,
        blank,
        patches,
        n,
        chunk,
    )
    spot = np.arange(n * chunk)
    spot = np.where(spot % chunk < real, spot // chunk * real + spot % chunk, -1)
    pieces = 2 if width // n % 32 == 0 else 1
    patch_all, up_grad, down_grad, at_grad, dec_grad, arrived, vectors = layer(
        n,
        pieces,
        strip_at,
        packed_at,
        x_all,
        norm1_gain,
        norm1_bias,
        qkv_weight.reshape(width, 3 * lw).T,
        qv_bias,
        out_weight,
        out_bias,
        norm2_gain,
        norm2_bias,
        up_weight,
        up_bias,
        down_weight,
        down_bias,
        dec_weight,
        dec_bias,
        key_bias,
        spread_cot,
        jnp.asarray(spot, jnp.int32).reshape(1, n * chunk),
        jnp.asarray(spot, jnp.int32).reshape(n * chunk, 1),
        mask_grad,
    )
    decoded, patches_grad, up_grad, down_grad, out_grad, qkv_grad, dec_grad = finish(
        owned_pos.reshape(held, 1, n * chunk),
        arrived,
        mask_token,
        patch_all,
        up_grad.reshape(width, width),
        down_grad.reshape(width, width),
        at_grad.reshape(width, width),
        dec_grad.reshape(width, feats),
        seq,
        vis,
    )
    qkv_grad = qkv_grad.T.reshape(width, 3, lw)
    mixed = vectors[7]
    return (
        decoded,
        patches_grad,
        vectors[0],
        vectors[1],
        qkv_grad,
        mixed[: 2 * lw].reshape(2, lw),
        out_grad,
        vectors[4],
        vectors[2],
        vectors[3],
        up_grad,
        vectors[6],
        down_grad,
        vectors[5],
        dec_grad,
        mixed[2 * lw : 2 * lw + feats],
        mixed[2 * lw + feats : 2 * lw + 2 * feats],
    )


def solution(mesh):
    return jax.shard_map(
        shards,
        mesh=mesh,
        in_specs=(
            P("dp", None),
            P(),
            P(),
            P(None, None, "mp"),
            P(None, "mp"),
            P("mp", None),
            P(),
            P(),
            P(),
            P(None, "mp"),
            P("mp"),
            P("mp", None),
            P(),
            P(None, "mp"),
            P("mp"),
            P("mp"),
            P(),
            P(),
            P(),
            P(),
            P("dp", None, "mp"),
        ),
        out_specs=(
            P("dp", None, "mp"),
            P("dp", None),
            P(),
            P(),
            P(None, None, "mp"),
            P(None, "mp"),
            P("mp", None),
            P(),
            P(),
            P(),
            P(None, "mp"),
            P("mp"),
            P("mp", None),
            P(),
            P(None, "mp"),
            P("mp"),
            P("mp"),
        ),
        check_vma=False,
    )
```

```python
from functools import partial

import jax
import jax.numpy as jnp
import numpy as np
from jax import lax
from jax.experimental import pallas as pl
from jax.experimental.pallas import tpu as pltpu
from jax.sharding import PartitionSpec as P

HD = 64
EPSILON = 1e-06
NEGATIVE = -1e30
F32 = jnp.float32
BF16 = jnp.bfloat16


def nn(a, b):
    return lax.dot_general(a, b, (((1,), (0,)), ((), ())), preferred_element_type=F32)


def tn(a, b):
    return lax.dot_general(a, b, (((0,), (0,)), ((), ())), preferred_element_type=F32)


def nt(a, b):
    return lax.dot_general(a, b, (((1,), (1,)), ((), ())), preferred_element_type=F32)


def norm_stats(inputs):
    centered = inputs - jnp.mean(inputs, -1, keepdims=True)
    inverse = lax.rsqrt(jnp.mean(centered * centered, -1, keepdims=True) + EPSILON)
    return centered * inverse, inverse


def norm_backward(incoming, normed, inverse, gain_vec):
    weighted = incoming * gain_vec
    inner = (
        weighted
        - jnp.mean(weighted, -1, keepdims=True)
        - normed * jnp.mean(weighted * normed, -1, keepdims=True)
    )
    return inner * inverse, jnp.sum(incoming * normed, 0), jnp.sum(incoming, 0)


def prepare_kernel(count, held_ref, len_ref, *refs):
    pos_ref, cot_ref, vis_ref, blank_ref, patches_ref, out_ref, mask_ref, bias_ref, x_ref = refs

    @pl.when(pl.program_id(0) == 0)
    def _():
        mask_ref[...] = jnp.zeros_like(mask_ref)

    seq = cot_ref.shape[1]
    n, _, chunk, feats = out_ref.shape
    rows = bias_ref.shape[2]
    spot = lax.broadcasted_iota(jnp.int32, (n * chunk, seq), 1)
    chosen = (pos_ref[0] == spot).astype(F32)
    picked = nn(chosen.astype(BF16), cot_ref[0])
    out_ref[...] = picked.astype(BF16).reshape(n, 1, chunk, feats)
    hidden = 1.0 - jnp.sum(chosen, 0, keepdims=True)
    hidden = jnp.broadcast_to(hidden, (8, seq)).astype(BF16)
    mask_ref[...] += nn(hidden, cot_ref[0])
    place = lax.broadcasted_iota(jnp.int32, (1, seq), 1)
    strip = held_ref[pl.program_id(0)]
    usable = (blank_ref[pl.ds(strip, 1)] == 0) & (place < len_ref[strip])
    usable = jnp.broadcast_to(usable.astype(F32), (8, seq)).astype(BF16)
    at = lax.broadcasted_iota(jnp.int32, (seq, rows), 0)
    allowed = nn(usable, (vis_ref[pl.ds(strip, 1)] == at).astype(F32).astype(BF16))
    bias_ref[0] = jnp.where(allowed[:1] > 0.5, 0.0, NEGATIVE)
    for s in range(patches_ref.shape[0] // count):

        @pl.when(pl.program_id(0) == s)
        def _():
            first, last = s * count, (s + 1) * count
            start = first // 16 * 16
            block = patches_ref[start:last].astype(F32)[first - start :]
            filler = jnp.zeros((rows - count, block.shape[1]), F32)
            x_ref[0] = jnp.concatenate([block, filler]).astype(BF16)


def prepare(held_strips, lengths, pos_col, cot, vis, blank, patches, n, chunk):
    held, seq, feats = cot.shape
    rows = vis.shape[1]
    width = patches.shape[1]
    return pl.pallas_call(
        partial(prepare_kernel, patches.shape[0] // held),
        grid_spec=pltpu.PrefetchScalarGridSpec(
            num_scalar_prefetch=2,
            grid=(held,),
            in_specs=[
                pl.BlockSpec((1, n * chunk, 1), lambda s, h, l: (s, 0, 0)),
                pl.BlockSpec((1, seq, feats), lambda s, h, l: (s, 0, 0)),
                pl.BlockSpec(vis.shape, lambda s, h, l: (0, 0)),
                pl.BlockSpec(blank.shape, lambda s, h, l: (0, 0)),
                pl.BlockSpec(patches.shape, lambda s, h, l: (0, 0)),
            ],
            out_specs=[
                pl.BlockSpec((n, 1, chunk, feats), lambda s, h, l: (0, s, 0, 0)),
                pl.BlockSpec((8, feats), lambda s, h, l: (0, 0)),
                pl.BlockSpec((1, 1, rows), lambda s, h, l: (s, 0, 0)),
                pl.BlockSpec((1, rows, width), lambda s, h, l: (s, 0, 0)),
            ],
        ),
        out_shape=[
            jax.ShapeDtypeStruct((n, held, chunk, feats), BF16),
            jax.ShapeDtypeStruct((8, feats), F32),
            jax.ShapeDtypeStruct((held, 1, rows), F32),
            jax.ShapeDtypeStruct((held, rows, width), BF16),
        ],
        name="prepare",
        compiler_params=pltpu.CompilerParams(vmem_limit_bytes=24 << 20),
    )(held_strips, lengths, pos_col, cot, vis, blank, patches)


def finish_kernel(vis, pos_ref, rows_ref, token_ref, patch_ref, *refs):
    up_ref, down_ref, at_ref, dec_ref = refs[:4]
    out_ref, patches_ref, up_out, down_out, out_out, qkv_out, dec_out = refs[4:]
    n, _, chunk, feats = rows_ref.shape
    seq = out_ref.shape[1]
    spot = lax.broadcasted_iota(jnp.int32, (seq, n * chunk), 0)
    chosen = (pos_ref[0] == spot).astype(F32)
    rows = nn(chosen.astype(BF16), rows_ref[...].reshape(n * chunk, feats))
    hidden = 1.0 - jnp.sum(chosen, 1, keepdims=True)
    token = token_ref[...].reshape(1, feats).astype(BF16).astype(F32)
    out_ref[0] = (rows + hidden * token).astype(BF16)
    up_out[...] = up_ref[...].astype(F32)
    down_out[...] = down_ref[...].astype(F32)
    dec_out[...] = dec_ref[...].astype(F32)

    @pl.when(pl.program_id(0) == 0)
    def _():
        out_out[...] = at_ref[...].astype(F32)

    @pl.when(pl.program_id(0) > 0)
    def _():
        qkv_out[...] = at_ref[...].astype(F32)

    for s in range(patches_ref.shape[0] // vis):

        @pl.when(pl.program_id(0) == s)
        def _():
            patches_ref[s * vis : (s + 1) * vis] = patch_ref[0, :vis].astype(F32)


def finish(pos_row, rows, token, patch_all, up_grad, down_grad, at_grad, dec_grad, seq, vis):
    n, held, chunk, feats = rows.shape
    _, each, width = patch_all.shape
    tall = width // held
    whole = pl.BlockSpec((held * vis, width), lambda s: (0, 0))
    tile = pl.BlockSpec((tall, width), lambda s: (s, 0))
    shape = jax.ShapeDtypeStruct
    return pl.pallas_call(
        partial(finish_kernel, vis),
        grid=(held,),
        in_specs=[
            pl.BlockSpec((1, 1, n * chunk), lambda s: (s, 0, 0)),
            pl.BlockSpec((n, 1, chunk, feats), lambda s: (0, s, 0, 0)),
            pl.BlockSpec(memory_space=pltpu.VMEM),
            pl.BlockSpec((1, each, width), lambda s: (s, 0, 0)),
            tile,
            tile,
            tile,
            pl.BlockSpec((tall, feats), lambda s: (s, 0)),
        ],
        out_specs=[
            pl.BlockSpec((1, seq, feats), lambda s: (s, 0, 0)),
            whole,
            tile,
            tile,
            pl.BlockSpec((tall, width), lambda s: (0, 0)),
            pl.BlockSpec((tall, width), lambda s: (jnp.maximum(s - 1, 0), 0)),
            pl.BlockSpec((tall, feats), lambda s: (s, 0)),
        ],
        out_shape=[
            shape((held, seq, feats), BF16),
            shape((held * vis, width), F32),
            shape((width, width), F32),
            shape((width, width), F32),
            shape((tall, width), F32),
            shape((width - tall, width), F32),
            shape((width, feats), F32),
        ],
        name="finish",
        compiler_params=pltpu.CompilerParams(vmem_limit_bytes=61 << 20),
    )(pos_row, rows, token, patch_all, up_grad, down_grad, at_grad, dec_grad)


MESH = pl.DeviceIdType.MESH


class Wires:
    def __init__(self, send, recv):
        self.send, self.recv, self.used = send, recv, 0

    def take(self, count=1):
        first = self.used
        self.used += count
        return first

    def copy(self, src, dst, target, index=None):
        index = self.take() if index is None else index
        return pltpu.make_async_remote_copy(
            src_ref=src,
            dst_ref=dst,
            send_sem=self.send.at[index],
            recv_sem=self.recv.at[index],
            device_id=target,
            device_id_type=MESH,
        )


class Place:
    def __init__(self, n):
        self.n = n
        self.d = lax.axis_index("dp")
        self.m = lax.axis_index("mp")
        self.core, self.y = self.m % 2, self.m // 2
        self.core_peer = (self.d, self.m + 1 - 2 * self.core)
        self.y_peer = (self.d, (self.m + 2) % 4)
        self.far_peer = (self.d, 3 - self.m)
        self.y_strip = (self.m + 2) % 4

    def strip(self, i):
        y = self.y + (1 - 2 * self.y) * (1 - i // 2)
        core = self.core + (1 - 2 * self.core) * (1 - i % 2)
        return 2 * y + core

    def dp_peer(self, k):
        return ((self.d + k) % self.n, self.m)


def meet_all(place):
    barrier = pltpu.get_barrier_semaphore()
    for peer in (place.core_peer, place.y_peer, place.far_peer):
        pl.semaphore_signal(barrier, inc=1, device_id=peer, device_id_type=MESH)

    def greet(k, carry):
        pl.semaphore_signal(barrier, inc=1, device_id=place.dp_peer(k), device_id_type=MESH)
        return carry

    lax.fori_loop(1, place.n, greet, 0)
    pl.semaphore_wait(barrier, place.n + 2)


class Spread:
    def __init__(self, wires, place, src, dst, blocks=True, local=True, tall=None):
        self.wires, self.place, self.src, self.blocks, self.local = wires, place, src, blocks, local
        d = place.d
        self.slot = dst.at[d] if tall is None else dst.at[pl.ds(pl.multiple_of(d * tall, tall), tall)]
        self.base = wires.take(place.n)

    def made(self, k):
        peer = self.place.dp_peer(k)
        src = self.src.at[peer[0]] if self.blocks else self.src
        return self.wires.copy(src, self.slot, peer, self.base + k)

    def start(self):
        def one(k, carry):
            self.made(k).start()
            return carry

        lax.fori_loop(1, self.place.n, one, 0)
        if self.local:
            self.slot[...] = self.src[self.place.d] if self.blocks else self.src[...]

    def wait(self):
        def one(k, carry):
            self.made(k).wait()
            return carry

        lax.fori_loop(1, self.place.n, one, 0)


class Scatter:
    def __init__(self, wires, place, core_send, core_recv, y_send, y_recv):
        self.core_send, self.core_recv, self.y_send, self.y_recv = core_send, core_recv, y_send, y_recv
        self.core = [
            wires.copy(core_send.at[i], core_recv.at[i], place.core_peer) for i in range(2)
        ]
        self.away = wires.copy(y_send, y_recv, place.y_peer)

    def give_core(self, i, value):
        self.core_send[i] = value.astype(BF16)
        self.core[i].start()

    def give_y(self, value):
        self.core[0].wait_recv()
        self.y_send[...] = (value + self.core_recv[0].astype(F32)).astype(BF16)

    def own(self, value, arrived=False):
        self.core[1].wait_recv()
        if not arrived:
            self.away.wait_recv()
        return value + self.core_recv[1].astype(F32) + self.y_recv[...].astype(F32)

    def close(self):
        for made in (*self.core, self.away):
            made.wait_send()


class Gather:
    def __init__(self, wires, place, full, src=None):
        spot, passing = full.at[place.m], full.at[place.y_strip]
        src = spot if src is None else src
        self.over_y = wires.copy(src, spot, place.y_peer)
        self.over_core = wires.copy(src, spot, place.core_peer)
        self.passed = wires.copy(passing, passing, place.core_peer)

    def start(self):
        self.over_y.start()
        self.over_core.start()

    def forward(self):
        self.over_y.wait_recv()
        self.passed.start()

    def wait(self):
        self.over_core.wait_recv()
        self.passed.wait_recv()

    def close(self):
        for made in (self.over_y, self.over_core, self.passed):
            made.wait_send()


class Reduce:
    def __init__(self, wires, place, g, recv, h, bits):
        self.g, self.recv, self.h = g, recv, h
        n = place.n
        base, size = 0, n
        self.halves, self.doubles, path = [], [], []
        for k in bits:
            half = size // 2
            bit = (place.d // (1 << k)) % 2
            peer = (place.d + (1 - 2 * bit) * (1 << k), place.m)
            keep, away, landing = base + bit * half, base + (1 - bit) * half, n - size
            made = wires.copy(g.at[pl.ds(away, half)], recv.at[pl.ds(landing, half)], peer)
            self.halves.append((made, keep, landing, half))
            path.append((base, peer))
            base, size = keep, half
        self.mine = base
        for start, peer in reversed(path):
            held = h.at[pl.ds(base, size)]
            self.doubles.append(wires.copy(held, held, peer))
            base, size = start, size * 2

    def steps(self):
        g, recv, h = self.g, self.recv, self.h
        for made, keep, landing, half in self.halves:
            made.start()
            yield
            made.wait_recv()

            def add(i, carry):
                total = g[keep + i].astype(F32) + recv[landing + i].astype(F32)
                g[keep + i] = total.astype(BF16)
                return carry

            lax.fori_loop(0, half, add, 0)
        h[self.mine] = g[self.mine]
        for made in self.doubles:
            made.start()
            yield
            made.wait_recv()
        for made in [half[0] for half in self.halves] + self.doubles:
            made.wait_send()


class Group:
    def __init__(self, sums):
        self.todo = [one.steps() for one in sums]

    def go(self):
        self.todo = [steps for steps in self.todo if next(steps, self) is not self]
        return bool(self.todo)


def layer_kernel(
    n,
    order_in,
    order_out,
    x_ref,
    gain1_ref,
    shift1_ref,
    qkv_w_ref,
    qv_b_ref,
    out_w_ref,
    out_b_ref,
    gain2_ref,
    shift2_ref,
    up_w_ref,
    up_b_ref,
    down_w_ref,
    down_b_ref,
    dec_w_ref,
    dec_b_ref,
    bias_ref,
    cot_ref,
    spot_row,
    spot_col,
    mask_ref,
    patch_hbm,
    h_up,
    h_down,
    h_at,
    h_dec,
    hop4,
    vec_ref,
    qkv,
    att,
    stat,
    mid,
    low2,
    act,
    slope,
    g3_low,
    mid_all,
    g_full,
    decs,
    a_cs,
    a_cr,
    a_ys,
    a_yr,
    b_cs,
    b_cr,
    b_ys,
    b_yr,
    own_a,
    own_b,
    own_c,
    acc,
    g_up,
    g_down,
    g_at,
    g_dec,
    r_up,
    r_down,
    r_at,
    r_dec,
    hop1,
    send2,
    hop2,
    v_own,
    w_own,
    w_all,
    copy_sem,
    send_sem,
    recv_sem,
):
    place = Place(n)
    wires = Wires(send_sem, recv_sem)
    held, rows, width = x_ref.shape
    lw = att.shape[2]
    chunk, feats = hop4.shape[2:]
    scale = HD ** (-0.5)
    row = lambda ref: ref[...].reshape(1, -1)
    total = lambda v: jnp.sum(v, 0, keepdims=True)
    m = place.m
    temp = acc.at[pl.ds(0, rows)]
    fin_all, patch_all, send3, hop3 = g3_low, act, send2, hop1

    decs_in = Gather(wires, place, decs, dec_w_ref)
    cot_one = Spread(wires, place, cot_ref, hop1)
    cot_two = Spread(wires, place, send2, hop2)
    att_sum = Scatter(wires, place, a_cs, a_cr, a_ys, a_yr)
    low2_in = Gather(wires, place, low2)
    g_in = Gather(wires, place, g_full)
    ff_sum = Scatter(wires, place, b_cs, b_cr, b_ys, b_yr)
    h2_sum = Scatter(wires, place, a_cs, a_cr, a_ys, a_yr)
    mid_in = Gather(wires, place, mid_all)
    fin_in = Gather(wires, place, fin_all)
    h1_sum = Scatter(wires, place, a_cs, a_cr, a_ys, a_yr)
    patch_in = Gather(wires, place, patch_all)
    out_one = Spread(wires, place, send3, hop3)
    out_two = Spread(wires, place, send3, hop4)
    told = Spread(wires, place, v_own, acc, blocks=False, tall=v_own.shape[0])
    shared = [
        wires.copy(w_own, w_all.at[m], peer)
        for peer in (place.core_peer, place.y_peer, place.far_peer)
    ]
    bits = list(range(n.bit_length() - 1))
    turned = [bits[1], bits[0], *bits[2:]]
    pieces = g_up.shape[0]
    ways = [bits, turned] if pieces > 1 else [bits]


    def group(g, recv, h):
        return Group(
            [Reduce(wires, place, g.at[i], recv.at[i], h.at[i], ways[i]) for i in range(pieces)]
        )

    up, down, at = group(g_up, r_up, h_up), group(g_down, r_down, h_down), group(g_at, r_at, h_at)
    dec_one = Spread(wires, place, g_dec, r_dec)
    dec_two = Spread(wires, place, h_dec.at[place.d], h_dec, blocks=False, local=False)

    meet_all(place)
    decs_in.start()
    decs[m] = dec_w_ref[...]
    cot_one.start()

    def regroup(order_ref, src, dst):
        def one(k, carry):
            j = order_ref[k]
            dst[k // held, k % held] = src[j // held, j % held]
            return carry

        lax.fori_loop(0, n * held, one, 0)

    qkv_shift = jnp.concatenate([qv_b_ref[0:1], jnp.zeros((1, lw), F32), qv_b_ref[1:2]], 1)
    lane = lax.broadcasted_iota(jnp.int32, (1, 3 * lw), 1)
    qkv_scale = jnp.where(lane < lw, scale, 1.0)

    def low_one(s):
        normed, _ = norm_stats(x_ref[s].astype(F32))
        return (normed * row(gain1_ref) + row(shift1_ref)).astype(BF16)

    def attention(i, carry):
        s = place.strip(i)
        proj = (nt(low_one(s), qkv_w_ref[...]) + qkv_shift) * qkv_scale
        qkv[s] = proj.astype(BF16)
        bias = bias_ref[s]
        outs = []
        spot = lax.broadcasted_iota(jnp.int32, (rows, 128), 1)
        stats = jnp.zeros((rows, 128), F32)
        for h in range(lw // HD):
            q = qkv[s, :, h * HD : (h + 1) * HD]
            k = qkv[s, :, lw + h * HD : lw + (h + 1) * HD]
            v = qkv[s, :, 2 * lw + h * HD : 2 * lw + (h + 1) * HD]
            scores = nt(q, k) + bias
            top = jnp.max(scores, -1, keepdims=True)
            e = jnp.exp(scores - top)
            norm = jnp.sum(e, -1, keepdims=True)
            outs.append((nn(e.astype(BF16), v) / norm).astype(BF16))
            stats = jnp.where(spot == h, top + jnp.log(norm), stats)
        att[s] = jnp.concatenate(outs, -1)
        stat[s] = stats
        temp[...] = nn(att[s], out_w_ref[...])

        @pl.when(i == 0)
        def _():
            att_sum.give_core(0, temp[...])

        @pl.when(i == 1)
        def _():
            att_sum.give_y(temp[...])
            decs_in.forward()
            att_sum.away.start()

        @pl.when(i == 2)
        def _():
            att_sum.give_core(1, temp[...])
            cot_one.wait()
            regroup(order_in, hop1, send2)
            cot_two.start()

        return carry

    lax.fori_loop(0, held, attention, 0)
    mid[...] = x_ref[m].astype(F32) + row(out_b_ref) + att_sum.own(temp[...])
    normed, _ = norm_stats(mid[...])
    low2[m] = (normed * row(gain2_ref) + row(shift2_ref)).astype(BF16)
    low2_in.start()
    att_sum.close()
    cot_two.wait()
    t = lax.broadcasted_iota(jnp.int32, (rows, n * chunk), 0)
    sel = (t == spot_row[...]).astype(F32).astype(BF16)
    for s in range(held):
        g_full[m, s] = nn(sel, hop2[:, s].reshape(n * chunk, feats)).astype(BF16)
    decs_in.wait()
    v_own[...] = jnp.zeros_like(v_own)
    low2_in.forward()
    g_in.start()
    low2_in.wait()

    tall = 16

    def feed_forward(i, carry):
        s = place.strip(i)
        temp[...] = nn(low2[s], up_w_ref[...]) + row(up_b_ref)

        def some(r, inner):
            at = pl.ds(pl.multiple_of(r * tall, tall), tall)
            pre = temp[at]
            half = 0.5 * (1.0 + lax.erf(pre * np.float32(0.5**0.5)))
            bell = jnp.exp(-0.5 * pre * pre) * np.float32((2 * np.pi) ** -0.5)
            act[s, at] = (pre * half).astype(BF16)
            slope[s, at] = (half + pre * bell).astype(BF16)
            return inner

        lax.fori_loop(0, rows // tall, some, 0)
        temp[...] = nn(act[s], down_w_ref[...])

        @pl.when(i == 0)
        def _():
            ff_sum.give_core(0, temp[...])

        @pl.when(i == 1)
        def _():
            ff_sum.give_y(temp[...])
            g_in.forward()
            ff_sum.away.start()

        @pl.when(i == 2)
        def _():
            ff_sum.give_core(1, temp[...])

        @pl.when(i == 3)
        def _():
            own_b[...] = temp[...].astype(BF16)

        return carry

    lax.fori_loop(0, held, feed_forward, 0)
    g_in.wait()

    def g_three(s):
        weight = jnp.concatenate([decs[i] for i in range(4)], 1)
        return nt(jnp.concatenate([g_full[i, s] for i in range(4)], 1), weight)

    def g_low(s, carry):
        g3_low[s] = g_three(s).astype(BF16)
        return carry

    lax.fori_loop(0, held, g_low, 0)

    def weight_grad(left, right, out):
        acc[...] = jnp.zeros_like(acc)

        def add(s, carry):
            acc[...] += tn(left[s], right[s])
            return carry

        lax.fori_loop(0, held, add, 0)
        out[...] = acc[...].reshape(out.shape).astype(BF16)

    weight_grad(act, g3_low, g_down)
    down.go()

    def backward_ff(i, carry):
        s = place.strip(i)
        g_pre = nt(g3_low[s], down_w_ref[...]) * slope[s].astype(F32)
        slope[s] = g_pre.astype(BF16)
        v_own[6:7] += total(g_pre)
        temp[...] = nt(slope[s], up_w_ref[...])

        @pl.when(i == 0)
        def _():
            h2_sum.give_core(0, temp[...])

        @pl.when(i == 1)
        def _():
            h2_sum.give_y(temp[...])
            ff_sum.away.wait_recv()
            h2_sum.away.start()
            down.go()

        @pl.when(i == 2)
        def _():
            h2_sum.give_core(1, temp[...])

        @pl.when(i == 3)
        def _():
            own_a[...] = temp[...]
            down.go()

        return carry

    lax.fori_loop(0, held, backward_ff, 0)
    weight_grad(low2, slope, g_up)
    up.go()
    final = mid[...] + ff_sum.own(own_b[...].astype(F32), arrived=True) + row(down_b_ref)
    fin_all[m] = final.astype(BF16)
    g_own = g_three(m)
    v_own[5:6] = total(g_own)

    g_h2 = h2_sum.own(own_a[...])
    normed, inverse = norm_stats(mid[...])
    g_norm, gain_sum, bias_sum = norm_backward(g_h2, normed, inverse, row(gain2_ref))
    g_mid = g_own + g_norm
    own_a[...] = g_mid
    mid_all[m] = g_mid.astype(BF16)
    mid_in.start()
    h2_sum.close()
    v_own[2:3] = gain_sum.reshape(1, width)
    v_own[3:4] = bias_sum.reshape(1, width)
    v_own[4:5] = total(g_mid)
    down.go()

    def dqkv(s):
        return slope[s, :, : 3 * lw]

    def attention_back(i, carry):
        s = place.strip(3 - i)

        @pl.when(i == 1)
        def _():
            mid_in.over_core.wait_recv()

        @pl.when(i == 2)
        def _():
            mid_in.forward()
            fin_in.start()

        @pl.when(i == 3)
        def _():
            mid_in.passed.wait_recv()

        grad = nt(mid_all[s], out_w_ref[...]).astype(BF16)
        bias = bias_ref[s]
        dq, dk, dv = [], [], []
        for h in range(lw // HD):
            q = qkv[s, :, h * HD : (h + 1) * HD]
            k = qkv[s, :, lw + h * HD : lw + (h + 1) * HD]
            v = qkv[s, :, 2 * lw + h * HD : 2 * lw + (h + 1) * HD]
            g = grad[:, h * HD : (h + 1) * HD]
            o = att[s, :, h * HD : (h + 1) * HD]
            p = jnp.exp(nt(q, k) + bias - stat[s, :, h : h + 1])
            dv.append(tn(p.astype(BF16), g).astype(BF16))
            inner = jnp.sum(g.astype(F32) * o.astype(F32), -1, keepdims=True)
            ds = (p * (nt(g, v) - inner)).astype(BF16)
            dq.append((nn(ds, k) * scale).astype(BF16))
            dk.append(tn(ds, q).astype(BF16))
        slope[s, :, : 3 * lw] = jnp.concatenate(dq + dk + dv, -1)
        temp[...] = nn(dqkv(s), qkv_w_ref[...])

        @pl.when(i == 0)
        def _():
            own_c[...] = temp[...].astype(BF16)
            up.go()

        @pl.when(i == 1)
        def _():
            h1_sum.give_core(1, temp[...])
            down.go()
            up.go()

        @pl.when(i == 2)
        def _():
            a_ys[...] = temp[...].astype(BF16)
            down.go()
            up.go()

        @pl.when(i == 3)
        def _():
            h1_sum.give_core(0, temp[...])
            h1_sum.give_y(a_ys[...].astype(F32))
            down.go()
            up.go()

        return carry

    lax.fori_loop(0, held, attention_back, 0)

    acc[...] = jnp.zeros_like(acc)

    def attention_grads(s, carry):
        acc[:lw] += tn(att[s], mid_all[s])
        acc[lw:] += tn(dqkv(s), low_one(s))
        return carry

    lax.fori_loop(0, held, attention_grads, 0)
    g_at[...] = acc[...].reshape(g_at.shape).astype(BF16)
    at.go()
    up.go()
    columns = jnp.zeros((1, 3 * lw), F32)
    dec_rows = jnp.zeros((1, feats), F32)
    for s in range(held):
        columns += total(dqkv(s).astype(F32))
        dec_rows += total(g_full[m, s].astype(F32))
    blank = jnp.zeros((1, width - 2 * lw - 2 * feats), F32)
    v_own[7:8] = jnp.concatenate(
        [columns[:, :lw], columns[:, 2 * lw :], dec_rows, mask_ref[0:1], blank], 1
    )

    fin_in.forward()
    h1_sum.away.start()
    fin_in.wait()
    t = lax.broadcasted_iota(jnp.int32, (n * chunk, rows), 1)
    sel = (t == spot_col[...]).astype(F32).astype(BF16)
    for s in range(held):
        projected = (nn(fin_all[s], dec_w_ref[...]) + row(dec_b_ref)).astype(BF16)
        send3[:, s] = nn(sel, projected).astype(BF16).reshape(n, chunk, feats)
    out_one.start()
    dec_grad = jnp.zeros((width, feats), F32)
    for s in range(held):
        dec_grad += tn(fin_all[s], g_full[m, s])
    g_dec[...] = dec_grad.reshape(g_dec.shape).astype(BF16)
    dec_one.start()
    up.go()
    at.go()
    up.go()
    at.go()

    g_h1 = h1_sum.own(own_c[...].astype(F32))
    normed, inverse = norm_stats(x_ref[m].astype(F32))
    g_norm, gain_sum, bias_sum = norm_backward(g_h1, normed, inverse, row(gain1_ref))
    patch_all[m] = (own_a[...] + g_norm).astype(BF16)
    patch_in.start()
    v_own[0:1] = gain_sum.reshape(1, width)
    v_own[1:2] = bias_sum.reshape(1, width)
    at.go()
    out_one.wait()
    regroup(order_out, hop3, send3)
    out_two.start()
    told.start()
    at.go()
    at.go()
    dec_one.wait()
    dec_total = lax.fori_loop(1, n, lambda i, v: v + r_dec[i].astype(F32), r_dec[0].astype(F32))
    h_dec[place.d] = dec_total.astype(BF16)
    dec_two.start()
    told.wait()
    w_own[...] = lax.fori_loop(
        1, n, lambda i, v: v + acc[pl.ds(pl.multiple_of(8 * i, 8), 8)], acc[0:8]
    )
    for made in shared:
        made.start()
    w_all[m] = w_own[...]
    out_two.wait()
    for made in shared:
        made.wait()
    summed = w_all[0] + w_all[1] + w_all[2] + w_all[3]
    vec_ref[...] = jnp.concatenate([summed[:6], w_own[6:8]], 0)
    patch_in.forward()
    while any([group.go() for group in (down, up, at)]):
        pass
    dec_two.wait()
    patch_in.wait()
    store = pltpu.make_async_copy(patch_all, patch_hbm, copy_sem)
    store.start()
    for made in (decs_in, low2_in, g_in, ff_sum, mid_in, fin_in, h1_sum, patch_in):
        made.close()
    store.wait()


def vmem(count):
    return [pl.BlockSpec(memory_space=pltpu.VMEM)] * count


def layer(n, pieces, order_in, order_out, x, *rest):
    held, rows, width = x.shape
    lw = rest[4].shape[0]
    _, _, chunk, feats = rest[-4].shape
    each = width // (pieces * n)
    shape = jax.ShapeDtypeStruct
    low = lambda *dims: pltpu.VMEM(dims, BF16)
    full = lambda *dims: pltpu.VMEM(dims, F32)
    bits = n.bit_length() - 1
    sems = 7 * n + 64 + 2 * (3 * pieces + 1) * bits
    part = (pieces, n, each, width)
    got = (pieces, n - 1, each, width)
    strips = low(held, rows, width)
    links = [low(2, rows, width), low(2, rows, width), low(rows, width), low(rows, width)]
    hop = low(n, held, chunk, feats)
    smem = pl.BlockSpec(memory_space=pltpu.SMEM)
    return pl.pallas_call(
        partial(layer_kernel, n),
        in_specs=[smem, smem] + vmem(1 + len(rest)),
        out_specs=[pl.BlockSpec(memory_space=pl.ANY)] + vmem(6),
        out_shape=[
            shape((held, rows, width), BF16),
            shape(part, BF16),
            shape(part, BF16),
            shape(part, BF16),
            shape((n, width // n, feats), BF16),
            shape((n, held, chunk, feats), BF16),
            shape((8, width), F32),
        ],
        scratch_shapes=[
            low(held, rows, 3 * lw),
            low(held, rows, lw),
            full(held, rows, 128),
            full(rows, width),
            strips,
            strips,
            strips,
            strips,
            strips,
            low(4, held, rows, feats),
            low(4, width, feats),
            *links,
            *links,
            full(rows, width),
            low(rows, width),
            low(rows, width),
            full(width, width),
            low(*part),
            low(*part),
            low(*part),
            low(n, width // n, feats),
            low(*got),
            low(*got),
            low(*got),
            low(n, width // n, feats),
            hop,
            hop,
            hop,
            full(8, width),
            full(8, width),
            full(4, 8, width),
            pltpu.SemaphoreType.DMA,
            pltpu.SemaphoreType.DMA((sems,)),
            pltpu.SemaphoreType.DMA((sems,)),
        ],
        name="layer",
        compiler_params=pltpu.CompilerParams(
            collective_id=0, has_side_effects=True, vmem_limit_bytes=62 << 20
        ),
    )(order_in, order_out, x, *rest)


def shards(
    patches,
    norm1_gain,
    norm1_bias,
    qkv_weight,
    qv_bias,
    out_weight,
    out_bias,
    norm2_gain,
    norm2_bias,
    up_weight,
    up_bias,
    down_weight,
    down_bias,
    dec_weight,
    dec_bias,
    mask_token,
    lengths,
    blank,
    visible,
    plan,
    dec_cot,
):
    n = lax.axis_size("dp")
    d = lax.axis_index("dp")
    held, seq, feats = dec_cot.shape
    vis = visible.shape[1]
    strips = plan.shape[0]
    width = patches.shape[1]
    lw = qkv_weight.shape[2]
    rows = -(-vis // 16) * 16
    real = -(-vis // n)
    chunk = -(-real // 8) * 8

    strip_ids = jnp.arange(strips, dtype=jnp.int32)
    earlier = (plan[None, :] == plan[:, None]) & (strip_ids[None, :] < strip_ids[:, None])
    packed_at = plan * held + jnp.sum(earlier.astype(jnp.int32), 1)
    strip_at = jnp.sum(
        jnp.where(packed_at[None, :] == strip_ids[:, None], strip_ids[None, :], 0), 1
    )
    held_strips = lax.dynamic_slice_in_dim(strip_at, d * held, held)
    owned_pos = lax.dynamic_slice_in_dim(visible, d * held, held)
    owned_pos = jnp.pad(owned_pos, ((0, 0), (0, n * real - vis)), constant_values=-1)
    owned_pos = jnp.pad(
        owned_pos.reshape(held, n, real), ((0, 0), (0, 0), (0, chunk - real)), constant_values=-1
    )

    vis_rows = jnp.pad(visible, ((0, 0), (0, rows - vis)), constant_values=-1)
    spread_cot, mask_grad, key_bias, x_all = prepare(
        held_strips,
        lengths,
        owned_pos.reshape(held, n * chunk, 1),
        dec_cot,
        vis_rows,
        blank,
        patches,
        n,
        chunk,
    )
    spot = np.arange(n * chunk)
    spot = np.where(spot % chunk < real, spot // chunk * real + spot % chunk, -1)
    pieces = 2 if width // n % 32 == 0 else 1
    patch_all, up_grad, down_grad, at_grad, dec_grad, arrived, vectors = layer(
        n,
        pieces,
        strip_at,
        packed_at,
        x_all,
        norm1_gain,
        norm1_bias,
        qkv_weight.reshape(width, 3 * lw).T,
        qv_bias,
        out_weight,
        out_bias,
        norm2_gain,
        norm2_bias,
        up_weight,
        up_bias,
        down_weight,
        down_bias,
        dec_weight,
        dec_bias,
        key_bias,
        spread_cot,
        jnp.asarray(spot, jnp.int32).reshape(1, n * chunk),
        jnp.asarray(spot, jnp.int32).reshape(n * chunk, 1),
        mask_grad,
    )
    decoded, patches_grad, up_grad, down_grad, out_grad, qkv_grad, dec_grad = finish(
        owned_pos.reshape(held, 1, n * chunk),
        arrived,
        mask_token,
        patch_all,
        up_grad.reshape(width, width),
        down_grad.reshape(width, width),
        at_grad.reshape(width, width),
        dec_grad.reshape(width, feats),
        seq,
        vis,
    )
    qkv_grad = qkv_grad.T.reshape(width, 3, lw)
    mixed = vectors[7]
    return (
        decoded,
        patches_grad,
        vectors[0],
        vectors[1],
        qkv_grad,
        mixed[: 2 * lw].reshape(2, lw),
        out_grad,
        vectors[4],
        vectors[2],
        vectors[3],
        up_grad,
        vectors[6],
        down_grad,
        vectors[5],
        dec_grad,
        mixed[2 * lw : 2 * lw + feats],
        mixed[2 * lw + feats : 2 * lw + 2 * feats],
    )


def solution(mesh):
    return jax.shard_map(
        shards,
        mesh=mesh,
        in_specs=(
            P("dp", None),
            P(),
            P(),
            P(None, None, "mp"),
            P(None, "mp"),
            P("mp", None),
            P(),
            P(),
            P(),
            P(None, "mp"),
            P("mp"),
            P("mp", None),
            P(),
            P(None, "mp"),
            P("mp"),
            P("mp"),
            P(),
            P(),
            P(),
            P(),
            P("dp", None, "mp"),
        ),
        out_specs=(
            P("dp", None, "mp"),
            P("dp", None),
            P(),
            P(),
            P(None, None, "mp"),
            P(None, "mp"),
            P("mp", None),
            P(),
            P(),
            P(),
            P(None, "mp"),
            P("mp"),
            P("mp", None),
            P(),
            P(None, "mp"),
            P("mp"),
            P("mp"),
        ),
        check_vma=False,
    )
```
